32 devices in a mesh: sample: 4 (over x, core), space: 8 (over z, y).
Axes of the slice: x: 2, y: 2, z: 4, core: 2. Of those that a mesh axis runs over, the one named last changes fastest.
Arguments:
- acts: bfloat16 [8, 8, 16, 8, 8, 128], P('sample', 'space'), may hold values from -6 to 6
- weight: float32 [3456, 128], P('space'), may hold values from -0.109375 to 0.109375
- moment: float32 [3456, 128], P('space'), may hold values from -3 to 3
- second: float32 [3456, 128], P('space'), may hold values from 0.05 to 2
- cotangent: bfloat16 [8, 8, 16, 8, 8, 128], P('sample', 'space'), may hold values from -6 to 6
Outputs:
- output: bfloat16 [8, 8, 16, 8, 8, 128], P('sample', 'space')
- input_grad: bfloat16 [8, 8, 16, 8, 8, 128], P('sample', 'space')
- weight_grad: float32 [3456, 128], P('space')
- new_weight: float32 [3456, 128], P('space')
- new_moment: float32 [3456, 128], P('space')
- new_second: float32 [3456, 128], P('space')
The draws below stay inside these ranges and needn't reach their ends.
All inputs are finite; a program needn't handle non-finite values.
Results may differ from the reference program's by a relative error of at most 0.0062.
Values may be sent and summed in bfloat16 or wider, within the bound.
A program may use at most 64 MiB of HBM per device.

```python
import math
import jax
import jax.numpy as jnp
from jax import lax

CH = 128
BX = 16
BY = 8
BZ = 8
GY = 2
GZ = 4
BRICKS = 8
BATCH = 8


def block_scale(rng, extent, pieces, low, high):
    factor_of = 1.0
    for position, shards_of in pieces:
        draws = jax.random.uniform(jax.random.fold_in(jax.random.fold_in(rng, 6), position), (shards_of,), jnp.float32, low / len(pieces), high / len(pieces))
        factor_of = factor_of * jnp.repeat(jnp.exp(draws), extent[position] // shards_of).reshape((-1,) + (1,) * (len(extent) - 1 - position))
    return factor_of


def noise(own_key, dims, width, most, cuts=(), dtype=jnp.bfloat16):
    array = jax.random.normal(own_key, dims, jnp.float32) * width
    if len(cuts) > 0:
        array = block_scale(own_key, dims, cuts, -0.22, 0.18) * array
    return jnp.clip(array, min=-most, max=most).astype(dtype)


def setup_inputs(seed: int = 0) -> dict:
    key_of = jax.random.split(jax.random.key(seed), 6)
    acts = noise(key_of[0], (BATCH, BRICKS, BX, BY, BZ, CH), 1.0, 6.0, ((0, 4), (1, 8)))
    weight = noise(key_of[1], (27 * CH, CH), (27 * CH) ** -0.5, 0.109375, ((0, 8),), jnp.float32)
    moment = noise(key_of[2], (27 * CH, CH), 0.5, 3.0, ((0, 8),), jnp.float32)
    second = jnp.clip(jnp.exp(math.log(2.0) - 3.6888794 * jax.random.uniform(key_of[3], (27 * CH, CH), jnp.float32) ** block_scale(key_of[3], (27 * CH, CH), ((0, 8),), -0.2, 0.2)), 0.05, 2.0)
    cotangent = noise(key_of[4], (BATCH, BRICKS, BX, BY, BZ, CH), 1.0, 6.0, ((0, 4), (1, 8)))
    return {"acts": acts, "weight": weight, "moment": moment, "second": second, "cotangent": cotangent}


root_coef = 0.7978845608
cubic_coef = 0.044715

def to_crop(field):
    nb, nr, sx, sy, sz, nc = field.shape
    groups = nr // (GY * GZ)
    shaped = field.reshape(nb, groups, GY, GZ, sx, sy, sz, nc)
    shaped = shaped.transpose(0, 1, 4, 2, 5, 3, 6, 7)
    return shaped.reshape(nb, groups * sx, GY * sy, GZ * sz, nc)

def to_bricks(field):
    nb, nx, ny, nz, nc = field.shape
    groups = nx // BX
    shaped = field.reshape(nb, groups, BX, GY, BY, GZ, BZ, nc)
    shaped = shaped.transpose(0, 1, 3, 5, 2, 4, 6, 7)
    return shaped.reshape(nb, groups * GY * GZ, BX, BY, BZ, nc)

def convolve(field, kernel, padding):
    return lax.conv_general_dilated(field, kernel, (1, 1, 1), padding, dimension_numbers=('NDHWC', 'DHWIO', 'NDHWC'), preferred_element_type=jnp.float32)

def activate(pre):
    inner = root_coef * (pre + cubic_coef * pre * pre * pre)
    tval = jnp.tanh(inner)
    value = 0.5 * pre * (1.0 + tval)
    slope = 0.5 * (1.0 + tval) + 0.5 * pre * (1.0 - tval * tval) * root_coef * (1.0 + 3.0 * cubic_coef * pre * pre)
    return (value, slope)

def kernel_terms(padded, grad_pre):
    nx, ny, nz = (grad_pre.shape[1], grad_pre.shape[2], grad_pre.shape[3])
    terms = []
    for kx in range(3):
        for ky in range(3):
            for kz in range(3):
                window = padded[:, kx:kx + nx, ky:ky + ny, kz:kz + nz, :]
                terms.append(lax.dot_general(window, grad_pre, (((0, 1, 2, 3), (0, 1, 2, 3)), ((), ())), preferred_element_type=jnp.float32))
    stacked = jnp.stack(terms, 0)
    return stacked.reshape(27 * stacked.shape[1], stacked.shape[2])

def adam(weight, moment, second, grad):
    new_moment = 0.9 * moment + 0.1 * grad
    new_second = 0.999 * second + 0.001 * grad * grad
    first_fix = 1.0 - 0.9 ** 10
    second_fix = 1.0 - 0.999 ** 10
    new_weight = weight - 0.001 * (new_moment / first_fix) / (jnp.sqrt(new_second / second_fix) + 1e-08)
    return (new_weight, new_moment, new_second)

def reference(acts, weight, moment, second, cotangent):
    crop = to_crop(acts)
    grad_out = to_crop(cotangent)
    channels = weight.shape[1]
    kernel = weight.astype(jnp.bfloat16).reshape(3, 3, 3, channels, channels)
    pad = [(1, 1), (1, 1), (1, 1)]
    pre = convolve(crop, kernel, pad)
    value, slope = activate(pre)
    output = value.astype(jnp.bfloat16)
    grad_pre = (grad_out.astype(jnp.float32) * slope).astype(jnp.bfloat16)
    flipped = jnp.flip(kernel, (0, 1, 2)).transpose(0, 1, 2, 4, 3)
    input_grad = convolve(grad_pre, flipped, pad).astype(jnp.bfloat16)
    padded = jnp.pad(crop, ((0, 0), (1, 1), (1, 1), (1, 1), (0, 0)))
    total = crop.shape[0] * crop.shape[1] * crop.shape[2] * crop.shape[3]
    weight_grad = kernel_terms(padded, grad_pre) * float(total) ** (-0.5)
    new_weight, new_moment, new_second = adam(weight, moment, second, weight_grad)
    return (to_bricks(output), to_bricks(input_grad), weight_grad, new_weight, new_moment, new_second)
```

```python
import functools

import jax
import jax.numpy as jnp
from jax import lax
from jax.experimental import pallas as pl
from jax.experimental.pallas import tpu as pltpu
from jax.sharding import PartitionSpec as P

GY = 2
GZ = 4
MESH = pl.DeviceIdType.MESH
VM = pl.BlockSpec(memory_space=pltpu.VMEM)

root_coef = 0.7978845608
cubic_coef = 0.044715

SIDES = (1, -1)
DIRS = [(0, 1), (0, -1), (1, 0), (-1, 0)] + [(dy, dz) for dy in SIDES for dz in SIDES]


def shifted(value, axis, by):
    devices = lax.axis_size(axis)
    pairs = [(i, i + by) for i in range(devices) if 0 <= i + by < devices]
    return lax.ppermute(value, axis, pairs)


def convolve(field, kernel):
    return lax.conv_general_dilated(
        field,
        kernel,
        (1, 1, 1),
        "VALID",
        dimension_numbers=("NDHWC", "DHWIO", "NDHWC"),
        preferred_element_type=jnp.float32,
    )


def activate(pre):
    inner = root_coef * (pre + cubic_coef * pre * pre * pre)
    tval = jnp.tanh(inner)
    value = 0.5 * pre * (1.0 + tval)
    slope = 0.5 * (1.0 + tval) + 0.5 * pre * (1.0 - tval * tval) * root_coef * (
        1.0 + 3.0 * cubic_coef * pre * pre
    )
    return (value, slope)


def extend_x(field):
    groups = lax.axis_size("space") // (GY * GZ)
    if groups == 1:
        return jnp.pad(field, ((0, 0), (1, 1), (0, 0), (0, 0), (0, 0)))
    coord = lax.axis_index("space") // (GZ * GY)
    length = field.shape[1]
    below = shifted(field[:, length - 1 : length], "space", GY * GZ)
    above = shifted(field[:, :1], "space", -GY * GZ)
    below = jnp.where(coord > 0, below, jnp.zeros_like(below))
    above = jnp.where(coord < groups - 1, above, jnp.zeros_like(above))
    return jnp.concatenate([below, field, above], 1)


def faces(field):
    ends = {1: field.shape[2] - 1, -1: 0}
    endz = {1: field.shape[3] - 1, -1: 0}
    zf = jnp.stack([field[:, :, :, endz[d], :] for d in SIDES])
    yf = jnp.stack([field[:, :, ends[d], :, :] for d in SIDES])
    cf = jnp.stack([field[:, :, ends[dy], endz[dz], :] for dy in SIDES for dz in SIDES])
    return (zf, yf, cf)


def assemble(field, zf, yf, cf):
    mid = jnp.concatenate([zf[0][:, :, :, None], field, zf[1][:, :, :, None]], 3)
    rows = []
    for i in range(2):
        low, high = cf[2 * i][:, :, None, :], cf[2 * i + 1][:, :, None, :]
        rows.append(jnp.concatenate([low, yf[i], high], 2)[:, :, None])
    return jnp.concatenate([rows[0], mid, rows[1]], 2)


class Halo:
    def __init__(self, ins, outs, send, recv):
        me = lax.axis_index("space")
        self.me, self.send, self.recv = me, send, recv
        self.cz, self.cy = lax.rem(me, GZ), lax.rem(me // GZ, GY)
        self.src = [ins[k // 2].at[k % 2] if k < 4 else ins[2].at[k - 4] for k in range(8)]
        self.dst = [outs[k // 2].at[k % 2] if k < 4 else outs[2].at[k - 4] for k in range(8)]

    def has(self, dy, dz):
        y, z = self.cy + dy, self.cz + dz
        return (y >= 0) & (y < GY) & (z >= 0) & (z < GZ)

    def copy(self, k, to):
        return pltpu.make_async_remote_copy(
            src_ref=self.src[k],
            dst_ref=self.dst[k],
            send_sem=self.send.at[k],
            recv_sem=self.recv.at[k],
            device_id={"space": to},
            device_id_type=MESH,
        )

    def start(self):
        for k, (dy, dz) in enumerate(DIRS):

            @pl.when(self.has(dy, dz))
            def _():
                self.copy(k, self.me + dy * GZ + dz).start()

            @pl.when(jnp.logical_not(self.has(-dy, -dz)))
            def _():
                self.dst[k][...] = jnp.zeros(self.dst[k].shape, self.dst[k].dtype)

    def finish(self):
        for k, (dy, dz) in enumerate(DIRS):

            @pl.when(self.has(-dy, -dz))
            def _():
                self.copy(k, self.me).wait_recv()

            @pl.when(self.has(dy, dz))
            def _():
                self.copy(k, self.me).wait_send()


def greet(n, me, sample):
    barrier = pltpu.get_barrier_semaphore()

    def space_peer(d, _):
        pl.semaphore_signal(barrier, 1, device_id={"space": lax.rem(me + d, n)}, device_id_type=MESH)
        return 0

    lax.fori_loop(1, n, space_peer, 0)
    for d in range(1, 4):
        pl.semaphore_signal(barrier, 1, device_id={"sample": lax.rem(sample + d, 4)}, device_id_type=MESH)
    pl.semaphore_wait(barrier, n + 2)


def remote(src, dst, send, recv, **to):
    return pltpu.make_async_remote_copy(
        src_ref=src, dst_ref=dst, send_sem=send, recv_sem=recv, device_id=to, device_id_type=MESH
    )


LAG = 6


def gather_kernel(n, w, zi, yi, ci, out, zo, yo, co, hs, hr, as_, ar, bs, br, cs, cr):
    me, sample = lax.axis_index("space"), lax.axis_index("sample")
    core, x = lax.rem(sample, 2), sample // 2
    across, partner = (1 - x) * 2 + core, x * 2 + 1 - core
    greet(n, me, sample)
    halo = Halo((zi, yi, ci), (zo, yo, co), hs, hr)
    halo.start()

    def first(d, _):
        o = lax.rem(me + d, n)
        remote(w.at[core, x], out.at[me, core, x], as_.at[o], ar.at[me], space=o).start()
        return 0

    lax.fori_loop(1, n, first, 0)
    out[me] = w[...]

    def rest(t, _):
        @pl.when(t < n)
        def _():
            j = lax.rem(me - t + n, n)
            slot = out.at[j, core, x]
            remote(slot, slot, as_.at[j], ar.at[j], space=me).wait_recv()
            remote(slot, slot, bs.at[j], br.at[j], sample=across).start()

        @pl.when(t > LAG)
        def _():
            j = lax.rem(me - t + LAG + n, n)
            slot = out.at[j, core, 1 - x]
            remote(slot, slot, bs.at[j], br.at[j], sample=across).wait_recv()
            pair = out.at[j, core]
            remote(pair, pair, cs.at[j], cr.at[j], sample=partner).start()

        return 0

    lax.fori_loop(1, n + LAG, rest, 0)

    def last(d, _):
        o = lax.rem(me + d, n)
        pair = out.at[o, 1 - core]
        remote(pair, pair, cs.at[o], cr.at[o], sample=partner).wait_recv()
        remote(w.at[core, x], out.at[me, core, x], as_.at[o], ar.at[me], space=o).wait_send()
        slot = out.at[o, core, x]
        remote(slot, slot, bs.at[o], br.at[o], sample=across).wait_send()
        mine = out.at[o, core]
        remote(mine, mine, cs.at[o], cr.at[o], sample=partner).wait_send()
        return 0

    lax.fori_loop(1, n, last, 0)
    halo.finish()


def reduce_kernel(n, g, zi, yi, ci, out, zo, yo, co, r1, s2, r2, s3, r3, hs, hr, as_, ar, bs, br, cs, cr, ds, dr):
    me, sample = lax.axis_index("space"), lax.axis_index("sample")
    core, x = lax.rem(sample, 2), sample // 2
    across, partner = (1 - x) * 2 + core, x * 2 + 1 - core
    f32, bf16 = jnp.float32, jnp.bfloat16
    greet(n, me, sample)
    halo = Halo((zi, yi, ci), (zo, yo, co), hs, hr)
    halo.start()

    def owner(d):
        return lax.rem(me + 1 + d, n)

    def copy1(o):
        return remote(g.at[o, 1 - core], r1.at[o], as_.at[o], ar.at[o], sample=partner)

    def copy2(o):
        return remote(s2.at[o, 1 - x], r2.at[o], bs.at[o], br.at[o], sample=across)

    def copy3(o):
        return remote(s3.at[o], r3.at[me], cs.at[o], cr.at[me], space=o)

    def first(d, _):
        copy1(owner(d)).start()
        return 0

    lax.fori_loop(0, n, first, 0)

    def rest(t, _):
        @pl.when(t < n)
        def _():
            o = owner(t)
            copy1(o).wait_recv()
            s2[o] = (g[o, core].astype(f32) + r1[o].astype(f32)).astype(bf16)
            copy2(o).start()

        @pl.when(t >= LAG)
        def _():
            o = owner(t - LAG)
            copy2(o).wait_recv()
            s3[o] = (s2[o, x].astype(f32) + r2[o].astype(f32)).astype(bf16)

            @pl.when(t < n + LAG - 1)
            def _():
                copy3(o).start()

        return 0

    lax.fori_loop(0, n + LAG, rest, 0)

    def gather(d, total):
        j = lax.rem(me + n - d, n)
        remote(s3.at[j], r3.at[j], cs.at[j], cr.at[j], space=j).wait_recv()
        return total + r3[j].astype(f32)

    out[core, x] = lax.fori_loop(1, n, gather, s3[me].astype(f32))

    def copy4(d):
        mine = out.at[core, x]
        return remote(mine, mine, ds.at[d], dr.at[d], sample=lax.rem(sample + 1 + d, 4))

    for d in range(3):
        copy4(d).start()
    for d in range(3):
        copy4(d).wait()

    def drain(d, _):
        o = owner(d)
        copy1(o).wait_send()
        copy2(o).wait_send()

        @pl.when(d < n - 1)
        def _():
            copy3(o).wait_send()

        return 0

    lax.fori_loop(0, n, drain, 0)
    halo.finish()


def quarters(value, lead):
    rows = value.shape[-2]
    q = -(-rows // 4)
    if rows != 4 * q:
        value = jnp.pad(value, [(0, 0)] * (value.ndim - 2) + [(0, 4 * q - rows), (0, 0)])
    return value.reshape(*lead, 2, 2, q, value.shape[-1])


def whole_rows(value, rows):
    lead = value.shape[:-4]
    return value.reshape(*lead, -1, value.shape[-1])[..., :rows, :]


def like(arrays):
    return [jax.ShapeDtypeStruct(a.shape, a.dtype) for a in arrays]


def sems(*counts):
    return [pltpu.SemaphoreType.DMA((c,)) for c in counts]


def gather_weights(rows_bf, field):
    n = lax.axis_size("space")
    halo = faces(field)
    w = quarters(rows_bf, ())
    whole, zf, yf, cf = pl.pallas_call(
        functools.partial(gather_kernel, n),
        name="gather_and_halo",
        out_shape=[jax.ShapeDtypeStruct((n, *w.shape), w.dtype), *like(halo)],
        in_specs=[VM] * 4,
        out_specs=[VM] * 4,
        scratch_shapes=sems(8, 8, n, n, n, n, n, n),
        compiler_params=pltpu.CompilerParams(collective_id=0, has_side_effects=True),
    )(w, *halo)
    whole = whole_rows(whole, rows_bf.shape[0]).reshape(-1, rows_bf.shape[1])
    return whole, assemble(field, zf, yf, cf)


def reduce_grads(terms, rows, field):
    n = lax.axis_size("space")
    halo = faces(field)
    channels = terms.shape[-1]
    g = quarters(terms.reshape(n, rows, channels), (n,)).astype(jnp.bfloat16)
    q = g.shape[3]
    bf16 = jnp.bfloat16
    total, zf, yf, cf = pl.pallas_call(
        functools.partial(reduce_kernel, n),
        name="reduce_and_halo",
        out_shape=[jax.ShapeDtypeStruct((2, 2, q, channels), jnp.float32), *like(halo)],
        in_specs=[VM] * 4,
        out_specs=[VM] * 4,
        scratch_shapes=[
            pltpu.VMEM((n, 2, q, channels), bf16),
            pltpu.VMEM((n, 2, q, channels), bf16),
            pltpu.VMEM((n, q, channels), bf16),
            pltpu.VMEM((n, q, channels), bf16),
            pltpu.VMEM((n, q, channels), bf16),
            *sems(8, 8, n, n, n, n, n, n, 3, 3),
        ],
        compiler_params=pltpu.CompilerParams(collective_id=1, has_side_effects=True),
    )(g, *halo)
    return whole_rows(total, rows), assemble(field, zf, yf, cf)


def kernel_terms(padded, grad_pre):
    terms = lax.conv_general_dilated(
        padded,
        grad_pre,
        (1, 1, 1),
        "VALID",
        dimension_numbers=("CDHWN", "IDHWO", "DHWNC"),
        preferred_element_type=jnp.float32,
    )
    return terms.reshape(-1, terms.shape[-1])


def plain(acts, weight, moment, second, cotangent):
    field = acts[:, 0]
    grad_out = cotangent[:, 0]
    channels = weight.shape[1]
    rows_bf = weight.astype(jnp.bfloat16)
    whole, padded = gather_weights(rows_bf, extend_x(field))
    kernel = whole.reshape(3, 3, 3, channels, channels)
    pre = convolve(padded, kernel)
    value, slope = activate(pre)
    output = value.astype(jnp.bfloat16)
    grad_pre = (grad_out.astype(jnp.float32) * slope).astype(jnp.bfloat16)
    flipped = jnp.flip(kernel, (0, 1, 2)).transpose(0, 1, 2, 4, 3)
    total = (
        field.shape[0]
        * lax.axis_size("sample")
        * lax.axis_size("space")
        * field.shape[1]
        * field.shape[2]
        * field.shape[3]
    )
    local_terms = kernel_terms(padded, grad_pre)
    summed, grad_padded = reduce_grads(local_terms, weight.shape[0], extend_x(grad_pre))
    input_grad = convolve(grad_padded, flipped).astype(jnp.bfloat16)
    weight_grad = summed * float(total) ** (-0.5)
    new_moment = 0.9 * moment + 0.1 * weight_grad
    new_second = 0.999 * second + 0.001 * weight_grad * weight_grad
    first_fix = 1.0 - 0.9**10
    second_fix = 1.0 - 0.999**10
    new_weight = weight - 0.001 * (new_moment / first_fix) / (
        jnp.sqrt(new_second / second_fix) + 1e-08
    )
    return (output[:, None], input_grad[:, None], weight_grad, new_weight, new_moment, new_second)


TILE = 16


def peers(n):
    me, sample = lax.axis_index("space"), lax.axis_index("sample")
    core, x = lax.rem(sample, 2), sample // 2
    return me, sample, core, x


class Field:
    def __init__(self, block, ends, faces, shifts, send, recv):
        self.block, self.ends, self.faces, self.shifts = block, ends, faces, shifts
        self.send, self.recv = send, recv
        me = lax.axis_index("space")
        self.me, self.cz, self.cy = me, lax.rem(me, GZ), lax.rem(me // GZ, GY)
        self.ny = block.shape[2] - 2

    def has(self, dy, dz):
        y, z = self.cy + dy, self.cz + dz
        return (y >= 0) & (y < GY) & (z >= 0) & (z < GZ)

    def extract(self):
        crops, nx, _, nz, _ = self.block.shape
        row = lax.broadcasted_iota(jnp.int32, (2 * nx, nx * nz), 0)
        col = lax.broadcasted_iota(jnp.int32, (2 * nx, nx * nz), 1)
        want = jnp.where(row < nx, row * nz + nz - 1, (row - nx) * nz)
        pick = jnp.where(col == want, 1.0, 0.0).astype(jnp.bfloat16)

        def step(y, _):
            for c in range(crops):
                rows = self.block[c, :, y + 1].reshape(nx * nz, -1)
                both = jnp.dot(pick, rows, preferred_element_type=jnp.float32).astype(jnp.bfloat16)
                self.faces[0, y, c] = both[:nx]
                self.faces[1, y, c] = both[nx:]
            return 0

        lax.fori_loop(0, self.ny, step, 0)

    def refs(self, dy, dz):
        last = self.ny - 1
        if dz == 0:
            src = self.block.at[:, :, last + 1 if dy > 0 else 1]
            dst = self.block.at[:, :, 0 if dy > 0 else last + 2]
            return src, dst
        side = 0 if dz > 0 else 1
        if dy == 0:
            return self.faces.at[side], self.ends.at[side, pl.ds(1, self.ny)]
        src = self.faces.at[side, last if dy > 0 else 0]
        return src, self.ends.at[side, 0 if dy > 0 else last + 2]

    def copy(self, k, to):
        src, dst = self.refs(*DIRS[k])
        return remote(src, dst, self.send.at[k], self.recv.at[k], space=to)

    def clear(self):
        for k, (dy, dz) in enumerate(DIRS):
            dst = self.refs(dy, dz)[1]

            @pl.when(jnp.logical_not(self.has(-dy, -dz)))
            def _():
                dst[...] = jnp.zeros(dst.shape, dst.dtype)

        nx = self.block.shape[1]
        for edge in (0, nx + 1):
            self.shifts[edge] = jnp.zeros(self.shifts.shape[1:], self.shifts.dtype)

    def start(self, faces_only):
        for k, (dy, dz) in enumerate(DIRS):
            if (dz == 0) == faces_only:

                @pl.when(self.has(dy, dz))
                def _():
                    self.copy(k, self.me + dy * GZ + dz).start()

    def finish(self):
        for k, (dy, dz) in enumerate(DIRS):

            @pl.when(self.has(-dy, -dz))
            def _():
                self.copy(k, self.me).wait_recv()

    def drain(self):
        for k, (dy, dz) in enumerate(DIRS):

            @pl.when(self.has(dy, dz))
            def _():
                self.copy(k, self.me).wait_send()

    def build(self):
        crops, nx, _, nz, ch = self.block.shape
        f32 = jnp.float32

        def step(y, _):
            out = ([], [], [])
            for c in range(crops):
                mid = self.block[c, :, y].astype(f32)
                low = self.ends[0, y, c].astype(f32)[:, None, :]
                high = self.ends[1, y, c].astype(f32)[:, None, :]
                z = lax.broadcasted_iota(jnp.int32, mid.shape, 1)
                out[0].append(jnp.where(z == 0, low, pltpu.roll(mid, 1, 1)))
                out[1].append(mid)
                out[2].append(jnp.where(z == nz - 1, high, pltpu.roll(mid, nz - 1, 1)))
            for kz in range(3):
                value = jnp.concatenate(out[kz], 1).astype(jnp.bfloat16)
                self.shifts[pl.ds(1, nx), y, :, kz * ch : (kz + 1) * ch] = value
            return 0

        lax.fori_loop(0, self.ny + 2, step, 0)

    def window(self, x0, kx, ky, step):
        rows = [
            self.shifts[pl.ds(x0 + kx, step), 2 * p + ky].reshape(-1, self.shifts.shape[-1])
            for p in range(self.ny // 2)
        ]
        return jnp.concatenate(rows, 0)

    def patch(self, x0, step):
        return jnp.concatenate([self.window(x0, kx, ky, step) for kx in range(3) for ky in range(4)], 1)


STEP = 4


def fused_kernel(
    n, scale,
    acts, cot, w, moment, second,
    output, igrad, wgrad, nweight, nmoment, nsecond,
    xb, xe, xf, xs, zb, ze, zf, zs, cotv,
    wall, w2, w2d, dzt, g, r1, s2, p2, s3, p3, total,
    ls, xhs, xhr, zhs, zhr,
    gzs, gzr, gxs, gxr, gys, gyr, gds, gdr, gcs, gcr,
    c1s, c1r, c2s, c2r, c3s, c3r, c4s, c4r,
):
    f32, bf16 = jnp.float32, jnp.bfloat16
    me, sample, core, x = peers(n)
    na = n // 2
    a, b = me // 2, lax.rem(me, 2)
    across, partner = (1 - x) * 2 + core, x * 2 + 1 - core
    beside = a * 2 + 1 - b
    groups = w.shape[0]
    q = wall.shape[1] // 4
    ch = w.shape[2]
    crops, nx, _, nz, _ = xb.shape
    ny = xb.shape[2] - 2

    load_x = pltpu.make_async_copy(acts, xb.at[:, :, pl.ds(1, ny)], ls.at[0])
    load_c = pltpu.make_async_copy(cot, cotv, ls.at[1])
    load_x.start()
    load_c.start()

    barrier = pltpu.get_barrier_semaphore()

    def greet_space(d, _):
        pl.semaphore_signal(barrier, 1, device_id={"space": lax.rem(me + d, n)}, device_id_type=MESH)
        return 0

    lax.fori_loop(1, n, greet_space, 0)
    for d in range(1, 4):
        pl.semaphore_signal(barrier, 1, device_id={"sample": lax.rem(sample + d, 4)}, device_id_type=MESH)
    pl.semaphore_signal(barrier, 1, device_id={"sample": across, "space": beside}, device_id_type=MESH)

    wall[me, pl.ds(0, groups)] = w[...].astype(bf16)
    wall[me, pl.ds(groups, 4 * q - groups)] = jnp.zeros((4 * q - groups, TILE, ch), bf16)
    field = Field(xb, xe, xf, xs, xhs, xhr)
    dfield = Field(zb, ze, zf, zs, zhs, zhr)
    field.clear()
    dfield.clear()
    for kx in range(3):
        w2[pl.ds((kx * 4 + 3) * 24, 24), :, 0:ch] = jnp.zeros((24, TILE, ch), bf16)
        w2[pl.ds(kx * 96, 24), :, ch : 2 * ch] = jnp.zeros((24, TILE, ch), bf16)
        w2d[pl.ds((kx * 4 + 3) * 24, 24), :, 0:ch] = jnp.zeros((24, TILE, ch), bf16)
        w2d[pl.ds(kx * 96, 24), :, ch : 2 * ch] = jnp.zeros((24, TILE, ch), bf16)
    g[:, pl.ds(groups, 4 * q - groups)] = jnp.zeros((n, 4 * q - groups, TILE, ch), bf16)

    pl.semaphore_wait(barrier, n + 3)

    def piece(s, c, h):
        return wall.at[s, pl.ds((c * 2 + h) * q, q)]

    def column(d):
        return lax.rem(a + na - d, na) * 2 + b

    def other(d):
        return lax.rem(a + na - d, na) * 2 + 1 - b

    def z_copy(d):
        part = piece(me, core, x)
        return remote(part, part, gzs.at[d], gzr.at[d], space=lax.rem(a + d, na) * 2 + b)

    def z_wait(d):
        part = piece(column(d), core, x)
        return remote(part, part, gzs.at[d], gzr.at[d], space=beside)

    def x_copy(d):
        part = piece(column(d), core, x)
        return remote(part, part, gxs.at[d], gxr.at[d], sample=across)

    def x_wait(d):
        part = piece(column(d), core, 1 - x)
        return remote(part, part, gxs.at[d], gxr.at[d], sample=across)

    def y_copy(d):
        part = piece(column(d), core, x)
        return remote(part, part, gys.at[d], gyr.at[d], space=beside)

    def y_wait(d):
        part = piece(other(d), core, x)
        return remote(part, part, gys.at[d], gyr.at[d], space=beside)

    def d_copy(d):
        part = piece(column(d), core, x)
        return remote(part, part, gds.at[d], gdr.at[d], sample=across, space=beside)

    def d_wait(d):
        part = piece(other(d), core, 1 - x)
        return remote(part, part, gds.at[d], gdr.at[d], sample=across, space=beside)

    def half(s, c):
        return wall.at[s, pl.ds(c * 2 * q, 2 * q)]

    def c_copy(i, s):
        part = half(s, core)
        return remote(part, part, gcs.at[i], gcr.at[i], sample=partner)

    def c_wait(i, s):
        part = half(s, 1 - core)
        return remote(part, part, gcs.at[i], gcr.at[i], sample=partner)

    for d in range(1, na):
        z_copy(d).start()
    y_copy(0).start()
    d_copy(0).start()
    load_x.wait()
    field.start(True)
    field.extract()
    field.start(False)

    def place(s):
        def step(i, _):
            r = s * groups + i
            at = r + (r // 72) * 24
            tile = wall[s, i]
            w2[at, :, 0:ch] = tile
            w2[at + 24, :, ch : 2 * ch] = tile
            return 0

        lax.fori_loop(0, groups, step, 0)

    place(me)

    def forward(d, _):
        z_wait(d).wait_recv()
        y_copy(d).start()
        d_copy(d).start()
        x_copy(d).start()
        return 0

    lax.fori_loop(1, na, forward, 0)
    field.finish()
    field.build()

    def finish_plane(d, _):
        y_wait(d).wait_recv()
        d_wait(d).wait_recv()
        c_copy(na + d, other(d)).start()

        @pl.when(d > 0)
        def _():
            x_wait(d).wait_recv()
            c_copy(d, column(d)).start()

        return 0

    lax.fori_loop(0, na, finish_plane, 0)

    def arrive(d, _):
        c_wait(na + d, other(d)).wait_recv()
        place(other(d))

        @pl.when(d > 0)
        def _():
            c_wait(d, column(d)).wait_recv()
            place(column(d))

        return 0

    lax.fori_loop(0, na, arrive, 0)

    load_c.wait()
    rows = w2.shape[0] * TILE

    def chunk(i, _):
        x0 = i * STEP
        pre = jnp.dot(field.patch(x0, STEP), w2[...].reshape(rows, 2 * ch), preferred_element_type=f32)
        square = pre * pre
        tval = jnp.tanh(pre * (root_coef + root_coef * cubic_coef * square))
        gate = 0.5 * (1.0 + tval)
        value = (pre * gate).astype(bf16)
        slope = gate + (0.5 * pre) * (1.0 - tval * tval) * (root_coef + 3.0 * root_coef * cubic_coef * square)
        pieces = []
        m = STEP * TILE
        for p in range(ny // 2):
            line = []
            for h in range(2):
                up = jnp.concatenate([cotv[c, pl.ds(x0, STEP), 2 * p + h].astype(f32) for c in range(crops)], 1)
                dz = up.reshape(m, ch) * slope[p * m : (p + 1) * m, h * ch : (h + 1) * ch]
                line.append(dz)
                out = value[p * m : (p + 1) * m, h * ch : (h + 1) * ch].reshape(STEP, TILE, ch)
                dzr = dz.astype(bf16).reshape(STEP, TILE, ch)
                for c in range(crops):
                    output[c, pl.ds(x0, STEP), 2 * p + h] = out[:, c * nz : (c + 1) * nz]
                    zb[c, pl.ds(x0, STEP), 2 * p + h + 1] = dzr[:, c * nz : (c + 1) * nz]
            pieces.append(jnp.concatenate(line, 1))
        dzm = jnp.concatenate(pieces, 0)
        cols = dzm.shape[0]
        dzt[:, pl.ds(pl.multiple_of(i * cols, 128), cols)] = dzm.T.astype(bf16)
        return 0

    lax.fori_loop(0, nx // STEP, chunk, 0)

    dfield.start(True)
    dfield.extract()
    dfield.start(False)

    def one(o):
        return remote(g.at[o, pl.ds((1 - core) * 2 * q, 2 * q)], r1.at[o], c1s.at[o], c1r.at[o], sample=partner)

    def two(k, j):
        own = j * 2 + (b if k == 0 else 1 - b)
        side = x if k == 1 else 1 - x
        to = {"sample": across} if k == 0 else {"space": beside}
        if k == 2:
            to = {"sample": across, "space": beside}
        return remote(s2.at[own, pl.ds(side * q, q)], p2.at[k, j], c2s.at[k, j], c2r.at[k, j], **to)

    def three(d):
        j = lax.rem(a + d, na)
        return remote(s3.at[j], p3.at[d], c3s.at[d], c3r.at[d], space=j * 2 + b)

    def four(d):
        mine = total.at[core * 2 + x]
        return remote(mine, mine, c4s.at[d], c4r.at[d], sample=lax.rem(sample + 1 + d, 4))

    def send_one(o, _):
        one(o).start()
        return 0

    def send_two(o, _):
        one(o).wait_recv()
        s2[o] = (g[o, pl.ds(core * 2 * q, 2 * q)].astype(f32) + r1[o].astype(f32)).astype(bf16)
        j = o // 2

        @pl.when(lax.rem(o, 2) == b)
        def _():
            two(0, j).start()

        @pl.when(lax.rem(o, 2) != b)
        def _():
            two(2, j).start()
            two(1, j).start()

        return 0

    def done(kx):
        return (kx * 72) // groups

    def terms(kx, _):
        window = [
            jnp.concatenate([field.window(i * STEP, kx, ky, STEP) for ky in range(4)], 1)
            for i in range(nx // STEP)
        ]
        pair = jnp.dot(dzt[...], jnp.concatenate(window, 0), preferred_element_type=f32)
        for ky in range(3):
            k = 3 * ch
            both = pair[:ch, ky * k : (ky + 1) * k] + pair[ch:, (ky + 1) * k : (ky + 2) * k]
            for kz in range(3):
                tap = both[:, kz * ch : (kz + 1) * ch].T.astype(bf16).reshape(ch // TILE, TILE, ch)
                for t in range(ch // TILE):
                    r = kx * 72 + (ky * 3 + kz) * (ch // TILE) + t
                    g[r // groups, lax.rem(r, groups)] = tap[t]
        lax.fori_loop(done(kx), done(kx + 1), send_one, 0)

        @pl.when(kx > 0)
        def _():
            lax.fori_loop(done(kx - 1), done(kx), send_two, 0)

        return 0

    lax.fori_loop(0, 3, terms, 0)
    lax.fori_loop(done(2), n, send_two, 0)

    def flip(t, _):
        kx, r = t // 9, lax.rem(t, 9)
        ky, kz = r // 3, lax.rem(r, 3)
        src = (kx * 4 + ky) * 24 + kz * 8
        dst = ((2 - kx) * 4 + 2 - ky) * 24 + (2 - kz) * 8
        tap = w2[pl.ds(src, 8), :, 0:ch].reshape(ch, ch).astype(f32).T.astype(bf16).reshape(8, TILE, ch)
        w2d[pl.ds(dst, 8), :, 0:ch] = tap
        w2d[pl.ds(dst + 24, 8), :, ch : 2 * ch] = tap
        return 0

    lax.fori_loop(0, 27, flip, 0)
    dfield.finish()
    dfield.build()

    def sum_two(j, _):
        for k in range(3):
            two(k, j).wait_recv()
        own = s2[j * 2 + b, pl.ds(x * q, q)].astype(f32)
        s3[j] = (own + p2[0, j].astype(f32) + p2[1, j].astype(f32) + p2[2, j].astype(f32)).astype(bf16)
        return 0

    def back(i, _):
        x0 = i * STEP
        grad = jnp.dot(
            dfield.patch(x0, STEP), w2d[...].reshape(rows, 2 * ch), preferred_element_type=f32
        ).astype(bf16)
        m = STEP * TILE
        for p in range(ny // 2):
            for h in range(2):
                out = grad[p * m : (p + 1) * m, h * ch : (h + 1) * ch].reshape(STEP, TILE, ch)
                for c in range(crops):
                    igrad[c, pl.ds(x0, STEP), 2 * p + h] = out[:, c * nz : (c + 1) * nz]

        @pl.when(i == SUM_AT)
        def _():
            lax.fori_loop(0, na, sum_two, 0)
            for d in range(1, na):
                three(d).start()

        return 0

    lax.fori_loop(0, nx // STEP, back, 0)

    result = s3[a].astype(f32)
    for d in range(1, na):
        three(d).wait_recv()
        result = result + p3[d].astype(f32)
    total[core * 2 + x] = result
    for d in range(3):
        four(d).start()
    for d in range(3):
        four(d).wait()
    grad = total[...].reshape(4 * q, TILE, ch)[:groups] * scale
    mom = 0.9 * moment[...] + 0.1 * grad
    sec = 0.999 * second[...] + 0.001 * grad * grad
    first_fix = 1.0 - 0.9**10
    second_fix = 1.0 - 0.999**10
    wgrad[...] = grad
    nmoment[...] = mom
    nsecond[...] = sec
    nweight[...] = w[...] - 0.001 * (mom / first_fix) / (jnp.sqrt(sec / second_fix) + 1e-08)

    field.drain()
    dfield.drain()
    y_copy(0).wait_send()
    d_copy(0).wait_send()

    def drain_gather(d, _):
        z_copy(d).wait_send()
        y_copy(d).wait_send()
        d_copy(d).wait_send()
        x_copy(d).wait_send()
        c_copy(d, column(d)).wait_send()
        three(d).wait_send()
        return 0

    lax.fori_loop(1, na, drain_gather, 0)

    def drain_plane(d, _):
        c_copy(na + d, other(d)).wait_send()
        for k in range(3):
            two(k, d).wait_send()
        return 0

    lax.fori_loop(0, na, drain_plane, 0)

    def drain_one(o, _):
        one(o).wait_send()
        return 0

    lax.fori_loop(0, n, drain_one, 0)


SUM_AT = 1


def fused(acts, weight, moment, second, cotangent, scale):
    n = lax.axis_size("space")
    na = n // 2
    bf16, f32 = jnp.bfloat16, jnp.float32
    crops, nx, ny, nz, ch = acts.shape
    groups = weight.shape[0] // TILE
    q = -(-groups // 4)
    tiles = [v.reshape(groups, TILE, ch) for v in (weight, moment, second)]
    state = jax.ShapeDtypeStruct((groups, TILE, ch), f32)
    block = pltpu.VMEM((crops, nx, ny + 2, nz, ch), bf16)
    ends = pltpu.VMEM((2, ny + 2, crops, nx, ch), bf16)
    face = pltpu.VMEM((2, ny, crops, nx, ch), bf16)
    shifts = pltpu.VMEM((nx + 2, ny + 2, crops * nz, 3 * ch), bf16)
    wide = pltpu.VMEM((3 * 4 * 3 * ch // TILE, TILE, 2 * ch), bf16)
    HBM = pl.BlockSpec(memory_space=pl.ANY)

    def sem(*shape):
        return pltpu.SemaphoreType.DMA(shape)

    outs = pl.pallas_call(
        functools.partial(fused_kernel, n, scale),
        name="whole_step",
        out_shape=[jax.ShapeDtypeStruct(acts.shape, bf16), jax.ShapeDtypeStruct(acts.shape, bf16)] + [state] * 4,
        in_specs=[HBM, HBM, VM, VM, VM],
        out_specs=[VM] * 6,
        scratch_shapes=[
            block, ends, face, shifts, block, ends, face, shifts,
            pltpu.VMEM((crops, nx, ny, nz, ch), bf16),
            pltpu.VMEM((n, 4 * q, TILE, ch), bf16),
            wide, wide,
            pltpu.VMEM((2 * ch, crops * nx * ny * nz // 2), bf16),
            pltpu.VMEM((n, 4 * q, TILE, ch), bf16),
            pltpu.VMEM((n, 2 * q, TILE, ch), bf16),
            pltpu.VMEM((n, 2 * q, TILE, ch), bf16),
            pltpu.VMEM((3, na, q, TILE, ch), bf16),
            pltpu.VMEM((na, q, TILE, ch), bf16),
            pltpu.VMEM((na, q, TILE, ch), bf16),
            pltpu.VMEM((4, q, TILE, ch), f32),
            sem(2), sem(8), sem(8), sem(8), sem(8),
            sem(na), sem(na), sem(na), sem(na), sem(na), sem(na), sem(na), sem(na), sem(n), sem(n),
            sem(n), sem(n), sem(3, na), sem(3, na), sem(na), sem(na), sem(3), sem(3),
        ],
        compiler_params=pltpu.CompilerParams(
            collective_id=2, has_side_effects=True, vmem_limit_bytes=60 * 1024 * 1024
        ),
    )(acts, cotangent, *tiles)
    return list(outs[:2]) + [v.reshape(weight.shape) for v in outs[2:]]


def local(acts, weight, moment, second, cotangent):
    n = lax.axis_size("space")
    crops, _, nx, ny, nz, channels = acts.shape
    total = crops * lax.axis_size("sample") * n * nx * ny * nz
    alone = n == GY * GZ and lax.axis_size("sample") == 4
    fits = crops * nz == TILE and nx == TILE and ny % 2 == 0 and channels == 128 and weight.shape[0] % TILE == 0
    if not (alone and fits):
        return plain(acts, weight, moment, second, cotangent)
    value, grad, *rest = fused(
        acts[:, 0], weight, moment, second, cotangent[:, 0], float(total) ** (-0.5)
    )
    return (value[:, None], grad[:, None], *rest)


def solution(mesh):
    in_specs = (
        P("sample", "space", None, None, None, None),
        P("space", None),
        P("space", None),
        P("space", None),
        P("sample", "space", None, None, None, None),
    )
    out_specs = (
        P("sample", "space", None, None, None, None),
        P("sample", "space", None, None, None, None),
        P("space", None),
        P("space", None),
        P("space", None),
        P("space", None),
    )
    return jax.shard_map(local, mesh=mesh, in_specs=in_specs, out_specs=out_specs, check_vma=False)
```

```python
import functools

import jax
import jax.numpy as jnp
from jax import lax
from jax.experimental import pallas as pl
from jax.experimental.pallas import tpu as pltpu
from jax.sharding import PartitionSpec as P

GY = 2
GZ = 4
MESH = pl.DeviceIdType.MESH
VM = pl.BlockSpec(memory_space=pltpu.VMEM)

root_coef = 0.7978845608
cubic_coef = 0.044715

SIDES = (1, -1)
DIRS = [(0, 1), (0, -1), (1, 0), (-1, 0)] + [(dy, dz) for dy in SIDES for dz in SIDES]


def shifted(value, axis, by):
    devices = lax.axis_size(axis)
    pairs = [(i, i + by) for i in range(devices) if 0 <= i + by < devices]
    return lax.ppermute(value, axis, pairs)


def convolve(field, kernel):
    return lax.conv_general_dilated(
        field,
        kernel,
        (1, 1, 1),
        "VALID",
        dimension_numbers=("NDHWC", "DHWIO", "NDHWC"),
        preferred_element_type=jnp.float32,
    )


def activate(pre):
    inner = root_coef * (pre + cubic_coef * pre * pre * pre)
    tval = jnp.tanh(inner)
    value = 0.5 * pre * (1.0 + tval)
    slope = 0.5 * (1.0 + tval) + 0.5 * pre * (1.0 - tval * tval) * root_coef * (
        1.0 + 3.0 * cubic_coef * pre * pre
    )
    return (value, slope)


def extend_x(field):
    groups = lax.axis_size("space") // (GY * GZ)
    if groups == 1:
        return jnp.pad(field, ((0, 0), (1, 1), (0, 0), (0, 0), (0, 0)))
    coord = lax.axis_index("space") // (GZ * GY)
    length = field.shape[1]
    below = shifted(field[:, length - 1 : length], "space", GY * GZ)
    above = shifted(field[:, :1], "space", -GY * GZ)
    below = jnp.where(coord > 0, below, jnp.zeros_like(below))
    above = jnp.where(coord < groups - 1, above, jnp.zeros_like(above))
    return jnp.concatenate([below, field, above], 1)


def faces(field):
    ends = {1: field.shape[2] - 1, -1: 0}
    endz = {1: field.shape[3] - 1, -1: 0}
    zf = jnp.stack([field[:, :, :, endz[d], :] for d in SIDES])
    yf = jnp.stack([field[:, :, ends[d], :, :] for d in SIDES])
    cf = jnp.stack([field[:, :, ends[dy], endz[dz], :] for dy in SIDES for dz in SIDES])
    return (zf, yf, cf)


def assemble(field, zf, yf, cf):
    mid = jnp.concatenate([zf[0][:, :, :, None], field, zf[1][:, :, :, None]], 3)
    rows = []
    for i in range(2):
        low, high = cf[2 * i][:, :, None, :], cf[2 * i + 1][:, :, None, :]
        rows.append(jnp.concatenate([low, yf[i], high], 2)[:, :, None])
    return jnp.concatenate([rows[0], mid, rows[1]], 2)


class Halo:
    def __init__(self, ins, outs, send, recv):
        me = lax.axis_index("space")
        self.me, self.send, self.recv = me, send, recv
        self.cz, self.cy = lax.rem(me, GZ), lax.rem(me // GZ, GY)
        self.src = [ins[k // 2].at[k % 2] if k < 4 else ins[2].at[k - 4] for k in range(8)]
        self.dst = [outs[k // 2].at[k % 2] if k < 4 else outs[2].at[k - 4] for k in range(8)]

    def has(self, dy, dz):
        y, z = self.cy + dy, self.cz + dz
        return (y >= 0) & (y < GY) & (z >= 0) & (z < GZ)

    def copy(self, k, to):
        return pltpu.make_async_remote_copy(
            src_ref=self.src[k],
            dst_ref=self.dst[k],
            send_sem=self.send.at[k],
            recv_sem=self.recv.at[k],
            device_id={"space": to},
            device_id_type=MESH,
        )

    def start(self):
        for k, (dy, dz) in enumerate(DIRS):

            @pl.when(self.has(dy, dz))
            def _():
                self.copy(k, self.me + dy * GZ + dz).start()

            @pl.when(jnp.logical_not(self.has(-dy, -dz)))
            def _():
                self.dst[k][...] = jnp.zeros(self.dst[k].shape, self.dst[k].dtype)

    def finish(self):
        for k, (dy, dz) in enumerate(DIRS):

            @pl.when(self.has(-dy, -dz))
            def _():
                self.copy(k, self.me).wait_recv()

            @pl.when(self.has(dy, dz))
            def _():
                self.copy(k, self.me).wait_send()


def greet(n, me, sample):
    barrier = pltpu.get_barrier_semaphore()

    def space_peer(d, _):
        pl.semaphore_signal(barrier, 1, device_id={"space": lax.rem(me + d, n)}, device_id_type=MESH)
        return 0

    lax.fori_loop(1, n, space_peer, 0)
    for d in range(1, 4):
        pl.semaphore_signal(barrier, 1, device_id={"sample": lax.rem(sample + d, 4)}, device_id_type=MESH)
    pl.semaphore_wait(barrier, n + 2)


def remote(src, dst, send, recv, **to):
    return pltpu.make_async_remote_copy(
        src_ref=src, dst_ref=dst, send_sem=send, recv_sem=recv, device_id=to, device_id_type=MESH
    )


LAG = 6


def gather_kernel(n, w, zi, yi, ci, out, zo, yo, co, hs, hr, as_, ar, bs, br, cs, cr):
    me, sample = lax.axis_index("space"), lax.axis_index("sample")
    core, x = lax.rem(sample, 2), sample // 2
    across, partner = (1 - x) * 2 + core, x * 2 + 1 - core
    greet(n, me, sample)
    halo = Halo((zi, yi, ci), (zo, yo, co), hs, hr)
    halo.start()

    def first(d, _):
        o = lax.rem(me + d, n)
        remote(w.at[core, x], out.at[me, core, x], as_.at[o], ar.at[me], space=o).start()
        return 0

    lax.fori_loop(1, n, first, 0)
    out[me] = w[...]

    def rest(t, _):
        @pl.when(t < n)
        def _():
            j = lax.rem(me - t + n, n)
            slot = out.at[j, core, x]
            remote(slot, slot, as_.at[j], ar.at[j], space=me).wait_recv()
            remote(slot, slot, bs.at[j], br.at[j], sample=across).start()

        @pl.when(t > LAG)
        def _():
            j = lax.rem(me - t + LAG + n, n)
            slot = out.at[j, core, 1 - x]
            remote(slot, slot, bs.at[j], br.at[j], sample=across).wait_recv()
            pair = out.at[j, core]
            remote(pair, pair, cs.at[j], cr.at[j], sample=partner).start()

        return 0

    lax.fori_loop(1, n + LAG, rest, 0)

    def last(d, _):
        o = lax.rem(me + d, n)
        pair = out.at[o, 1 - core]
        remote(pair, pair, cs.at[o], cr.at[o], sample=partner).wait_recv()
        remote(w.at[core, x], out.at[me, core, x], as_.at[o], ar.at[me], space=o).wait_send()
        slot = out.at[o, core, x]
        remote(slot, slot, bs.at[o], br.at[o], sample=across).wait_send()
        mine = out.at[o, core]
        remote(mine, mine, cs.at[o], cr.at[o], sample=partner).wait_send()
        return 0

    lax.fori_loop(1, n, last, 0)
    halo.finish()


def reduce_kernel(n, g, zi, yi, ci, out, zo, yo, co, r1, s2, r2, s3, r3, hs, hr, as_, ar, bs, br, cs, cr, ds, dr):
    me, sample = lax.axis_index("space"), lax.axis_index("sample")
    core, x = lax.rem(sample, 2), sample // 2
    across, partner = (1 - x) * 2 + core, x * 2 + 1 - core
    f32, bf16 = jnp.float32, jnp.bfloat16
    greet(n, me, sample)
    halo = Halo((zi, yi, ci), (zo, yo, co), hs, hr)
    halo.start()

    def owner(d):
        return lax.rem(me + 1 + d, n)

    def copy1(o):
        return remote(g.at[o, 1 - core], r1.at[o], as_.at[o], ar.at[o], sample=partner)

    def copy2(o):
        return remote(s2.at[o, 1 - x], r2.at[o], bs.at[o], br.at[o], sample=across)

    def copy3(o):
        return remote(s3.at[o], r3.at[me], cs.at[o], cr.at[me], space=o)

    def first(d, _):
        copy1(owner(d)).start()
        return 0

    lax.fori_loop(0, n, first, 0)

    def rest(t, _):
        @pl.when(t < n)
        def _():
            o = owner(t)
            copy1(o).wait_recv()
            s2[o] = (g[o, core].astype(f32) + r1[o].astype(f32)).astype(bf16)
            copy2(o).start()

        @pl.when(t >= LAG)
        def _():
            o = owner(t - LAG)
            copy2(o).wait_recv()
            s3[o] = (s2[o, x].astype(f32) + r2[o].astype(f32)).astype(bf16)

            @pl.when(t < n + LAG - 1)
            def _():
                copy3(o).start()

        return 0

    lax.fori_loop(0, n + LAG, rest, 0)

    def gather(d, total):
        j = lax.rem(me + n - d, n)
        remote(s3.at[j], r3.at[j], cs.at[j], cr.at[j], space=j).wait_recv()
        return total + r3[j].astype(f32)

    out[core, x] = lax.fori_loop(1, n, gather, s3[me].astype(f32))

    def copy4(d):
        mine = out.at[core, x]
        return remote(mine, mine, ds.at[d], dr.at[d], sample=lax.rem(sample + 1 + d, 4))

    for d in range(3):
        copy4(d).start()
    for d in range(3):
        copy4(d).wait()

    def drain(d, _):
        o = owner(d)
        copy1(o).wait_send()
        copy2(o).wait_send()

        @pl.when(d < n - 1)
        def _():
            copy3(o).wait_send()

        return 0

    lax.fori_loop(0, n, drain, 0)
    halo.finish()


def quarters(value, lead):
    rows = value.shape[-2]
    q = -(-rows // 4)
    if rows != 4 * q:
        value = jnp.pad(value, [(0, 0)] * (value.ndim - 2) + [(0, 4 * q - rows), (0, 0)])
    return value.reshape(*lead, 2, 2, q, value.shape[-1])


def whole_rows(value, rows):
    lead = value.shape[:-4]
    return value.reshape(*lead, -1, value.shape[-1])[..., :rows, :]


def like(arrays):
    return [jax.ShapeDtypeStruct(a.shape, a.dtype) for a in arrays]


def sems(*counts):
    return [pltpu.SemaphoreType.DMA((c,)) for c in counts]


def gather_weights(rows_bf, field):
    n = lax.axis_size("space")
    halo = faces(field)
    w = quarters(rows_bf, ())
    whole, zf, yf, cf = pl.pallas_call(
        functools.partial(gather_kernel, n),
        name="gather_and_halo",
        out_shape=[jax.ShapeDtypeStruct((n, *w.shape), w.dtype), *like(halo)],
        in_specs=[VM] * 4,
        out_specs=[VM] * 4,
        scratch_shapes=sems(8, 8, n, n, n, n, n, n),
        compiler_params=pltpu.CompilerParams(collective_id=0, has_side_effects=True),
    )(w, *halo)
    whole = whole_rows(whole, rows_bf.shape[0]).reshape(-1, rows_bf.shape[1])
    return whole, assemble(field, zf, yf, cf)


def reduce_grads(terms, rows, field):
    n = lax.axis_size("space")
    halo = faces(field)
    channels = terms.shape[-1]
    g = quarters(terms.reshape(n, rows, channels), (n,)).astype(jnp.bfloat16)
    q = g.shape[3]
    bf16 = jnp.bfloat16
    total, zf, yf, cf = pl.pallas_call(
        functools.partial(reduce_kernel, n),
        name="reduce_and_halo",
        out_shape=[jax.ShapeDtypeStruct((2, 2, q, channels), jnp.float32), *like(halo)],
        in_specs=[VM] * 4,
        out_specs=[VM] * 4,
        scratch_shapes=[
            pltpu.VMEM((n, 2, q, channels), bf16),
            pltpu.VMEM((n, 2, q, channels), bf16),
            pltpu.VMEM((n, q, channels), bf16),
            pltpu.VMEM((n, q, channels), bf16),
            pltpu.VMEM((n, q, channels), bf16),
            *sems(8, 8, n, n, n, n, n, n, 3, 3),
        ],
        compiler_params=pltpu.CompilerParams(collective_id=1, has_side_effects=True),
    )(g, *halo)
    return whole_rows(total, rows), assemble(field, zf, yf, cf)


def kernel_terms(padded, grad_pre):
    terms = lax.conv_general_dilated(
        padded,
        grad_pre,
        (1, 1, 1),
        "VALID",
        dimension_numbers=("CDHWN", "IDHWO", "DHWNC"),
        preferred_element_type=jnp.float32,
    )
    return terms.reshape(-1, terms.shape[-1])


def plain(acts, weight, moment, second, cotangent):
    field = acts[:, 0]
    grad_out = cotangent[:, 0]
    channels = weight.shape[1]
    rows_bf = weight.astype(jnp.bfloat16)
    whole, padded = gather_weights(rows_bf, extend_x(field))
    kernel = whole.reshape(3, 3, 3, channels, channels)
    pre = convolve(padded, kernel)
    value, slope = activate(pre)
    output = value.astype(jnp.bfloat16)
    grad_pre = (grad_out.astype(jnp.float32) * slope).astype(jnp.bfloat16)
    flipped = jnp.flip(kernel, (0, 1, 2)).transpose(0, 1, 2, 4, 3)
    total = (
        field.shape[0]
        * lax.axis_size("sample")
        * lax.axis_size("space")
        * field.shape[1]
        * field.shape[2]
        * field.shape[3]
    )
    local_terms = kernel_terms(padded, grad_pre)
    summed, grad_padded = reduce_grads(local_terms, weight.shape[0], extend_x(grad_pre))
    input_grad = convolve(grad_padded, flipped).astype(jnp.bfloat16)
    weight_grad = summed * float(total) ** (-0.5)
    new_moment = 0.9 * moment + 0.1 * weight_grad
    new_second = 0.999 * second + 0.001 * weight_grad * weight_grad
    first_fix = 1.0 - 0.9**10
    second_fix = 1.0 - 0.999**10
    new_weight = weight - 0.001 * (new_moment / first_fix) / (
        jnp.sqrt(new_second / second_fix) + 1e-08
    )
    return (output[:, None], input_grad[:, None], weight_grad, new_weight, new_moment, new_second)


TILE = 16


def peers(n):
    me, sample = lax.axis_index("space"), lax.axis_index("sample")
    core, x = lax.rem(sample, 2), sample // 2
    return me, sample, core, x


class Field:
    def __init__(self, block, ends, faces, shifts, send, recv):
        self.block, self.ends, self.faces, self.shifts = block, ends, faces, shifts
        self.send, self.recv = send, recv
        me = lax.axis_index("space")
        self.me, self.cz, self.cy = me, lax.rem(me, GZ), lax.rem(me // GZ, GY)
        self.ny = block.shape[2] - 2

    def has(self, dy, dz):
        y, z = self.cy + dy, self.cz + dz
        return (y >= 0) & (y < GY) & (z >= 0) & (z < GZ)

    def extract(self):
        crops, nx, _, nz, _ = self.block.shape
        row = lax.broadcasted_iota(jnp.int32, (2 * nx, nx * nz), 0)
        col = lax.broadcasted_iota(jnp.int32, (2 * nx, nx * nz), 1)
        want = jnp.where(row < nx, row * nz + nz - 1, (row - nx) * nz)
        pick = jnp.where(col == want, 1.0, 0.0).astype(jnp.bfloat16)

        def step(y, _):
            for c in range(crops):
                rows = self.block[c, :, y + 1].reshape(nx * nz, -1)
                both = jnp.dot(pick, rows, preferred_element_type=jnp.float32).astype(jnp.bfloat16)
                self.faces[0, y, c] = both[:nx]
                self.faces[1, y, c] = both[nx:]
            return 0

        lax.fori_loop(0, self.ny, step, 0)

    def refs(self, dy, dz):
        last = self.ny - 1
        if dz == 0:
            src = self.block.at[:, :, last + 1 if dy > 0 else 1]
            dst = self.block.at[:, :, 0 if dy > 0 else last + 2]
            return src, dst
        side = 0 if dz > 0 else 1
        if dy == 0:
            return self.faces.at[side], self.ends.at[side, pl.ds(1, self.ny)]
        src = self.faces.at[side, last if dy > 0 else 0]
        return src, self.ends.at[side, 0 if dy > 0 else last + 2]

    def copy(self, k, to):
        src, dst = self.refs(*DIRS[k])
        return remote(src, dst, self.send.at[k], self.recv.at[k], space=to)

    def clear(self):
        for k, (dy, dz) in enumerate(DIRS):
            dst = self.refs(dy, dz)[1]

            @pl.when(jnp.logical_not(self.has(-dy, -dz)))
            def _():
                dst[...] = jnp.zeros(dst.shape, dst.dtype)

        nx = self.block.shape[1]
        for edge in (0, nx + 1):
            self.shifts[edge] = jnp.zeros(self.shifts.shape[1:], self.shifts.dtype)

    def start(self, faces_only):
        for k, (dy, dz) in enumerate(DIRS):
            if (dz == 0) == faces_only:

                @pl.when(self.has(dy, dz))
                def _():
                    self.copy(k, self.me + dy * GZ + dz).start()

    def finish(self):
        for k, (dy, dz) in enumerate(DIRS):

            @pl.when(self.has(-dy, -dz))
            def _():
                self.copy(k, self.me).wait_recv()

    def drain(self):
        for k, (dy, dz) in enumerate(DIRS):

            @pl.when(self.has(dy, dz))
            def _():
                self.copy(k, self.me).wait_send()

    def build(self):
        crops, nx, _, nz, ch = self.block.shape
        f32 = jnp.float32

        def step(y, _):
            out = ([], [], [])
            for c in range(crops):
                mid = self.block[c, :, y].astype(f32)
                low = self.ends[0, y, c].astype(f32)[:, None, :]
                high = self.ends[1, y, c].astype(f32)[:, None, :]
                z = lax.broadcasted_iota(jnp.int32, mid.shape, 1)
                out[0].append(jnp.where(z == 0, low, pltpu.roll(mid, 1, 1)))
                out[1].append(mid)
                out[2].append(jnp.where(z == nz - 1, high, pltpu.roll(mid, nz - 1, 1)))
            for kz in range(3):
                value = jnp.concatenate(out[kz], 1).astype(jnp.bfloat16)
                self.shifts[pl.ds(1, nx), y, :, kz * ch : (kz + 1) * ch] = value
            return 0

        lax.fori_loop(0, self.ny + 2, step, 0)

    def window(self, x0, kx, ky, step):
        rows = [
            self.shifts[pl.ds(x0 + kx, step), 2 * p + ky].reshape(-1, self.shifts.shape[-1])
            for p in range(self.ny // 2)
        ]
        return jnp.concatenate(rows, 0)

    def patch(self, x0, step):
        return jnp.concatenate([self.window(x0, kx, ky, step) for kx in range(3) for ky in range(4)], 1)


STEP = 4


def fused_kernel(
    n, scale,
    acts, cot, weight, moment_in, second_in,
    output, igrad, wgrad, nweight, nmoment, nsecond,
    xb, xe, xf, xs, zb, ze, zf, zs, cotv, w, moment, second,
    wall, w2, w2d, dzt, g, r1, s2, p2, s3, p3, total,
    ls, xhs, xhr, zhs, zhr,
    gzs, gzr, gxs, gxr, gys, gyr, gds, gdr, gcs, gcr,
    c1s, c1r, c2s, c2r, c3s, c3r, c4s, c4r,
):
    f32, bf16 = jnp.float32, jnp.bfloat16
    me, sample, core, x = peers(n)
    na = n // 2
    a, b = me // 2, lax.rem(me, 2)
    across, partner = (1 - x) * 2 + core, x * 2 + 1 - core
    beside = a * 2 + 1 - b
    groups = w.shape[0]
    q = wall.shape[1] // 4
    ch = w.shape[2]
    crops, nx, _, nz, _ = xb.shape
    ny = xb.shape[2] - 2

    load_x = pltpu.make_async_copy(acts, xb.at[:, :, pl.ds(1, ny)], ls.at[0])
    load_c = pltpu.make_async_copy(cot, cotv, ls.at[1])
    load_w = pltpu.make_async_copy(weight, w, ls.at[2])
    load_m = pltpu.make_async_copy(moment_in, moment, ls.at[3])
    load_s = pltpu.make_async_copy(second_in, second, ls.at[4])
    for load in (load_w, load_x, load_c, load_m, load_s):
        load.start()

    barrier = pltpu.get_barrier_semaphore()

    def greet_space(d, _):
        pl.semaphore_signal(barrier, 1, device_id={"space": lax.rem(me + d, n)}, device_id_type=MESH)
        return 0

    lax.fori_loop(1, n, greet_space, 0)
    for d in range(1, 4):
        pl.semaphore_signal(barrier, 1, device_id={"sample": lax.rem(sample + d, 4)}, device_id_type=MESH)
    pl.semaphore_signal(barrier, 1, device_id={"sample": across, "space": beside}, device_id_type=MESH)

    wall[me, pl.ds(groups, 4 * q - groups)] = jnp.zeros((4 * q - groups, TILE, ch), bf16)
    field = Field(xb, xe, xf, xs, xhs, xhr)
    dfield = Field(zb, ze, zf, zs, zhs, zhr)
    field.clear()
    dfield.clear()
    for kx in range(3):
        w2[pl.ds((kx * 4 + 3) * 24, 24), :, 0:ch] = jnp.zeros((24, TILE, ch), bf16)
        w2[pl.ds(kx * 96, 24), :, ch : 2 * ch] = jnp.zeros((24, TILE, ch), bf16)
        w2d[pl.ds((kx * 4 + 3) * 24, 24), :, 0:ch] = jnp.zeros((24, TILE, ch), bf16)
        w2d[pl.ds(kx * 96, 24), :, ch : 2 * ch] = jnp.zeros((24, TILE, ch), bf16)
    g[:, pl.ds(groups, 4 * q - groups)] = jnp.zeros((n, 4 * q - groups, TILE, ch), bf16)

    load_w.wait()
    wall[me, pl.ds(0, groups)] = w[...].astype(bf16)
    pl.semaphore_wait(barrier, n + 3)

    def piece(s, c, h):
        return wall.at[s, pl.ds((c * 2 + h) * q, q)]

    def column(d):
        return lax.rem(a + na - d, na) * 2 + b

    def other(d):
        return lax.rem(a + na - d, na) * 2 + 1 - b

    def z_copy(d):
        part = piece(me, core, x)
        return remote(part, part, gzs.at[d], gzr.at[d], space=lax.rem(a + d, na) * 2 + b)

    def z_wait(d):
        part = piece(column(d), core, x)
        return remote(part, part, gzs.at[d], gzr.at[d], space=beside)

    def x_copy(d):
        part = piece(column(d), core, x)
        return remote(part, part, gxs.at[d], gxr.at[d], sample=across)

    def x_wait(d):
        part = piece(column(d), core, 1 - x)
        return remote(part, part, gxs.at[d], gxr.at[d], sample=across)

    def y_copy(d):
        part = piece(column(d), core, x)
        return remote(part, part, gys.at[d], gyr.at[d], space=beside)

    def y_wait(d):
        part = piece(other(d), core, x)
        return remote(part, part, gys.at[d], gyr.at[d], space=beside)

    def d_copy(d):
        part = piece(column(d), core, x)
        return remote(part, part, gds.at[d], gdr.at[d], sample=across, space=beside)

    def d_wait(d):
        part = piece(other(d), core, 1 - x)
        return remote(part, part, gds.at[d], gdr.at[d], sample=across, space=beside)

    def half(s, c):
        return wall.at[s, pl.ds(c * 2 * q, 2 * q)]

    def c_copy(i, s):
        part = half(s, core)
        return remote(part, part, gcs.at[i], gcr.at[i], sample=partner)

    def c_wait(i, s):
        part = half(s, 1 - core)
        return remote(part, part, gcs.at[i], gcr.at[i], sample=partner)

    for d in range(1, na):
        z_copy(d).start()
    y_copy(0).start()
    d_copy(0).start()
    load_x.wait()
    field.start(True)
    field.extract()
    field.start(False)

    def place(s):
        def step(i, _):
            r = s * groups + i
            at = r + (r // 72) * 24
            tile = wall[s, i]
            w2[at, :, 0:ch] = tile
            w2[at + 24, :, ch : 2 * ch] = tile
            return 0

        lax.fori_loop(0, groups, step, 0)

    place(me)

    def forward(d, _):
        z_wait(d).wait_recv()
        y_copy(d).start()
        d_copy(d).start()
        x_copy(d).start()
        return 0

    lax.fori_loop(1, na, forward, 0)
    field.finish()
    field.build()

    def finish_plane(d, _):
        y_wait(d).wait_recv()
        d_wait(d).wait_recv()
        c_copy(na + d, other(d)).start()

        @pl.when(d > 0)
        def _():
            x_wait(d).wait_recv()
            c_copy(d, column(d)).start()

        return 0

    lax.fori_loop(0, na, finish_plane, 0)

    def arrive(d, _):
        c_wait(na + d, other(d)).wait_recv()
        place(other(d))

        @pl.when(d > 0)
        def _():
            c_wait(d, column(d)).wait_recv()
            place(column(d))

        return 0

    lax.fori_loop(0, na, arrive, 0)

    load_c.wait()
    rows = w2.shape[0] * TILE

    def chunk(i, _):
        x0 = i * STEP
        pre = jnp.dot(field.patch(x0, STEP), w2[...].reshape(rows, 2 * ch), preferred_element_type=f32)
        square = pre * pre
        tval = jnp.tanh(pre * (root_coef + root_coef * cubic_coef * square))
        gate = 0.5 * (1.0 + tval)
        value = (pre * gate).astype(bf16)
        slope = gate + (0.5 * pre) * (1.0 - tval * tval) * (root_coef + 3.0 * root_coef * cubic_coef * square)
        pieces = []
        m = STEP * TILE
        for p in range(ny // 2):
            line = []
            for h in range(2):
                up = jnp.concatenate([cotv[c, pl.ds(x0, STEP), 2 * p + h].astype(f32) for c in range(crops)], 1)
                dz = up.reshape(m, ch) * slope[p * m : (p + 1) * m, h * ch : (h + 1) * ch]
                line.append(dz)
                out = value[p * m : (p + 1) * m, h * ch : (h + 1) * ch].reshape(STEP, TILE, ch)
                dzr = dz.astype(bf16).reshape(STEP, TILE, ch)
                for c in range(crops):
                    output[c, pl.ds(x0, STEP), 2 * p + h] = out[:, c * nz : (c + 1) * nz]
                    zb[c, pl.ds(x0, STEP), 2 * p + h + 1] = dzr[:, c * nz : (c + 1) * nz]
            pieces.append(jnp.concatenate(line, 1))
        dzm = jnp.concatenate(pieces, 0)
        cols = dzm.shape[0]
        dzt[:, pl.ds(pl.multiple_of(i * cols, 128), cols)] = dzm.T.astype(bf16)
        return 0

    lax.fori_loop(0, nx // STEP, chunk, 0)

    dfield.start(True)
    dfield.extract()
    dfield.start(False)

    def one(o):
        return remote(g.at[o, pl.ds((1 - core) * 2 * q, 2 * q)], r1.at[o], c1s.at[o], c1r.at[o], sample=partner)

    def two(k, j):
        own = j * 2 + (b if k == 0 else 1 - b)
        side = x if k == 1 else 1 - x
        to = {"sample": across} if k == 0 else {"space": beside}
        if k == 2:
            to = {"sample": across, "space": beside}
        return remote(s2.at[own, pl.ds(side * q, q)], p2.at[k, j], c2s.at[k, j], c2r.at[k, j], **to)

    def three(d):
        j = lax.rem(a + d, na)
        return remote(s3.at[j], p3.at[d], c3s.at[d], c3r.at[d], space=j * 2 + b)

    def four(d):
        mine = total.at[core * 2 + x]
        return remote(mine, mine, c4s.at[d], c4r.at[d], sample=lax.rem(sample + 1 + d, 4))

    def send_one(o, _):
        one(o).start()
        return 0

    def send_two(o, _):
        one(o).wait_recv()
        s2[o] = (g[o, pl.ds(core * 2 * q, 2 * q)].astype(f32) + r1[o].astype(f32)).astype(bf16)
        j = o // 2

        @pl.when(lax.rem(o, 2) == b)
        def _():
            two(0, j).start()

        @pl.when(lax.rem(o, 2) != b)
        def _():
            two(2, j).start()
            two(1, j).start()

        return 0

    def done(kx):
        return (kx * 72) // groups

    def terms(kx, _):
        window = [
            jnp.concatenate([field.window(i * STEP, kx, ky, STEP) for ky in range(4)], 1)
            for i in range(nx // STEP)
        ]
        pair = jnp.dot(dzt[...], jnp.concatenate(window, 0), preferred_element_type=f32)
        for ky in range(3):
            k = 3 * ch
            both = pair[:ch, ky * k : (ky + 1) * k] + pair[ch:, (ky + 1) * k : (ky + 2) * k]
            for kz in range(3):
                tap = both[:, kz * ch : (kz + 1) * ch].T.astype(bf16).reshape(ch // TILE, TILE, ch)
                for t in range(ch // TILE):
                    r = kx * 72 + (ky * 3 + kz) * (ch // TILE) + t
                    g[r // groups, lax.rem(r, groups)] = tap[t]
        lax.fori_loop(done(kx), done(kx + 1), send_one, 0)

        @pl.when(kx > 0)
        def _():
            lax.fori_loop(done(kx - 1), done(kx), send_two, 0)

        return 0

    lax.fori_loop(0, 3, terms, 0)
    lax.fori_loop(done(2), n, send_two, 0)

    def flip(t, _):
        kx, r = t // 9, lax.rem(t, 9)
        ky, kz = r // 3, lax.rem(r, 3)
        src = (kx * 4 + ky) * 24 + kz * 8
        dst = ((2 - kx) * 4 + 2 - ky) * 24 + (2 - kz) * 8
        tap = w2[pl.ds(src, 8), :, 0:ch].reshape(ch, ch).astype(f32).T.astype(bf16).reshape(8, TILE, ch)
        w2d[pl.ds(dst, 8), :, 0:ch] = tap
        w2d[pl.ds(dst + 24, 8), :, ch : 2 * ch] = tap
        return 0

    lax.fori_loop(0, 27, flip, 0)
    dfield.finish()
    dfield.build()

    def sum_two(j, _):
        for k in range(3):
            two(k, j).wait_recv()
        own = s2[j * 2 + b, pl.ds(x * q, q)].astype(f32)
        s3[j] = (own + p2[0, j].astype(f32) + p2[1, j].astype(f32) + p2[2, j].astype(f32)).astype(bf16)
        return 0

    def back(i, _):
        x0 = i * STEP
        grad = jnp.dot(
            dfield.patch(x0, STEP), w2d[...].reshape(rows, 2 * ch), preferred_element_type=f32
        ).astype(bf16)
        m = STEP * TILE
        for p in range(ny // 2):
            for h in range(2):
                out = grad[p * m : (p + 1) * m, h * ch : (h + 1) * ch].reshape(STEP, TILE, ch)
                for c in range(crops):
                    igrad[c, pl.ds(x0, STEP), 2 * p + h] = out[:, c * nz : (c + 1) * nz]

        @pl.when(i == SUM_AT)
        def _():
            lax.fori_loop(0, na, sum_two, 0)
            for d in range(1, na):
                three(d).start()

        return 0

    lax.fori_loop(0, nx // STEP, back, 0)

    result = s3[a].astype(f32)
    for d in range(1, na):
        three(d).wait_recv()
        result = result + p3[d].astype(f32)
    total[core * 2 + x] = result
    for d in range(3):
        four(d).start()
    for d in range(3):
        four(d).wait()
    load_m.wait()
    load_s.wait()
    grad = total[...].reshape(4 * q, TILE, ch)[:groups] * scale
    mom = 0.9 * moment[...] + 0.1 * grad
    sec = 0.999 * second[...] + 0.001 * grad * grad
    first_fix = 1.0 - 0.9**10
    second_fix = 1.0 - 0.999**10
    wgrad[...] = grad
    nmoment[...] = mom
    nsecond[...] = sec
    nweight[...] = w[...] - 0.001 * (mom / first_fix) / (jnp.sqrt(sec / second_fix) + 1e-08)

    field.drain()
    dfield.drain()
    y_copy(0).wait_send()
    d_copy(0).wait_send()

    def drain_gather(d, _):
        z_copy(d).wait_send()
        y_copy(d).wait_send()
        d_copy(d).wait_send()
        x_copy(d).wait_send()
        c_copy(d, column(d)).wait_send()
        three(d).wait_send()
        return 0

    lax.fori_loop(1, na, drain_gather, 0)

    def drain_plane(d, _):
        c_copy(na + d, other(d)).wait_send()
        for k in range(3):
            two(k, d).wait_send()
        return 0

    lax.fori_loop(0, na, drain_plane, 0)

    def drain_one(o, _):
        one(o).wait_send()
        return 0

    lax.fori_loop(0, n, drain_one, 0)


def put_kernel(*refs):
    k = len(refs) // 2
    copies = [pltpu.make_async_copy(refs[i], refs[k + i], refs[-1].at[i]) for i in range(k)]
    for copy in copies:
        copy.start()
    for copy in copies:
        copy.wait()


SUM_AT = 1


def fused(acts, weight, moment, second, cotangent, scale):
    n = lax.axis_size("space")
    na = n // 2
    bf16, f32 = jnp.bfloat16, jnp.float32
    crops, nx, ny, nz, ch = acts.shape
    groups = weight.shape[0] // TILE
    q = -(-groups // 4)
    tiles = [v.reshape(groups, TILE, ch) for v in (weight, moment, second)]
    state = jax.ShapeDtypeStruct((groups, TILE, ch), f32)
    block = pltpu.VMEM((crops, nx, ny + 2, nz, ch), bf16)
    ends = pltpu.VMEM((2, ny + 2, crops, nx, ch), bf16)
    face = pltpu.VMEM((2, ny, crops, nx, ch), bf16)
    shifts = pltpu.VMEM((nx + 2, ny + 2, crops * nz, 3 * ch), bf16)
    wide = pltpu.VMEM((3 * 4 * 3 * ch // TILE, TILE, 2 * ch), bf16)
    HBM = pl.BlockSpec(memory_space=pltpu.HBM)

    def sem(*shape):
        return pltpu.SemaphoreType.DMA(shape)

    outs = pl.pallas_call(
        functools.partial(fused_kernel, n, scale),
        name="whole_step",
        out_shape=[jax.ShapeDtypeStruct(acts.shape, bf16), jax.ShapeDtypeStruct(acts.shape, bf16)] + [state] * 4,
        in_specs=[HBM] * 5,
        out_specs=[VM] * 6,
        scratch_shapes=[
            block, ends, face, shifts, block, ends, face, shifts,
            pltpu.VMEM((crops, nx, ny, nz, ch), bf16),
            pltpu.VMEM((groups, TILE, ch), f32), pltpu.VMEM((groups, TILE, ch), f32), pltpu.VMEM((groups, TILE, ch), f32),
            pltpu.VMEM((n, 4 * q, TILE, ch), bf16),
            wide, wide,
            pltpu.VMEM((2 * ch, crops * nx * ny * nz // 2), bf16),
            pltpu.VMEM((n, 4 * q, TILE, ch), bf16),
            pltpu.VMEM((n, 2 * q, TILE, ch), bf16),
            pltpu.VMEM((n, 2 * q, TILE, ch), bf16),
            pltpu.VMEM((3, na, q, TILE, ch), bf16),
            pltpu.VMEM((na, q, TILE, ch), bf16),
            pltpu.VMEM((na, q, TILE, ch), bf16),
            pltpu.VMEM((4, q, TILE, ch), f32),
            sem(5), sem(8), sem(8), sem(8), sem(8),
            sem(na), sem(na), sem(na), sem(na), sem(na), sem(na), sem(na), sem(na), sem(n), sem(n),
            sem(n), sem(n), sem(3, na), sem(3, na), sem(na), sem(na), sem(3), sem(3),
        ],
        compiler_params=pltpu.CompilerParams(
            collective_id=2, has_side_effects=True, vmem_limit_bytes=32 * 1024 * 1024
        ),
    )(*[pltpu.with_memory_space_constraint(v, pltpu.HBM) for v in (acts, cotangent, *tiles)])
    outs = pl.pallas_call(
        put_kernel,
        name="put",
        out_shape=like(outs),
        in_specs=[VM] * 6,
        out_specs=[HBM] * 6,
        scratch_shapes=[sem(6)],
        compiler_params=pltpu.CompilerParams(vmem_limit_bytes=2 * 1024 * 1024),
    )(*outs)
    return list(outs[:2]) + [v.reshape(weight.shape) for v in outs[2:]]


def local(acts, weight, moment, second, cotangent):
    n = lax.axis_size("space")
    crops, _, nx, ny, nz, channels = acts.shape
    total = crops * lax.axis_size("sample") * n * nx * ny * nz
    alone = n == GY * GZ and lax.axis_size("sample") == 4
    fits = crops * nz == TILE and nx == TILE and ny % 2 == 0 and channels == 128 and weight.shape[0] % TILE == 0
    if not (alone and fits):
        return plain(acts, weight, moment, second, cotangent)
    value, grad, *rest = fused(
        acts[:, 0], weight, moment, second, cotangent[:, 0], float(total) ** (-0.5)
    )
    return (value[:, None], grad[:, None], *rest)


def solution(mesh):
    in_specs = (
        P("sample", "space", None, None, None, None),
        P("space", None),
        P("space", None),
        P("space", None),
        P("sample", "space", None, None, None, None),
    )
    out_specs = (
        P("sample", "space", None, None, None, None),
        P("sample", "space", None, None, None, None),
        P("space", None),
        P("space", None),
        P("space", None),
        P("space", None),
    )
    return jax.shard_map(local, mesh=mesh, in_specs=in_specs, out_specs=out_specs, check_vma=False)
```

```python
import functools

import jax
import jax.numpy as jnp
from jax import lax
from jax.experimental import pallas as pl
from jax.experimental.pallas import tpu as pltpu
from jax.sharding import PartitionSpec as P

GY = 2
GZ = 4
MESH = pl.DeviceIdType.MESH
VM = pl.BlockSpec(memory_space=pltpu.VMEM)

root_coef = 0.7978845608
cubic_coef = 0.044715

SIDES = (1, -1)
DIRS = [(0, 1), (0, -1), (1, 0), (-1, 0)] + [(dy, dz) for dy in SIDES for dz in SIDES]


def shifted(value, axis, by):
    devices = lax.axis_size(axis)
    pairs = [(i, i + by) for i in range(devices) if 0 <= i + by < devices]
    return lax.ppermute(value, axis, pairs)


def convolve(field, kernel):
    return lax.conv_general_dilated(
        field,
        kernel,
        (1, 1, 1),
        "VALID",
        dimension_numbers=("NDHWC", "DHWIO", "NDHWC"),
        preferred_element_type=jnp.float32,
    )


def activate(pre):
    inner = root_coef * (pre + cubic_coef * pre * pre * pre)
    tval = jnp.tanh(inner)
    value = 0.5 * pre * (1.0 + tval)
    slope = 0.5 * (1.0 + tval) + 0.5 * pre * (1.0 - tval * tval) * root_coef * (
        1.0 + 3.0 * cubic_coef * pre * pre
    )
    return (value, slope)


def extend_x(field):
    groups = lax.axis_size("space") // (GY * GZ)
    if groups == 1:
        return jnp.pad(field, ((0, 0), (1, 1), (0, 0), (0, 0), (0, 0)))
    coord = lax.axis_index("space") // (GZ * GY)
    length = field.shape[1]
    below = shifted(field[:, length - 1 : length], "space", GY * GZ)
    above = shifted(field[:, :1], "space", -GY * GZ)
    below = jnp.where(coord > 0, below, jnp.zeros_like(below))
    above = jnp.where(coord < groups - 1, above, jnp.zeros_like(above))
    return jnp.concatenate([below, field, above], 1)


def faces(field):
    ends = {1: field.shape[2] - 1, -1: 0}
    endz = {1: field.shape[3] - 1, -1: 0}
    zf = jnp.stack([field[:, :, :, endz[d], :] for d in SIDES])
    yf = jnp.stack([field[:, :, ends[d], :, :] for d in SIDES])
    cf = jnp.stack([field[:, :, ends[dy], endz[dz], :] for dy in SIDES for dz in SIDES])
    return (zf, yf, cf)


def assemble(field, zf, yf, cf):
    mid = jnp.concatenate([zf[0][:, :, :, None], field, zf[1][:, :, :, None]], 3)
    rows = []
    for i in range(2):
        low, high = cf[2 * i][:, :, None, :], cf[2 * i + 1][:, :, None, :]
        rows.append(jnp.concatenate([low, yf[i], high], 2)[:, :, None])
    return jnp.concatenate([rows[0], mid, rows[1]], 2)


class Halo:
    def __init__(self, ins, outs, send, recv):
        me = lax.axis_index("space")
        self.me, self.send, self.recv = me, send, recv
        self.cz, self.cy = lax.rem(me, GZ), lax.rem(me // GZ, GY)
        self.src = [ins[k // 2].at[k % 2] if k < 4 else ins[2].at[k - 4] for k in range(8)]
        self.dst = [outs[k // 2].at[k % 2] if k < 4 else outs[2].at[k - 4] for k in range(8)]

    def has(self, dy, dz):
        y, z = self.cy + dy, self.cz + dz
        return (y >= 0) & (y < GY) & (z >= 0) & (z < GZ)

    def copy(self, k, to):
        return pltpu.make_async_remote_copy(
            src_ref=self.src[k],
            dst_ref=self.dst[k],
            send_sem=self.send.at[k],
            recv_sem=self.recv.at[k],
            device_id={"space": to},
            device_id_type=MESH,
        )

    def start(self):
        for k, (dy, dz) in enumerate(DIRS):

            @pl.when(self.has(dy, dz))
            def _():
                self.copy(k, self.me + dy * GZ + dz).start()

            @pl.when(jnp.logical_not(self.has(-dy, -dz)))
            def _():
                self.dst[k][...] = jnp.zeros(self.dst[k].shape, self.dst[k].dtype)

    def finish(self):
        for k, (dy, dz) in enumerate(DIRS):

            @pl.when(self.has(-dy, -dz))
            def _():
                self.copy(k, self.me).wait_recv()

            @pl.when(self.has(dy, dz))
            def _():
                self.copy(k, self.me).wait_send()


def greet(n, me, sample):
    barrier = pltpu.get_barrier_semaphore()

    def space_peer(d, _):
        pl.semaphore_signal(barrier, 1, device_id={"space": lax.rem(me + d, n)}, device_id_type=MESH)
        return 0

    lax.fori_loop(1, n, space_peer, 0)
    for d in range(1, 4):
        pl.semaphore_signal(barrier, 1, device_id={"sample": lax.rem(sample + d, 4)}, device_id_type=MESH)
    pl.semaphore_wait(barrier, n + 2)


def remote(src, dst, send, recv, **to):
    return pltpu.make_async_remote_copy(
        src_ref=src, dst_ref=dst, send_sem=send, recv_sem=recv, device_id=to, device_id_type=MESH
    )


LAG = 6


def gather_kernel(n, w, zi, yi, ci, out, zo, yo, co, hs, hr, as_, ar, bs, br, cs, cr):
    me, sample = lax.axis_index("space"), lax.axis_index("sample")
    core, x = lax.rem(sample, 2), sample // 2
    across, partner = (1 - x) * 2 + core, x * 2 + 1 - core
    greet(n, me, sample)
    halo = Halo((zi, yi, ci), (zo, yo, co), hs, hr)
    halo.start()

    def first(d, _):
        o = lax.rem(me + d, n)
        remote(w.at[core, x], out.at[me, core, x], as_.at[o], ar.at[me], space=o).start()
        return 0

    lax.fori_loop(1, n, first, 0)
    out[me] = w[...]

    def rest(t, _):
        @pl.when(t < n)
        def _():
            j = lax.rem(me - t + n, n)
            slot = out.at[j, core, x]
            remote(slot, slot, as_.at[j], ar.at[j], space=me).wait_recv()
            remote(slot, slot, bs.at[j], br.at[j], sample=across).start()

        @pl.when(t > LAG)
        def _():
            j = lax.rem(me - t + LAG + n, n)
            slot = out.at[j, core, 1 - x]
            remote(slot, slot, bs.at[j], br.at[j], sample=across).wait_recv()
            pair = out.at[j, core]
            remote(pair, pair, cs.at[j], cr.at[j], sample=partner).start()

        return 0

    lax.fori_loop(1, n + LAG, rest, 0)

    def last(d, _):
        o = lax.rem(me + d, n)
        pair = out.at[o, 1 - core]
        remote(pair, pair, cs.at[o], cr.at[o], sample=partner).wait_recv()
        remote(w.at[core, x], out.at[me, core, x], as_.at[o], ar.at[me], space=o).wait_send()
        slot = out.at[o, core, x]
        remote(slot, slot, bs.at[o], br.at[o], sample=across).wait_send()
        mine = out.at[o, core]
        remote(mine, mine, cs.at[o], cr.at[o], sample=partner).wait_send()
        return 0

    lax.fori_loop(1, n, last, 0)
    halo.finish()


def reduce_kernel(n, g, zi, yi, ci, out, zo, yo, co, r1, s2, r2, s3, r3, hs, hr, as_, ar, bs, br, cs, cr, ds, dr):
    me, sample = lax.axis_index("space"), lax.axis_index("sample")
    core, x = lax.rem(sample, 2), sample // 2
    across, partner = (1 - x) * 2 + core, x * 2 + 1 - core
    f32, bf16 = jnp.float32, jnp.bfloat16
    greet(n, me, sample)
    halo = Halo((zi, yi, ci), (zo, yo, co), hs, hr)
    halo.start()

    def owner(d):
        return lax.rem(me + 1 + d, n)

    def copy1(o):
        return remote(g.at[o, 1 - core], r1.at[o], as_.at[o], ar.at[o], sample=partner)

    def copy2(o):
        return remote(s2.at[o, 1 - x], r2.at[o], bs.at[o], br.at[o], sample=across)

    def copy3(o):
        return remote(s3.at[o], r3.at[me], cs.at[o], cr.at[me], space=o)

    def first(d, _):
        copy1(owner(d)).start()
        return 0

    lax.fori_loop(0, n, first, 0)

    def rest(t, _):
        @pl.when(t < n)
        def _():
            o = owner(t)
            copy1(o).wait_recv()
            s2[o] = (g[o, core].astype(f32) + r1[o].astype(f32)).astype(bf16)
            copy2(o).start()

        @pl.when(t >= LAG)
        def _():
            o = owner(t - LAG)
            copy2(o).wait_recv()
            s3[o] = (s2[o, x].astype(f32) + r2[o].astype(f32)).astype(bf16)

            @pl.when(t < n + LAG - 1)
            def _():
                copy3(o).start()

        return 0

    lax.fori_loop(0, n + LAG, rest, 0)

    def gather(d, total):
        j = lax.rem(me + n - d, n)
        remote(s3.at[j], r3.at[j], cs.at[j], cr.at[j], space=j).wait_recv()
        return total + r3[j].astype(f32)

    out[core, x] = lax.fori_loop(1, n, gather, s3[me].astype(f32))

    def copy4(d):
        mine = out.at[core, x]
        return remote(mine, mine, ds.at[d], dr.at[d], sample=lax.rem(sample + 1 + d, 4))

    for d in range(3):
        copy4(d).start()
    for d in range(3):
        copy4(d).wait()

    def drain(d, _):
        o = owner(d)
        copy1(o).wait_send()
        copy2(o).wait_send()

        @pl.when(d < n - 1)
        def _():
            copy3(o).wait_send()

        return 0

    lax.fori_loop(0, n, drain, 0)
    halo.finish()


def quarters(value, lead):
    rows = value.shape[-2]
    q = -(-rows // 4)
    if rows != 4 * q:
        value = jnp.pad(value, [(0, 0)] * (value.ndim - 2) + [(0, 4 * q - rows), (0, 0)])
    return value.reshape(*lead, 2, 2, q, value.shape[-1])


def whole_rows(value, rows):
    lead = value.shape[:-4]
    return value.reshape(*lead, -1, value.shape[-1])[..., :rows, :]


def like(arrays):
    return [jax.ShapeDtypeStruct(a.shape, a.dtype) for a in arrays]


def sems(*counts):
    return [pltpu.SemaphoreType.DMA((c,)) for c in counts]


def gather_weights(rows_bf, field):
    n = lax.axis_size("space")
    halo = faces(field)
    w = quarters(rows_bf, ())
    whole, zf, yf, cf = pl.pallas_call(
        functools.partial(gather_kernel, n),
        name="gather_and_halo",
        out_shape=[jax.ShapeDtypeStruct((n, *w.shape), w.dtype), *like(halo)],
        in_specs=[VM] * 4,
        out_specs=[VM] * 4,
        scratch_shapes=sems(8, 8, n, n, n, n, n, n),
        compiler_params=pltpu.CompilerParams(collective_id=0, has_side_effects=True),
    )(w, *halo)
    whole = whole_rows(whole, rows_bf.shape[0]).reshape(-1, rows_bf.shape[1])
    return whole, assemble(field, zf, yf, cf)


def reduce_grads(terms, rows, field):
    n = lax.axis_size("space")
    halo = faces(field)
    channels = terms.shape[-1]
    g = quarters(terms.reshape(n, rows, channels), (n,)).astype(jnp.bfloat16)
    q = g.shape[3]
    bf16 = jnp.bfloat16
    total, zf, yf, cf = pl.pallas_call(
        functools.partial(reduce_kernel, n),
        name="reduce_and_halo",
        out_shape=[jax.ShapeDtypeStruct((2, 2, q, channels), jnp.float32), *like(halo)],
        in_specs=[VM] * 4,
        out_specs=[VM] * 4,
        scratch_shapes=[
            pltpu.VMEM((n, 2, q, channels), bf16),
            pltpu.VMEM((n, 2, q, channels), bf16),
            pltpu.VMEM((n, q, channels), bf16),
            pltpu.VMEM((n, q, channels), bf16),
            pltpu.VMEM((n, q, channels), bf16),
            *sems(8, 8, n, n, n, n, n, n, 3, 3),
        ],
        compiler_params=pltpu.CompilerParams(collective_id=1, has_side_effects=True),
    )(g, *halo)
    return whole_rows(total, rows), assemble(field, zf, yf, cf)


def kernel_terms(padded, grad_pre):
    terms = lax.conv_general_dilated(
        padded,
        grad_pre,
        (1, 1, 1),
        "VALID",
        dimension_numbers=("CDHWN", "IDHWO", "DHWNC"),
        preferred_element_type=jnp.float32,
    )
    return terms.reshape(-1, terms.shape[-1])


def plain(acts, weight, moment, second, cotangent):
    field = acts[:, 0]
    grad_out = cotangent[:, 0]
    channels = weight.shape[1]
    rows_bf = weight.astype(jnp.bfloat16)
    whole, padded = gather_weights(rows_bf, extend_x(field))
    kernel = whole.reshape(3, 3, 3, channels, channels)
    pre = convolve(padded, kernel)
    value, slope = activate(pre)
    output = value.astype(jnp.bfloat16)
    grad_pre = (grad_out.astype(jnp.float32) * slope).astype(jnp.bfloat16)
    flipped = jnp.flip(kernel, (0, 1, 2)).transpose(0, 1, 2, 4, 3)
    total = (
        field.shape[0]
        * lax.axis_size("sample")
        * lax.axis_size("space")
        * field.shape[1]
        * field.shape[2]
        * field.shape[3]
    )
    local_terms = kernel_terms(padded, grad_pre)
    summed, grad_padded = reduce_grads(local_terms, weight.shape[0], extend_x(grad_pre))
    input_grad = convolve(grad_padded, flipped).astype(jnp.bfloat16)
    weight_grad = summed * float(total) ** (-0.5)
    new_moment = 0.9 * moment + 0.1 * weight_grad
    new_second = 0.999 * second + 0.001 * weight_grad * weight_grad
    first_fix = 1.0 - 0.9**10
    second_fix = 1.0 - 0.999**10
    new_weight = weight - 0.001 * (new_moment / first_fix) / (
        jnp.sqrt(new_second / second_fix) + 1e-08
    )
    return (output[:, None], input_grad[:, None], weight_grad, new_weight, new_moment, new_second)


TILE = 16


def peers(n):
    me, sample = lax.axis_index("space"), lax.axis_index("sample")
    core, x = lax.rem(sample, 2), sample // 2
    return me, sample, core, x


class Field:
    def __init__(self, block, ends, faces, shifts, send, recv):
        self.block, self.ends, self.faces, self.shifts = block, ends, faces, shifts
        self.send, self.recv = send, recv
        me = lax.axis_index("space")
        self.me, self.cz, self.cy = me, lax.rem(me, GZ), lax.rem(me // GZ, GY)
        self.ny = block.shape[2] - 2

    def has(self, dy, dz):
        y, z = self.cy + dy, self.cz + dz
        return (y >= 0) & (y < GY) & (z >= 0) & (z < GZ)

    def extract(self):
        crops, nx, _, nz, _ = self.block.shape
        row = lax.broadcasted_iota(jnp.int32, (2 * nx, nx * nz), 0)
        col = lax.broadcasted_iota(jnp.int32, (2 * nx, nx * nz), 1)
        want = jnp.where(row < nx, row * nz + nz - 1, (row - nx) * nz)
        pick = jnp.where(col == want, 1.0, 0.0).astype(jnp.bfloat16)

        for y in range(self.ny):
            for c in range(crops):
                rows = self.block[c, :, y + 1].reshape(nx * nz, -1)
                both = jnp.dot(pick, rows, preferred_element_type=jnp.float32).astype(jnp.bfloat16)
                self.faces[0, y, c] = both[:nx]
                self.faces[1, y, c] = both[nx:]

    def refs(self, dy, dz):
        last = self.ny - 1
        if dz == 0:
            src = self.block.at[:, :, last + 1 if dy > 0 else 1]
            dst = self.block.at[:, :, 0 if dy > 0 else last + 2]
            return src, dst
        side = 0 if dz > 0 else 1
        if dy == 0:
            return self.faces.at[side], self.ends.at[side, pl.ds(1, self.ny)]
        src = self.faces.at[side, last if dy > 0 else 0]
        return src, self.ends.at[side, 0 if dy > 0 else last + 2]

    def copy(self, k, to):
        src, dst = self.refs(*DIRS[k])
        return remote(src, dst, self.send.at[k], self.recv.at[k], space=to)

    def clear(self):
        for k, (dy, dz) in enumerate(DIRS):
            dst = self.refs(dy, dz)[1]

            @pl.when(jnp.logical_not(self.has(-dy, -dz)))
            def _():
                dst[...] = jnp.zeros(dst.shape, dst.dtype)

        nx = self.block.shape[1]
        for edge in (0, nx + 1):
            self.shifts[edge] = jnp.zeros(self.shifts.shape[1:], self.shifts.dtype)

    def start(self, faces_only):
        for k, (dy, dz) in enumerate(DIRS):
            if (dz == 0) == faces_only:

                @pl.when(self.has(dy, dz))
                def _():
                    self.copy(k, self.me + dy * GZ + dz).start()

    def finish(self):
        for k, (dy, dz) in enumerate(DIRS):

            @pl.when(self.has(-dy, -dz))
            def _():
                self.copy(k, self.me).wait_recv()

    def drain(self):
        for k, (dy, dz) in enumerate(DIRS):

            @pl.when(self.has(dy, dz))
            def _():
                self.copy(k, self.me).wait_send()

    def build(self):
        crops, nx, _, nz, ch = self.block.shape
        f32 = jnp.float32

        def step(y, _):
            out = ([], [], [])
            for c in range(crops):
                mid = self.block[c, :, y].astype(f32)
                low = self.ends[0, y, c].astype(f32)[:, None, :]
                high = self.ends[1, y, c].astype(f32)[:, None, :]
                z = lax.broadcasted_iota(jnp.int32, mid.shape, 1)
                out[0].append(jnp.where(z == 0, low, pltpu.roll(mid, 1, 1)))
                out[1].append(mid)
                out[2].append(jnp.where(z == nz - 1, high, pltpu.roll(mid, nz - 1, 1)))
            for kz in range(3):
                value = jnp.concatenate(out[kz], 1).astype(jnp.bfloat16)
                self.shifts[pl.ds(1, nx), y, :, kz * ch : (kz + 1) * ch] = value
            return 0

        lax.fori_loop(0, self.ny + 2, step, 0)

    def window(self, x0, kx, ky, step):
        rows = [
            self.shifts[pl.ds(x0 + kx, step), 2 * p + ky].reshape(-1, self.shifts.shape[-1])
            for p in range(self.ny // 2)
        ]
        return jnp.concatenate(rows, 0)

    def patch(self, x0, step):
        return jnp.concatenate([self.window(x0, kx, ky, step) for kx in range(3) for ky in range(4)], 1)


STEP = 4


def fused_kernel(
    n, scale,
    acts, cot, weight, moment_in, second_in,
    output, igrad, wgrad, nweight, nmoment, nsecond,
    xb, xe, xf, xs, zb, ze, zf, zs, cotv, w, moment, second,
    wall, w2, wt, dzt, g, r1, s2, p2, s3, p3, total,
    ls, xhs, xhr, zhs, zhr,
    gzs, gzr, gxs, gxr, gys, gyr, gds, gdr, gcs, gcr,
    c1s, c1r, c2s, c2r, c3s, c3r, c4s, c4r,
):
    f32, bf16 = jnp.float32, jnp.bfloat16
    me, sample, core, x = peers(n)
    na = n // 2
    a, b = me // 2, lax.rem(me, 2)
    across, partner = (1 - x) * 2 + core, x * 2 + 1 - core
    beside = a * 2 + 1 - b
    groups = w.shape[0]
    q = wall.shape[1] // 4
    ch = w.shape[2]
    crops, nx, _, nz, _ = xb.shape
    ny = xb.shape[2] - 2

    load_x = pltpu.make_async_copy(acts, xb.at[:, :, pl.ds(1, ny)], ls.at[0])
    load_c = pltpu.make_async_copy(cot, cotv, ls.at[1])
    load_w = pltpu.make_async_copy(weight, w, ls.at[2])
    load_m = pltpu.make_async_copy(moment_in, moment, ls.at[3])
    load_s = pltpu.make_async_copy(second_in, second, ls.at[4])
    for load in (load_w, load_x, load_c, load_m, load_s):
        load.start()

    barrier = pltpu.get_barrier_semaphore()

    def greet_space(d, _):
        pl.semaphore_signal(barrier, 1, device_id={"space": lax.rem(me + d, n)}, device_id_type=MESH)
        return 0

    lax.fori_loop(1, n, greet_space, 0)
    for d in range(1, 4):
        pl.semaphore_signal(barrier, 1, device_id={"sample": lax.rem(sample + d, 4)}, device_id_type=MESH)
    pl.semaphore_signal(barrier, 1, device_id={"sample": across, "space": beside}, device_id_type=MESH)

    wall[me, pl.ds(groups, 4 * q - groups)] = jnp.zeros((4 * q - groups, TILE, ch), bf16)
    field = Field(xb, xe, xf, xs, xhs, xhr)
    dfield = Field(zb, ze, zf, zs, zhs, zhr)
    load_w.wait()
    wall[me, pl.ds(0, groups)] = w[...].astype(bf16)
    pl.semaphore_wait(barrier, n + 3)

    def piece(s, c, h):
        return wall.at[s, pl.ds((c * 2 + h) * q, q)]

    def column(d):
        return lax.rem(a + na - d, na) * 2 + b

    def other(d):
        return lax.rem(a + na - d, na) * 2 + 1 - b

    def z_copy(d):
        part = piece(me, core, x)
        return remote(part, part, gzs.at[d], gzr.at[d], space=lax.rem(a + d, na) * 2 + b)

    def z_wait(d):
        part = piece(column(d), core, x)
        return remote(part, part, gzs.at[d], gzr.at[d], space=beside)

    def x_copy(d):
        part = piece(column(d), core, x)
        return remote(part, part, gxs.at[d], gxr.at[d], sample=across)

    def x_wait(d):
        part = piece(column(d), core, 1 - x)
        return remote(part, part, gxs.at[d], gxr.at[d], sample=across)

    def y_copy(d):
        part = piece(column(d), core, x)
        return remote(part, part, gys.at[d], gyr.at[d], space=beside)

    def y_wait(d):
        part = piece(other(d), core, x)
        return remote(part, part, gys.at[d], gyr.at[d], space=beside)

    def d_copy(d):
        part = piece(column(d), core, x)
        return remote(part, part, gds.at[d], gdr.at[d], sample=across, space=beside)

    def d_wait(d):
        part = piece(other(d), core, 1 - x)
        return remote(part, part, gds.at[d], gdr.at[d], sample=across, space=beside)

    def half(s, c):
        return wall.at[s, pl.ds(c * 2 * q, 2 * q)]

    def c_copy(i, s):
        part = half(s, core)
        return remote(part, part, gcs.at[i], gcr.at[i], sample=partner)

    def c_wait(i, s):
        part = half(s, 1 - core)
        return remote(part, part, gcs.at[i], gcr.at[i], sample=partner)

    for d in range(1, na):
        z_copy(d).start()
    y_copy(0).start()
    d_copy(0).start()
    load_x.wait()
    field.start(True)
    field.extract()
    field.start(False)
    field.clear()
    dfield.clear()
    for kx in range(3):
        w2[pl.ds((kx * 4 + 3) * 24, 24), :, 0:ch] = jnp.zeros((24, TILE, ch), bf16)
        w2[pl.ds(kx * 96, 24), :, ch : 2 * ch] = jnp.zeros((24, TILE, ch), bf16)
        wt[pl.ds(kx * 12 + 9, 3), pl.ds(0, 8)] = jnp.zeros((3, 8, TILE, ch), bf16)
        wt[pl.ds(kx * 12, 3), pl.ds(8, 8)] = jnp.zeros((3, 8, TILE, ch), bf16)
    g[:, pl.ds(groups, 4 * q - groups)] = jnp.zeros((n, 4 * q - groups, TILE, ch), bf16)


    def place(s):
        for i in range(groups):
            r = s * groups + i
            at = r + (r // 72) * 24
            tile = wall[s, i]
            w2[at, :, 0:ch] = tile
            w2[at + 24, :, ch : 2 * ch] = tile

    low_end = 2 * a < na

    def rank(j):
        return jnp.where(low_end, j, na - 1 - j)

    def forward(j, _):
        d = lax.rem(a - rank(j) + na, na)

        @pl.when(d > 0)
        def _():
            z_wait(d).wait_recv()
            y_copy(d).start()
            d_copy(d).start()
            x_copy(d).start()

        return 0

    lax.fori_loop(0, na, forward, 0)

    def relay(j, _):
        d = lax.rem(a - rank(j) + na, na)
        y_wait(d).wait_recv()
        d_wait(d).wait_recv()
        c_copy(na + d, other(d)).start()

        @pl.when(d > 0)
        def _():
            x_wait(d).wait_recv()
            c_copy(d, column(d)).start()

        return 0

    def arrive(j, _):
        d = lax.rem(a - rank(j) + na, na)

        @pl.when(d > 0)
        def _():
            c_wait(d, column(d)).wait_recv()

        place(column(d))
        c_wait(na + d, other(d)).wait_recv()
        place(other(d))
        return 0

    lax.fori_loop(0, 2, relay, 0)
    lax.fori_loop(0, 2, arrive, 0)
    lax.fori_loop(2, na, relay, 0)
    field.finish()
    field.build()
    lax.fori_loop(2, na, arrive, 0)
    load_c.wait()
    rows = w2.shape[0] * TILE
    m = STEP * TILE

    def chunk(i, _):
        x0 = i * STEP
        pre = jnp.dot(field.patch(x0, STEP), w2[...].reshape(rows, 2 * ch), preferred_element_type=f32)
        square = pre * pre
        tval = jnp.tanh(pre * (root_coef + root_coef * cubic_coef * square))
        gate = 0.5 * (1.0 + tval)
        value = (pre * gate).astype(bf16)
        slope = gate + (0.5 * pre) * (1.0 - tval * tval) * (root_coef + 3.0 * root_coef * cubic_coef * square)
        pieces = []
        for p in range(ny // 2):
            line = []
            for h in range(2):
                up = jnp.concatenate([cotv[c, pl.ds(x0, STEP), 2 * p + h].astype(f32) for c in range(crops)], 1)
                dz = up.reshape(m, ch) * slope[p * m : (p + 1) * m, h * ch : (h + 1) * ch]
                line.append(dz)
                out = value[p * m : (p + 1) * m, h * ch : (h + 1) * ch].reshape(STEP, TILE, ch)
                dzr = dz.astype(bf16).reshape(STEP, TILE, ch)
                for c in range(crops):
                    output[c, pl.ds(x0, STEP), 2 * p + h] = out[:, c * nz : (c + 1) * nz]
                    zb[c, pl.ds(x0, STEP), 2 * p + h + 1] = dzr[:, c * nz : (c + 1) * nz]
            pieces.append(jnp.concatenate(line, 1))
        dzm = jnp.concatenate(pieces, 0)
        cols = dzm.shape[0]
        dzt[:, pl.ds(pl.multiple_of(i * cols, 128), cols)] = dzm.T.astype(bf16)
        return 0

    lax.fori_loop(0, nx // STEP, chunk, 0)

    dfield.start(True)

    def one(o):
        return remote(g.at[o, pl.ds((1 - core) * 2 * q, 2 * q)], r1.at[o], c1s.at[o], c1r.at[o], sample=partner)

    def two(k, j):
        own = j * 2 + (b if k == 0 else 1 - b)
        side = x if k == 1 else 1 - x
        to = {"sample": across} if k == 0 else {"space": beside}
        if k == 2:
            to = {"sample": across, "space": beside}
        return remote(s2.at[own, pl.ds(side * q, q)], p2.at[k, j], c2s.at[k, j], c2r.at[k, j], **to)

    def three(d):
        j = lax.rem(a + d, na)
        return remote(s3.at[j], p3.at[d], c3s.at[d], c3r.at[d], space=j * 2 + b)

    def four(d):
        mine = total.at[core * 2 + x]
        return remote(mine, mine, c4s.at[d], c4r.at[d], sample=lax.rem(sample + 1 + d, 4))

    def send_one(o, _):
        one(o).start()
        return 0

    def send_two(o, _):
        one(o).wait_recv()
        s2[o] = (g[o, pl.ds(core * 2 * q, 2 * q)].astype(f32) + r1[o].astype(f32)).astype(bf16)
        j = o // 2

        @pl.when(lax.rem(o, 2) == b)
        def _():
            two(0, j).start()

        @pl.when(lax.rem(o, 2) != b)
        def _():
            two(2, j).start()
            two(1, j).start()

        return 0

    def done(kx):
        return (kx * 72) // groups

    def terms(kx, _):
        window = [
            jnp.concatenate([field.window(i * STEP, kx, ky, STEP) for ky in range(4)], 1)
            for i in range(nx // STEP)
        ]
        pair = jnp.dot(dzt[...], jnp.concatenate(window, 0), preferred_element_type=f32)
        for ky in range(3):
            k = 3 * ch
            both = pair[:ch, ky * k : (ky + 1) * k] + pair[ch:, (ky + 1) * k : (ky + 2) * k]
            for kz in range(3):
                tap = both[:, kz * ch : (kz + 1) * ch].T.astype(bf16).reshape(ch // TILE, TILE, ch)
                for t in range(ch // TILE):
                    r = kx * 72 + (ky * 3 + kz) * (ch // TILE) + t
                    g[r // groups, lax.rem(r, groups)] = tap[t]
        lax.fori_loop(done(kx), done(kx + 1), send_one, 0)

        @pl.when(kx == 0)
        def _():
            dfield.extract()
            dfield.start(False)
            lax.fori_loop(0, done(1), send_two, 0)

        @pl.when(kx == 2)
        def _():
            lax.fori_loop(done(1), done(2), send_two, 0)

        return 0

    lax.fori_loop(0, 3, terms, 0)

    def flip(t, _):
        kx = t // 9
        src = kx * 96 + (t - kx * 9) * 8
        tap = w2[pl.ds(src, 8), :, 0:ch]
        back_t = 26 - t
        col = back_t + (back_t // 9) * 3
        wt[col, pl.ds(0, 8)] = tap
        wt[col + 3, pl.ds(8, 8)] = tap
        return 0

    lax.fori_loop(0, 14, flip, 0)
    lax.fori_loop(done(2), n, send_two, 0)
    lax.fori_loop(14, 27, flip, 0)

    def sum_two(j, _):
        for k in range(3):
            two(k, j).wait_recv()
        own = s2[j * 2 + b, pl.ds(x * q, q)].astype(f32)
        s3[j] = (own + p2[0, j].astype(f32) + p2[1, j].astype(f32) + p2[2, j].astype(f32)).astype(bf16)

        @pl.when(j != a)
        def _():
            three(lax.rem(j - a + na, na)).start()

        return 0

    dfield.finish()
    dfield.build()

    def back(i, _):
        x0 = i * STEP
        taps = jnp.concatenate([wt[k].reshape(2 * ch, ch) for k in range(wt.shape[0])], 1)
        grad = lax.dot_general(
            dfield.patch(x0, STEP), taps, (((1,), (1,)), ((), ())), preferred_element_type=f32
        ).astype(bf16)
        for p in range(ny // 2):
            for h in range(2):
                out = grad[p * m : (p + 1) * m, h * ch : (h + 1) * ch].reshape(STEP, TILE, ch)
                for c in range(crops):
                    igrad[c, pl.ds(x0, STEP), 2 * p + h] = out[:, c * nz : (c + 1) * nz]

        @pl.when(i >= SUM_AT)
        def _():
            lax.fori_loop((i - SUM_AT) * 2, (i - SUM_AT) * 2 + 2, sum_two, 0)

        return 0

    lax.fori_loop(0, nx // STEP, back, 0)

    result = s3[a].astype(f32)
    for d in range(1, na):
        three(d).wait_recv()
        result = result + p3[d].astype(f32)
    total[core * 2 + x] = result.astype(bf16)
    for d in range(3):
        four(d).start()
    for d in range(3):
        four(d).wait()
    load_m.wait()
    load_s.wait()
    grad = total[...].reshape(4 * q, TILE, ch)[:groups].astype(f32) * scale
    mom = 0.9 * moment[...] + 0.1 * grad
    sec = 0.999 * second[...] + 0.001 * grad * grad
    first_fix = 1.0 - 0.9**10
    second_fix = 1.0 - 0.999**10
    wgrad[...] = grad
    nmoment[...] = mom
    nsecond[...] = sec
    nweight[...] = w[...] - 0.001 * (mom / first_fix) / (jnp.sqrt(sec / second_fix) + 1e-08)

    field.drain()
    dfield.drain()
    y_copy(0).wait_send()
    d_copy(0).wait_send()

    def drain_gather(d, _):
        z_copy(d).wait_send()
        y_copy(d).wait_send()
        d_copy(d).wait_send()
        x_copy(d).wait_send()
        c_copy(d, column(d)).wait_send()
        three(d).wait_send()
        return 0

    lax.fori_loop(1, na, drain_gather, 0)

    def drain_plane(d, _):
        c_copy(na + d, other(d)).wait_send()
        for k in range(3):
            two(k, d).wait_send()
        return 0

    lax.fori_loop(0, na, drain_plane, 0)

    def drain_one(o, _):
        one(o).wait_send()
        return 0

    lax.fori_loop(0, n, drain_one, 0)


SUM_AT = 2


def put_kernel(*refs):
    k = len(refs) // 2
    copies = [pltpu.make_async_copy(refs[i], refs[k + i], refs[-1].at[i]) for i in range(k)]
    for copy in copies:
        copy.start()
    for copy in copies:
        copy.wait()


def fused(acts, weight, moment, second, cotangent, scale):
    n = lax.axis_size("space")
    na = n // 2
    bf16, f32 = jnp.bfloat16, jnp.float32
    crops, nx, ny, nz, ch = acts.shape
    groups = weight.shape[0] // TILE
    q = -(-groups // 4)
    tiles = [v.reshape(groups, TILE, ch) for v in (weight, moment, second)]
    state = jax.ShapeDtypeStruct((groups, TILE, ch), f32)
    block = pltpu.VMEM((crops, nx, ny + 2, nz, ch), bf16)
    ends = pltpu.VMEM((2, ny + 2, crops, nx, ch), bf16)
    face = pltpu.VMEM((2, ny, crops, nx, ch), bf16)
    shifts = pltpu.VMEM((nx + 2, ny + 2, crops * nz, 3 * ch), bf16)
    wide = pltpu.VMEM((3 * 4 * 3 * ch // TILE, TILE, 2 * ch), bf16)
    HBM = pl.BlockSpec(memory_space=pltpu.HBM)

    def sem(*shape):
        return pltpu.SemaphoreType.DMA(shape)

    outs = pl.pallas_call(
        functools.partial(fused_kernel, n, scale),
        name="whole_step",
        out_shape=[jax.ShapeDtypeStruct(acts.shape, bf16), jax.ShapeDtypeStruct(acts.shape, bf16)] + [state] * 4,
        in_specs=[HBM] * 5,
        out_specs=[VM] * 6,
        scratch_shapes=[
            block, ends, face, shifts, block, ends, face, shifts,
            pltpu.VMEM((crops, nx, ny, nz, ch), bf16),
            pltpu.VMEM((groups, TILE, ch), f32), pltpu.VMEM((groups, TILE, ch), f32), pltpu.VMEM((groups, TILE, ch), f32),
            pltpu.VMEM((n, 4 * q, TILE, ch), bf16),
            wide, pltpu.VMEM((36, 2 * ch // TILE, TILE, ch), bf16),
            pltpu.VMEM((2 * ch, crops * nx * ny * nz // 2), bf16),
            pltpu.VMEM((n, 4 * q, TILE, ch), bf16),
            pltpu.VMEM((n, 2 * q, TILE, ch), bf16),
            pltpu.VMEM((n, 2 * q, TILE, ch), bf16),
            pltpu.VMEM((3, na, q, TILE, ch), bf16),
            pltpu.VMEM((na, q, TILE, ch), bf16),
            pltpu.VMEM((na, q, TILE, ch), bf16),
            pltpu.VMEM((4, q, TILE, ch), bf16),
            sem(5), sem(8), sem(8), sem(8), sem(8),
            sem(na), sem(na), sem(na), sem(na), sem(na), sem(na), sem(na), sem(na), sem(n), sem(n),
            sem(n), sem(n), sem(3, na), sem(3, na), sem(na), sem(na), sem(3), sem(3),
        ],
        compiler_params=pltpu.CompilerParams(
            collective_id=2, has_side_effects=True, vmem_limit_bytes=32 * 1024 * 1024
        ),
    )(*[pltpu.with_memory_space_constraint(v, pltpu.HBM) for v in (acts, cotangent, *tiles)])
    outs = pl.pallas_call(
        put_kernel,
        name="put",
        out_shape=like(outs),
        in_specs=[VM] * 6,
        out_specs=[HBM] * 6,
        scratch_shapes=[sem(6)],
        compiler_params=pltpu.CompilerParams(vmem_limit_bytes=2 * 1024 * 1024),
    )(*outs)
    return list(outs[:2]) + [v.reshape(weight.shape) for v in outs[2:]]


def local(acts, weight, moment, second, cotangent):
    n = lax.axis_size("space")
    crops, _, nx, ny, nz, channels = acts.shape
    total = crops * lax.axis_size("sample") * n * nx * ny * nz
    alone = n == GY * GZ and lax.axis_size("sample") == 4
    fits = crops * nz == TILE and nx == TILE and ny % 2 == 0 and channels == 128 and weight.shape[0] % TILE == 0
    if not (alone and fits):
        return plain(acts, weight, moment, second, cotangent)
    value, grad, *rest = fused(
        acts[:, 0], weight, moment, second, cotangent[:, 0], float(total) ** (-0.5)
    )
    return (value[:, None], grad[:, None], *rest)


def solution(mesh):
    in_specs = (
        P("sample", "space", None, None, None, None),
        P("space", None),
        P("space", None),
        P("space", None),
        P("sample", "space", None, None, None, None),
    )
    out_specs = (
        P("sample", "space", None, None, None, None),
        P("sample", "space", None, None, None, None),
        P("space", None),
        P("space", None),
        P("space", None),
        P("space", None),
    )
    return jax.shard_map(local, mesh=mesh, in_specs=in_specs, out_specs=out_specs, check_vma=False)
```

```python
import functools

import jax
import jax.numpy as jnp
from jax import lax
from jax.experimental import pallas as pl
from jax.experimental.pallas import tpu as pltpu
from jax.sharding import PartitionSpec as P

GY = 2
GZ = 4
MESH = pl.DeviceIdType.MESH
VM = pl.BlockSpec(memory_space=pltpu.VMEM)

root_coef = 0.7978845608
cubic_coef = 0.044715

SIDES = (1, -1)
DIRS = [(0, 1), (0, -1), (1, 0), (-1, 0)] + [(dy, dz) for dy in SIDES for dz in SIDES]


def shifted(value, axis, by):
    devices = lax.axis_size(axis)
    pairs = [(i, i + by) for i in range(devices) if 0 <= i + by < devices]
    return lax.ppermute(value, axis, pairs)


def convolve(field, kernel):
    return lax.conv_general_dilated(
        field,
        kernel,
        (1, 1, 1),
        "VALID",
        dimension_numbers=("NDHWC", "DHWIO", "NDHWC"),
        preferred_element_type=jnp.float32,
    )


def activate(pre):
    inner = root_coef * (pre + cubic_coef * pre * pre * pre)
    tval = jnp.tanh(inner)
    value = 0.5 * pre * (1.0 + tval)
    slope = 0.5 * (1.0 + tval) + 0.5 * pre * (1.0 - tval * tval) * root_coef * (
        1.0 + 3.0 * cubic_coef * pre * pre
    )
    return (value, slope)


def extend_x(field):
    groups = lax.axis_size("space") // (GY * GZ)
    if groups == 1:
        return jnp.pad(field, ((0, 0), (1, 1), (0, 0), (0, 0), (0, 0)))
    coord = lax.axis_index("space") // (GZ * GY)
    length = field.shape[1]
    below = shifted(field[:, length - 1 : length], "space", GY * GZ)
    above = shifted(field[:, :1], "space", -GY * GZ)
    below = jnp.where(coord > 0, below, jnp.zeros_like(below))
    above = jnp.where(coord < groups - 1, above, jnp.zeros_like(above))
    return jnp.concatenate([below, field, above], 1)


def faces(field):
    ends = {1: field.shape[2] - 1, -1: 0}
    endz = {1: field.shape[3] - 1, -1: 0}
    zf = jnp.stack([field[:, :, :, endz[d], :] for d in SIDES])
    yf = jnp.stack([field[:, :, ends[d], :, :] for d in SIDES])
    cf = jnp.stack([field[:, :, ends[dy], endz[dz], :] for dy in SIDES for dz in SIDES])
    return (zf, yf, cf)


def assemble(field, zf, yf, cf):
    mid = jnp.concatenate([zf[0][:, :, :, None], field, zf[1][:, :, :, None]], 3)
    rows = []
    for i in range(2):
        low, high = cf[2 * i][:, :, None, :], cf[2 * i + 1][:, :, None, :]
        rows.append(jnp.concatenate([low, yf[i], high], 2)[:, :, None])
    return jnp.concatenate([rows[0], mid, rows[1]], 2)


class Halo:
    def __init__(self, ins, outs, send, recv):
        me = lax.axis_index("space")
        self.me, self.send, self.recv = me, send, recv
        self.cz, self.cy = lax.rem(me, GZ), lax.rem(me // GZ, GY)
        self.src = [ins[k // 2].at[k % 2] if k < 4 else ins[2].at[k - 4] for k in range(8)]
        self.dst = [outs[k // 2].at[k % 2] if k < 4 else outs[2].at[k - 4] for k in range(8)]

    def has(self, dy, dz):
        y, z = self.cy + dy, self.cz + dz
        return (y >= 0) & (y < GY) & (z >= 0) & (z < GZ)

    def copy(self, k, to):
        return pltpu.make_async_remote_copy(
            src_ref=self.src[k],
            dst_ref=self.dst[k],
            send_sem=self.send.at[k],
            recv_sem=self.recv.at[k],
            device_id={"space": to},
            device_id_type=MESH,
        )

    def start(self):
        for k, (dy, dz) in enumerate(DIRS):

            @pl.when(self.has(dy, dz))
            def _():
                self.copy(k, self.me + dy * GZ + dz).start()

            @pl.when(jnp.logical_not(self.has(-dy, -dz)))
            def _():
                self.dst[k][...] = jnp.zeros(self.dst[k].shape, self.dst[k].dtype)

    def finish(self):
        for k, (dy, dz) in enumerate(DIRS):

            @pl.when(self.has(-dy, -dz))
            def _():
                self.copy(k, self.me).wait_recv()

            @pl.when(self.has(dy, dz))
            def _():
                self.copy(k, self.me).wait_send()


def greet(n, me, sample):
    barrier = pltpu.get_barrier_semaphore()

    def space_peer(d, _):
        pl.semaphore_signal(barrier, 1, device_id={"space": lax.rem(me + d, n)}, device_id_type=MESH)
        return 0

    lax.fori_loop(1, n, space_peer, 0)
    for d in range(1, 4):
        pl.semaphore_signal(barrier, 1, device_id={"sample": lax.rem(sample + d, 4)}, device_id_type=MESH)
    pl.semaphore_wait(barrier, n + 2)


def remote(src, dst, send, recv, **to):
    return pltpu.make_async_remote_copy(
        src_ref=src, dst_ref=dst, send_sem=send, recv_sem=recv, device_id=to, device_id_type=MESH
    )


LAG = 6


def gather_kernel(n, w, zi, yi, ci, out, zo, yo, co, hs, hr, as_, ar, bs, br, cs, cr):
    me, sample = lax.axis_index("space"), lax.axis_index("sample")
    core, x = lax.rem(sample, 2), sample // 2
    across, partner = (1 - x) * 2 + core, x * 2 + 1 - core
    greet(n, me, sample)
    halo = Halo((zi, yi, ci), (zo, yo, co), hs, hr)
    halo.start()

    def first(d, _):
        o = lax.rem(me + d, n)
        remote(w.at[core, x], out.at[me, core, x], as_.at[o], ar.at[me], space=o).start()
        return 0

    lax.fori_loop(1, n, first, 0)
    out[me] = w[...]

    def rest(t, _):
        @pl.when(t < n)
        def _():
            j = lax.rem(me - t + n, n)
            slot = out.at[j, core, x]
            remote(slot, slot, as_.at[j], ar.at[j], space=me).wait_recv()
            remote(slot, slot, bs.at[j], br.at[j], sample=across).start()

        @pl.when(t > LAG)
        def _():
            j = lax.rem(me - t + LAG + n, n)
            slot = out.at[j, core, 1 - x]
            remote(slot, slot, bs.at[j], br.at[j], sample=across).wait_recv()
            pair = out.at[j, core]
            remote(pair, pair, cs.at[j], cr.at[j], sample=partner).start()

        return 0

    lax.fori_loop(1, n + LAG, rest, 0)

    def last(d, _):
        o = lax.rem(me + d, n)
        pair = out.at[o, 1 - core]
        remote(pair, pair, cs.at[o], cr.at[o], sample=partner).wait_recv()
        remote(w.at[core, x], out.at[me, core, x], as_.at[o], ar.at[me], space=o).wait_send()
        slot = out.at[o, core, x]
        remote(slot, slot, bs.at[o], br.at[o], sample=across).wait_send()
        mine = out.at[o, core]
        remote(mine, mine, cs.at[o], cr.at[o], sample=partner).wait_send()
        return 0

    lax.fori_loop(1, n, last, 0)
    halo.finish()


def reduce_kernel(n, g, zi, yi, ci, out, zo, yo, co, r1, s2, r2, s3, r3, hs, hr, as_, ar, bs, br, cs, cr, ds, dr):
    me, sample = lax.axis_index("space"), lax.axis_index("sample")
    core, x = lax.rem(sample, 2), sample // 2
    across, partner = (1 - x) * 2 + core, x * 2 + 1 - core
    f32, bf16 = jnp.float32, jnp.bfloat16
    greet(n, me, sample)
    halo = Halo((zi, yi, ci), (zo, yo, co), hs, hr)
    halo.start()

    def owner(d):
        return lax.rem(me + 1 + d, n)

    def copy1(o):
        return remote(g.at[o, 1 - core], r1.at[o], as_.at[o], ar.at[o], sample=partner)

    def copy2(o):
        return remote(s2.at[o, 1 - x], r2.at[o], bs.at[o], br.at[o], sample=across)

    def copy3(o):
        return remote(s3.at[o], r3.at[me], cs.at[o], cr.at[me], space=o)

    def first(d, _):
        copy1(owner(d)).start()
        return 0

    lax.fori_loop(0, n, first, 0)

    def rest(t, _):
        @pl.when(t < n)
        def _():
            o = owner(t)
            copy1(o).wait_recv()
            s2[o] = (g[o, core].astype(f32) + r1[o].astype(f32)).astype(bf16)
            copy2(o).start()

        @pl.when(t >= LAG)
        def _():
            o = owner(t - LAG)
            copy2(o).wait_recv()
            s3[o] = (s2[o, x].astype(f32) + r2[o].astype(f32)).astype(bf16)

            @pl.when(t < n + LAG - 1)
            def _():
                copy3(o).start()

        return 0

    lax.fori_loop(0, n + LAG, rest, 0)

    def gather(d, total):
        j = lax.rem(me + n - d, n)
        remote(s3.at[j], r3.at[j], cs.at[j], cr.at[j], space=j).wait_recv()
        return total + r3[j].astype(f32)

    out[core, x] = lax.fori_loop(1, n, gather, s3[me].astype(f32))

    def copy4(d):
        mine = out.at[core, x]
        return remote(mine, mine, ds.at[d], dr.at[d], sample=lax.rem(sample + 1 + d, 4))

    for d in range(3):
        copy4(d).start()
    for d in range(3):
        copy4(d).wait()

    def drain(d, _):
        o = owner(d)
        copy1(o).wait_send()
        copy2(o).wait_send()

        @pl.when(d < n - 1)
        def _():
            copy3(o).wait_send()

        return 0

    lax.fori_loop(0, n, drain, 0)
    halo.finish()


def quarters(value, lead):
    rows = value.shape[-2]
    q = -(-rows // 4)
    if rows != 4 * q:
        value = jnp.pad(value, [(0, 0)] * (value.ndim - 2) + [(0, 4 * q - rows), (0, 0)])
    return value.reshape(*lead, 2, 2, q, value.shape[-1])


def whole_rows(value, rows):
    lead = value.shape[:-4]
    return value.reshape(*lead, -1, value.shape[-1])[..., :rows, :]


def like(arrays):
    return [jax.ShapeDtypeStruct(a.shape, a.dtype) for a in arrays]


def sems(*counts):
    return [pltpu.SemaphoreType.DMA((c,)) for c in counts]


def gather_weights(rows_bf, field):
    n = lax.axis_size("space")
    halo = faces(field)
    w = quarters(rows_bf, ())
    whole, zf, yf, cf = pl.pallas_call(
        functools.partial(gather_kernel, n),
        name="gather_and_halo",
        out_shape=[jax.ShapeDtypeStruct((n, *w.shape), w.dtype), *like(halo)],
        in_specs=[VM] * 4,
        out_specs=[VM] * 4,
        scratch_shapes=sems(8, 8, n, n, n, n, n, n),
        compiler_params=pltpu.CompilerParams(collective_id=0, has_side_effects=True),
    )(w, *halo)
    whole = whole_rows(whole, rows_bf.shape[0]).reshape(-1, rows_bf.shape[1])
    return whole, assemble(field, zf, yf, cf)


def reduce_grads(terms, rows, field):
    n = lax.axis_size("space")
    halo = faces(field)
    channels = terms.shape[-1]
    g = quarters(terms.reshape(n, rows, channels), (n,)).astype(jnp.bfloat16)
    q = g.shape[3]
    bf16 = jnp.bfloat16
    total, zf, yf, cf = pl.pallas_call(
        functools.partial(reduce_kernel, n),
        name="reduce_and_halo",
        out_shape=[jax.ShapeDtypeStruct((2, 2, q, channels), jnp.float32), *like(halo)],
        in_specs=[VM] * 4,
        out_specs=[VM] * 4,
        scratch_shapes=[
            pltpu.VMEM((n, 2, q, channels), bf16),
            pltpu.VMEM((n, 2, q, channels), bf16),
            pltpu.VMEM((n, q, channels), bf16),
            pltpu.VMEM((n, q, channels), bf16),
            pltpu.VMEM((n, q, channels), bf16),
            *sems(8, 8, n, n, n, n, n, n, 3, 3),
        ],
        compiler_params=pltpu.CompilerParams(collective_id=1, has_side_effects=True),
    )(g, *halo)
    return whole_rows(total, rows), assemble(field, zf, yf, cf)


def kernel_terms(padded, grad_pre):
    terms = lax.conv_general_dilated(
        padded,
        grad_pre,
        (1, 1, 1),
        "VALID",
        dimension_numbers=("CDHWN", "IDHWO", "DHWNC"),
        preferred_element_type=jnp.float32,
    )
    return terms.reshape(-1, terms.shape[-1])


def plain(acts, weight, moment, second, cotangent):
    field = acts[:, 0]
    grad_out = cotangent[:, 0]
    channels = weight.shape[1]
    rows_bf = weight.astype(jnp.bfloat16)
    whole, padded = gather_weights(rows_bf, extend_x(field))
    kernel = whole.reshape(3, 3, 3, channels, channels)
    pre = convolve(padded, kernel)
    value, slope = activate(pre)
    output = value.astype(jnp.bfloat16)
    grad_pre = (grad_out.astype(jnp.float32) * slope).astype(jnp.bfloat16)
    flipped = jnp.flip(kernel, (0, 1, 2)).transpose(0, 1, 2, 4, 3)
    total = (
        field.shape[0]
        * lax.axis_size("sample")
        * lax.axis_size("space")
        * field.shape[1]
        * field.shape[2]
        * field.shape[3]
    )
    local_terms = kernel_terms(padded, grad_pre)
    summed, grad_padded = reduce_grads(local_terms, weight.shape[0], extend_x(grad_pre))
    input_grad = convolve(grad_padded, flipped).astype(jnp.bfloat16)
    weight_grad = summed * float(total) ** (-0.5)
    new_moment = 0.9 * moment + 0.1 * weight_grad
    new_second = 0.999 * second + 0.001 * weight_grad * weight_grad
    first_fix = 1.0 - 0.9**10
    second_fix = 1.0 - 0.999**10
    new_weight = weight - 0.001 * (new_moment / first_fix) / (
        jnp.sqrt(new_second / second_fix) + 1e-08
    )
    return (output[:, None], input_grad[:, None], weight_grad, new_weight, new_moment, new_second)


TILE = 16


def peers(n):
    me, sample = lax.axis_index("space"), lax.axis_index("sample")
    core, x = lax.rem(sample, 2), sample // 2
    return me, sample, core, x


class Field:
    def __init__(self, block, ends, faces, shifts, send, recv):
        self.block, self.ends, self.faces, self.shifts = block, ends, faces, shifts
        self.send, self.recv = send, recv
        me = lax.axis_index("space")
        self.me, self.cz, self.cy = me, lax.rem(me, GZ), lax.rem(me // GZ, GY)
        self.ny = block.shape[2] - 2

    def has(self, dy, dz):
        y, z = self.cy + dy, self.cz + dz
        return (y >= 0) & (y < GY) & (z >= 0) & (z < GZ)

    def extract(self):
        crops, nx, _, nz, _ = self.block.shape
        row = lax.broadcasted_iota(jnp.int32, (2 * nx, nx * nz), 0)
        col = lax.broadcasted_iota(jnp.int32, (2 * nx, nx * nz), 1)
        want = jnp.where(row < nx, row * nz + nz - 1, (row - nx) * nz)
        pick = jnp.where(col == want, 1.0, 0.0).astype(jnp.bfloat16)

        for y in range(self.ny):
            for c in range(crops):
                rows = self.block[c, :, y + 1].reshape(nx * nz, -1)
                both = jnp.dot(pick, rows, preferred_element_type=jnp.float32).astype(jnp.bfloat16)
                self.faces[0, y, c] = both[:nx]
                self.faces[1, y, c] = both[nx:]

    def refs(self, dy, dz):
        last = self.ny - 1
        if dz == 0:
            src = self.block.at[:, :, last + 1 if dy > 0 else 1]
            dst = self.block.at[:, :, 0 if dy > 0 else last + 2]
            return src, dst
        side = 0 if dz > 0 else 1
        if dy == 0:
            return self.faces.at[side], self.ends.at[side, pl.ds(1, self.ny)]
        src = self.faces.at[side, last if dy > 0 else 0]
        return src, self.ends.at[side, 0 if dy > 0 else last + 2]

    def copy(self, k, to):
        src, dst = self.refs(*DIRS[k])
        return remote(src, dst, self.send.at[k], self.recv.at[k], space=to)

    def clear(self):
        for k, (dy, dz) in enumerate(DIRS):
            dst = self.refs(dy, dz)[1]

            @pl.when(jnp.logical_not(self.has(-dy, -dz)))
            def _():
                dst[...] = jnp.zeros(dst.shape, dst.dtype)

        nx = self.block.shape[1]
        for edge in (0, nx + 1):
            self.shifts[edge] = jnp.zeros(self.shifts.shape[1:], self.shifts.dtype)

    def start(self, faces_only):
        for k, (dy, dz) in enumerate(DIRS):
            if (dz == 0) == faces_only:

                @pl.when(self.has(dy, dz))
                def _():
                    self.copy(k, self.me + dy * GZ + dz).start()

    def finish(self):
        for k, (dy, dz) in enumerate(DIRS):

            @pl.when(self.has(-dy, -dz))
            def _():
                self.copy(k, self.me).wait_recv()

    def drain(self):
        for k, (dy, dz) in enumerate(DIRS):

            @pl.when(self.has(dy, dz))
            def _():
                self.copy(k, self.me).wait_send()

    def build(self):
        crops, nx, _, nz, ch = self.block.shape
        f32 = jnp.float32

        def step(y, _):
            out = ([], [], [])
            for c in range(crops):
                mid = self.block[c, :, y].astype(f32)
                low = self.ends[0, y, c].astype(f32)[:, None, :]
                high = self.ends[1, y, c].astype(f32)[:, None, :]
                z = lax.broadcasted_iota(jnp.int32, mid.shape, 1)
                out[0].append(jnp.where(z == 0, low, pltpu.roll(mid, 1, 1)))
                out[1].append(mid)
                out[2].append(jnp.where(z == nz - 1, high, pltpu.roll(mid, nz - 1, 1)))
            for kz in range(3):
                value = jnp.concatenate(out[kz], 1).astype(jnp.bfloat16)
                self.shifts[pl.ds(1, nx), y, :, kz * ch : (kz + 1) * ch] = value
            return 0

        lax.fori_loop(0, self.ny + 2, step, 0)

    def window(self, x0, kx, ky, step):
        rows = [
            self.shifts[pl.ds(x0 + kx, step), 2 * p + ky].reshape(-1, self.shifts.shape[-1])
            for p in range(self.ny // 2)
        ]
        return jnp.concatenate(rows, 0)

    def patch(self, x0, step):
        return jnp.concatenate([self.window(x0, kx, ky, step) for kx in range(3) for ky in range(4)], 1)


STEP = 8


def fused_kernel(
    n, scale,
    acts, cot, weight, moment_in, second_in,
    output, igrad, wgrad, nweight, nmoment, nsecond,
    xb, xe, xf, xs, zb, ze, zf, zs, cotv, w, moment, second,
    wall, w2, wt, dzt, g, r1, s2, p2, s3, p3, total,
    ls, xhs, xhr, zhs, zhr,
    gzs, gzr, gxs, gxr, gys, gyr, gds, gdr, gcs, gcr,
    c1s, c1r, c2s, c2r, c3s, c3r, c4s, c4r,
):
    f32, bf16 = jnp.float32, jnp.bfloat16
    me, sample, core, x = peers(n)
    na = n // 2
    a, b = me // 2, lax.rem(me, 2)
    across, partner = (1 - x) * 2 + core, x * 2 + 1 - core
    beside = a * 2 + 1 - b
    groups = w.shape[0]
    q = wall.shape[1] // 4
    ch = w.shape[2]
    crops, nx, _, nz, _ = xb.shape
    ny = xb.shape[2] - 2

    load_x = pltpu.make_async_copy(acts, xb.at[:, :, pl.ds(1, ny)], ls.at[0])
    load_c = pltpu.make_async_copy(cot, cotv, ls.at[1])
    load_w = pltpu.make_async_copy(weight, w, ls.at[2])
    load_m = pltpu.make_async_copy(moment_in, moment, ls.at[3])
    load_s = pltpu.make_async_copy(second_in, second, ls.at[4])
    for load in (load_w, load_x, load_c, load_m, load_s):
        load.start()

    barrier = pltpu.get_barrier_semaphore()

    def greet_space(d, _):
        pl.semaphore_signal(barrier, 1, device_id={"space": lax.rem(me + d, n)}, device_id_type=MESH)
        return 0

    lax.fori_loop(1, n, greet_space, 0)
    for d in range(1, 4):
        pl.semaphore_signal(barrier, 1, device_id={"sample": lax.rem(sample + d, 4)}, device_id_type=MESH)
    pl.semaphore_signal(barrier, 1, device_id={"sample": across, "space": beside}, device_id_type=MESH)

    wall[me, pl.ds(groups, 4 * q - groups)] = jnp.zeros((4 * q - groups, TILE, ch), bf16)
    field = Field(xb, xe, xf, xs, xhs, xhr)
    dfield = Field(zb, ze, zf, zs, zhs, zhr)
    load_w.wait()
    wall[me, pl.ds(0, groups)] = w[...].astype(bf16)
    pl.semaphore_wait(barrier, n + 3)

    def piece(s, c, h):
        return wall.at[s, pl.ds((c * 2 + h) * q, q)]

    def column(d):
        return lax.rem(a + na - d, na) * 2 + b

    def other(d):
        return lax.rem(a + na - d, na) * 2 + 1 - b

    def z_copy(d):
        part = piece(me, core, x)
        return remote(part, part, gzs.at[d], gzr.at[d], space=lax.rem(a + d, na) * 2 + b)

    def z_wait(d):
        part = piece(column(d), core, x)
        return remote(part, part, gzs.at[d], gzr.at[d], space=beside)

    def x_copy(d):
        part = piece(column(d), core, x)
        return remote(part, part, gxs.at[d], gxr.at[d], sample=across)

    def x_wait(d):
        part = piece(column(d), core, 1 - x)
        return remote(part, part, gxs.at[d], gxr.at[d], sample=across)

    def y_copy(d):
        part = piece(column(d), core, x)
        return remote(part, part, gys.at[d], gyr.at[d], space=beside)

    def y_wait(d):
        part = piece(other(d), core, x)
        return remote(part, part, gys.at[d], gyr.at[d], space=beside)

    def d_copy(d):
        part = piece(column(d), core, x)
        return remote(part, part, gds.at[d], gdr.at[d], sample=across, space=beside)

    def d_wait(d):
        part = piece(other(d), core, 1 - x)
        return remote(part, part, gds.at[d], gdr.at[d], sample=across, space=beside)

    def half(s, c):
        return wall.at[s, pl.ds(c * 2 * q, 2 * q)]

    def c_copy(i, s):
        part = half(s, core)
        return remote(part, part, gcs.at[i], gcr.at[i], sample=partner)

    def c_wait(i, s):
        part = half(s, 1 - core)
        return remote(part, part, gcs.at[i], gcr.at[i], sample=partner)

    for d in range(1, na):
        z_copy(d).start()
    y_copy(0).start()
    d_copy(0).start()
    load_x.wait()
    field.extract()
    field.start(False)
    field.clear()
    dfield.clear()
    for kx in range(3):
        w2[pl.ds((kx * 4 + 3) * 24, 24), :, 0:ch] = jnp.zeros((24, TILE, ch), bf16)
        w2[pl.ds(kx * 96, 24), :, ch : 2 * ch] = jnp.zeros((24, TILE, ch), bf16)
        wt[pl.ds(kx * 12 + 9, 3), pl.ds(0, 8)] = jnp.zeros((3, 8, TILE, ch), bf16)
        wt[pl.ds(kx * 12, 3), pl.ds(8, 8)] = jnp.zeros((3, 8, TILE, ch), bf16)
    g[:, pl.ds(groups, 4 * q - groups)] = jnp.zeros((n, 4 * q - groups, TILE, ch), bf16)


    def place(s):
        for i in range(groups):
            r = s * groups + i
            at = r + (r // 72) * 24
            tile = wall[s, i]
            w2[at, :, 0:ch] = tile
            w2[at + 24, :, ch : 2 * ch] = tile

    low_end = 2 * a < na

    def rank(j):
        return jnp.where(low_end, j, na - 1 - j)

    def forward(j, _):
        d = lax.rem(a - rank(j) + na, na)

        @pl.when(d > 0)
        def _():
            z_wait(d).wait_recv()
            y_copy(d).start()
            d_copy(d).start()
            x_copy(d).start()

        return 0

    lax.fori_loop(0, 2, forward, 0)
    field.start(True)
    lax.fori_loop(2, na, forward, 0)

    def relay(j, _):
        d = lax.rem(a - rank(j) + na, na)
        y_wait(d).wait_recv()
        d_wait(d).wait_recv()
        c_copy(na + d, other(d)).start()

        @pl.when(d > 0)
        def _():
            x_wait(d).wait_recv()
            c_copy(d, column(d)).start()

        return 0

    def arrive(j, _):
        d = lax.rem(a - rank(j) + na, na)

        @pl.when(d > 0)
        def _():
            c_wait(d, column(d)).wait_recv()

        place(column(d))
        c_wait(na + d, other(d)).wait_recv()
        place(other(d))
        return 0

    lax.fori_loop(0, na, relay, 0)
    field.finish()
    field.build()
    lax.fori_loop(0, na, arrive, 0)
    load_c.wait()
    rows = w2.shape[0] * TILE
    m = STEP * TILE

    def chunk(i, _):
        x0 = i * STEP
        pre = jnp.dot(field.patch(x0, STEP), w2[...].reshape(rows, 2 * ch), preferred_element_type=f32)
        square = pre * pre
        tval = jnp.tanh(pre * (root_coef + root_coef * cubic_coef * square))
        gate = 0.5 * (1.0 + tval)
        value = (pre * gate).astype(bf16)
        slope = gate + (0.5 * pre) * (1.0 - tval * tval) * (root_coef + 3.0 * root_coef * cubic_coef * square)
        pieces = []
        for p in range(ny // 2):
            line = []
            for h in range(2):
                up = jnp.concatenate([cotv[c, pl.ds(x0, STEP), 2 * p + h].astype(f32) for c in range(crops)], 1)
                dz = up.reshape(m, ch) * slope[p * m : (p + 1) * m, h * ch : (h + 1) * ch]
                line.append(dz)
                out = value[p * m : (p + 1) * m, h * ch : (h + 1) * ch].reshape(STEP, TILE, ch)
                dzr = dz.astype(bf16).reshape(STEP, TILE, ch)
                for c in range(crops):
                    output[c, pl.ds(x0, STEP), 2 * p + h] = out[:, c * nz : (c + 1) * nz]
                    zb[c, pl.ds(x0, STEP), 2 * p + h + 1] = dzr[:, c * nz : (c + 1) * nz]
            pieces.append(jnp.concatenate(line, 1))
        dzm = jnp.concatenate(pieces, 0)
        cols = dzm.shape[0]
        dzt[:, pl.ds(i * cols, cols)] = dzm.T.astype(bf16)
        return 0

    for i in range(nx // STEP):
        chunk(i, 0)

    dfield.start(True)

    def one(o):
        return remote(g.at[o, pl.ds((1 - core) * 2 * q, 2 * q)], r1.at[o], c1s.at[o], c1r.at[o], sample=partner)

    def two(k, j):
        own = j * 2 + (b if k == 0 else 1 - b)
        side = x if k == 1 else 1 - x
        to = {"sample": across} if k == 0 else {"space": beside}
        if k == 2:
            to = {"sample": across, "space": beside}
        return remote(s2.at[own, pl.ds(side * q, q)], p2.at[k, j], c2s.at[k, j], c2r.at[k, j], **to)

    def three(d):
        j = lax.rem(a + d, na)
        return remote(s3.at[j], p3.at[d], c3s.at[d], c3r.at[d], space=j * 2 + b)

    def four(d):
        mine = total.at[core * 2 + x]
        return remote(mine, mine, c4s.at[d], c4r.at[d], sample=lax.rem(sample + 1 + d, 4))

    def send_one(o, _):
        one(o).start()
        return 0

    def send_two(o, _):
        one(o).wait_recv()
        s2[o] = (g[o, pl.ds(core * 2 * q, 2 * q)].astype(f32) + r1[o].astype(f32)).astype(bf16)
        j = o // 2

        @pl.when(lax.rem(o, 2) == b)
        def _():
            two(0, j).start()

        @pl.when(lax.rem(o, 2) != b)
        def _():
            two(2, j).start()
            two(1, j).start()

        return 0

    def done(kx):
        return (kx * 72) // groups

    def terms(kx):
        window = [
            jnp.concatenate([field.window(i * STEP, kx, ky, STEP) for ky in range(4)], 1)
            for i in range(nx // STEP)
        ]
        pair = jnp.dot(dzt[...], jnp.concatenate(window, 0), preferred_element_type=f32)
        for ky in range(3):
            k = 3 * ch
            both = pair[:ch, ky * k : (ky + 1) * k] + pair[ch:, (ky + 1) * k : (ky + 2) * k]
            for kz in range(3):
                tap = both[:, kz * ch : (kz + 1) * ch].T.astype(bf16).reshape(ch // TILE, TILE, ch)
                for t in range(ch // TILE):
                    r = kx * 72 + (ky * 3 + kz) * (ch // TILE) + t
                    g[r // groups, r % groups] = tap[t]
            k = kx * 3 + ky
            for o in range(k * 24 // groups, (k + 1) * 24 // groups):
                send_one(o, 0)

    terms(0)
    dfield.extract()
    dfield.start(False)
    lax.fori_loop(0, done(1), send_two, 0)
    terms(1)
    terms(2)
    lax.fori_loop(done(1), done(2), send_two, 0)

    def flip(t, _):
        kx = t // 9
        src = kx * 96 + (t - kx * 9) * 8
        tap = w2[pl.ds(src, 8), :, 0:ch]
        back_t = 26 - t
        col = back_t + (back_t // 9) * 3
        wt[col, pl.ds(0, 8)] = tap
        wt[col + 3, pl.ds(8, 8)] = tap
        return 0

    lax.fori_loop(0, 14, flip, 0)
    lax.fori_loop(done(2), n, send_two, 0)
    lax.fori_loop(14, 27, flip, 0)

    def sum_two(j, _):
        for k in range(3):
            two(k, j).wait_recv()
        own = s2[j * 2 + b, pl.ds(x * q, q)].astype(f32)
        s3[j] = (own + p2[0, j].astype(f32) + p2[1, j].astype(f32) + p2[2, j].astype(f32)).astype(bf16)

        @pl.when(j != a)
        def _():
            three(lax.rem(j - a + na, na)).start()

        return 0

    dfield.finish()
    dfield.build()

    def back(i, _):
        x0 = i * STEP
        taps = jnp.concatenate([wt[k].reshape(2 * ch, ch) for k in range(wt.shape[0])], 1)
        grad = lax.dot_general(
            dfield.patch(x0, STEP), taps, (((1,), (1,)), ((), ())), preferred_element_type=f32
        ).astype(bf16)
        for p in range(ny // 2):
            for h in range(2):
                out = grad[p * m : (p + 1) * m, h * ch : (h + 1) * ch].reshape(STEP, TILE, ch)
                for c in range(crops):
                    igrad[c, pl.ds(x0, STEP), 2 * p + h] = out[:, c * nz : (c + 1) * nz]

        @pl.when(i >= SUM_AT)
        def _():
            lax.fori_loop((i - SUM_AT) * 2, (i - SUM_AT) * 2 + 2, sum_two, 0)

        return 0

    lax.fori_loop(0, nx // STEP, back, 0)

    result = s3[a].astype(f32)
    for d in range(1, na):
        three(d).wait_recv()
        result = result + p3[d].astype(f32)
    total[core * 2 + x] = result.astype(bf16)
    for d in range(3):
        four(d).start()
    for d in range(3):
        four(d).wait()
    load_m.wait()
    load_s.wait()
    grad = total[...].reshape(4 * q, TILE, ch)[:groups].astype(f32) * scale
    mom = 0.9 * moment[...] + 0.1 * grad
    sec = 0.999 * second[...] + 0.001 * grad * grad
    first_fix = 1.0 - 0.9**10
    second_fix = 1.0 - 0.999**10
    wgrad[...] = grad
    nmoment[...] = mom
    nsecond[...] = sec
    nweight[...] = w[...] - 0.001 * (mom / first_fix) / (jnp.sqrt(sec / second_fix) + 1e-08)

    field.drain()
    dfield.drain()
    y_copy(0).wait_send()
    d_copy(0).wait_send()

    def drain_gather(d, _):
        z_copy(d).wait_send()
        y_copy(d).wait_send()
        d_copy(d).wait_send()
        x_copy(d).wait_send()
        c_copy(d, column(d)).wait_send()
        three(d).wait_send()
        return 0

    lax.fori_loop(1, na, drain_gather, 0)

    def drain_plane(d, _):
        c_copy(na + d, other(d)).wait_send()
        for k in range(3):
            two(k, d).wait_send()
        return 0

    lax.fori_loop(0, na, drain_plane, 0)

    def drain_one(o, _):
        one(o).wait_send()
        return 0

    lax.fori_loop(0, n, drain_one, 0)


SUM_AT = 0


def put_kernel(*refs):
    k = len(refs) // 2
    copies = [pltpu.make_async_copy(refs[i], refs[k + i], refs[-1].at[i]) for i in range(k)]
    for copy in copies:
        copy.start()
    for copy in copies:
        copy.wait()


def fused(acts, weight, moment, second, cotangent, scale):
    n = lax.axis_size("space")
    na = n // 2
    bf16, f32 = jnp.bfloat16, jnp.float32
    crops, nx, ny, nz, ch = acts.shape
    groups = weight.shape[0] // TILE
    q = -(-groups // 4)
    tiles = [v.reshape(groups, TILE, ch) for v in (weight, moment, second)]
    state = jax.ShapeDtypeStruct((groups, TILE, ch), f32)
    block = pltpu.VMEM((crops, nx, ny + 2, nz, ch), bf16)
    ends = pltpu.VMEM((2, ny + 2, crops, nx, ch), bf16)
    face = pltpu.VMEM((2, ny, crops, nx, ch), bf16)
    shifts = pltpu.VMEM((nx + 2, ny + 2, crops * nz, 3 * ch), bf16)
    wide = pltpu.VMEM((3 * 4 * 3 * ch // TILE, TILE, 2 * ch), bf16)
    HBM = pl.BlockSpec(memory_space=pltpu.HBM)

    def sem(*shape):
        return pltpu.SemaphoreType.DMA(shape)

    outs = pl.pallas_call(
        functools.partial(fused_kernel, n, scale),
        name="whole_step",
        out_shape=[jax.ShapeDtypeStruct(acts.shape, bf16), jax.ShapeDtypeStruct(acts.shape, bf16)] + [state] * 4,
        in_specs=[HBM] * 5,
        out_specs=[VM] * 6,
        scratch_shapes=[
            block, ends, face, shifts, block, ends, face, shifts,
            pltpu.VMEM((crops, nx, ny, nz, ch), bf16),
            pltpu.VMEM((groups, TILE, ch), f32), pltpu.VMEM((groups, TILE, ch), f32), pltpu.VMEM((groups, TILE, ch), f32),
            pltpu.VMEM((n, 4 * q, TILE, ch), bf16),
            wide, pltpu.VMEM((36, 2 * ch // TILE, TILE, ch), bf16),
            pltpu.VMEM((2 * ch, crops * nx * ny * nz // 2), bf16),
            pltpu.VMEM((n, 4 * q, TILE, ch), bf16),
            pltpu.VMEM((n, 2 * q, TILE, ch), bf16),
            pltpu.VMEM((n, 2 * q, TILE, ch), bf16),
            pltpu.VMEM((3, na, q, TILE, ch), bf16),
            pltpu.VMEM((na, q, TILE, ch), bf16),
            pltpu.VMEM((na, q, TILE, ch), bf16),
            pltpu.VMEM((4, q, TILE, ch), bf16),
            sem(5), sem(8), sem(8), sem(8), sem(8),
            sem(na), sem(na), sem(na), sem(na), sem(na), sem(na), sem(na), sem(na), sem(n), sem(n),
            sem(n), sem(n), sem(3, na), sem(3, na), sem(na), sem(na), sem(3), sem(3),
        ],
        compiler_params=pltpu.CompilerParams(
            collective_id=2, has_side_effects=True, vmem_limit_bytes=32 * 1024 * 1024
        ),
    )(*[pltpu.with_memory_space_constraint(v, pltpu.HBM) for v in (acts, cotangent, *tiles)])
    outs = pl.pallas_call(
        put_kernel,
        name="put",
        out_shape=like(outs),
        in_specs=[VM] * 6,
        out_specs=[HBM] * 6,
        scratch_shapes=[sem(6)],
        compiler_params=pltpu.CompilerParams(vmem_limit_bytes=2 * 1024 * 1024),
    )(*outs)
    return list(outs[:2]) + [v.reshape(weight.shape) for v in outs[2:]]


def local(acts, weight, moment, second, cotangent):
    n = lax.axis_size("space")
    crops, _, nx, ny, nz, channels = acts.shape
    total = crops * lax.axis_size("sample") * n * nx * ny * nz
    alone = n == GY * GZ and lax.axis_size("sample") == 4
    fits = crops * nz == TILE and nx == TILE and ny % 2 == 0 and channels == 128 and weight.shape[0] % TILE == 0
    if not (alone and fits):
        return plain(acts, weight, moment, second, cotangent)
    value, grad, *rest = fused(
        acts[:, 0], weight, moment, second, cotangent[:, 0], float(total) ** (-0.5)
    )
    return (value[:, None], grad[:, None], *rest)


def solution(mesh):
    in_specs = (
        P("sample", "space", None, None, None, None),
        P("space", None),
        P("space", None),
        P("space", None),
        P("sample", "space", None, None, None, None),
    )
    out_specs = (
        P("sample", "space", None, None, None, None),
        P("sample", "space", None, None, None, None),
        P("space", None),
        P("space", None),
        P("space", None),
        P("space", None),
    )
    return jax.shard_map(local, mesh=mesh, in_specs=in_specs, out_specs=out_specs, check_vma=False)
```

```python
import functools

import jax
import jax.numpy as jnp
from jax import lax
from jax.experimental import pallas as pl
from jax.experimental.pallas import tpu as pltpu
from jax.sharding import PartitionSpec as P

GY = 2
GZ = 4
MESH = pl.DeviceIdType.MESH
VM = pl.BlockSpec(memory_space=pltpu.VMEM)

root_coef = 0.7978845608
cubic_coef = 0.044715

SIDES = (1, -1)
DIRS = [(0, 1), (0, -1), (1, 0), (-1, 0)] + [(dy, dz) for dy in SIDES for dz in SIDES]


def shifted(value, axis, by):
    devices = lax.axis_size(axis)
    pairs = [(i, i + by) for i in range(devices) if 0 <= i + by < devices]
    return lax.ppermute(value, axis, pairs)


def convolve(field, kernel):
    return lax.conv_general_dilated(
        field,
        kernel,
        (1, 1, 1),
        "VALID",
        dimension_numbers=("NDHWC", "DHWIO", "NDHWC"),
        preferred_element_type=jnp.float32,
    )


def activate(pre):
    inner = root_coef * (pre + cubic_coef * pre * pre * pre)
    tval = jnp.tanh(inner)
    value = 0.5 * pre * (1.0 + tval)
    slope = 0.5 * (1.0 + tval) + 0.5 * pre * (1.0 - tval * tval) * root_coef * (
        1.0 + 3.0 * cubic_coef * pre * pre
    )
    return (value, slope)


def extend_x(field):
    groups = lax.axis_size("space") // (GY * GZ)
    if groups == 1:
        return jnp.pad(field, ((0, 0), (1, 1), (0, 0), (0, 0), (0, 0)))
    coord = lax.axis_index("space") // (GZ * GY)
    length = field.shape[1]
    below = shifted(field[:, length - 1 : length], "space", GY * GZ)
    above = shifted(field[:, :1], "space", -GY * GZ)
    below = jnp.where(coord > 0, below, jnp.zeros_like(below))
    above = jnp.where(coord < groups - 1, above, jnp.zeros_like(above))
    return jnp.concatenate([below, field, above], 1)


def faces(field):
    ends = {1: field.shape[2] - 1, -1: 0}
    endz = {1: field.shape[3] - 1, -1: 0}
    zf = jnp.stack([field[:, :, :, endz[d], :] for d in SIDES])
    yf = jnp.stack([field[:, :, ends[d], :, :] for d in SIDES])
    cf = jnp.stack([field[:, :, ends[dy], endz[dz], :] for dy in SIDES for dz in SIDES])
    return (zf, yf, cf)


def assemble(field, zf, yf, cf):
    mid = jnp.concatenate([zf[0][:, :, :, None], field, zf[1][:, :, :, None]], 3)
    rows = []
    for i in range(2):
        low, high = cf[2 * i][:, :, None, :], cf[2 * i + 1][:, :, None, :]
        rows.append(jnp.concatenate([low, yf[i], high], 2)[:, :, None])
    return jnp.concatenate([rows[0], mid, rows[1]], 2)


class Halo:
    def __init__(self, ins, outs, send, recv):
        me = lax.axis_index("space")
        self.me, self.send, self.recv = me, send, recv
        self.cz, self.cy = lax.rem(me, GZ), lax.rem(me // GZ, GY)
        self.src = [ins[k // 2].at[k % 2] if k < 4 else ins[2].at[k - 4] for k in range(8)]
        self.dst = [outs[k // 2].at[k % 2] if k < 4 else outs[2].at[k - 4] for k in range(8)]

    def has(self, dy, dz):
        y, z = self.cy + dy, self.cz + dz
        return (y >= 0) & (y < GY) & (z >= 0) & (z < GZ)

    def copy(self, k, to):
        return pltpu.make_async_remote_copy(
            src_ref=self.src[k],
            dst_ref=self.dst[k],
            send_sem=self.send.at[k],
            recv_sem=self.recv.at[k],
            device_id={"space": to},
            device_id_type=MESH,
        )

    def start(self):
        for k, (dy, dz) in enumerate(DIRS):

            @pl.when(self.has(dy, dz))
            def _():
                self.copy(k, self.me + dy * GZ + dz).start()

            @pl.when(jnp.logical_not(self.has(-dy, -dz)))
            def _():
                self.dst[k][...] = jnp.zeros(self.dst[k].shape, self.dst[k].dtype)

    def finish(self):
        for k, (dy, dz) in enumerate(DIRS):

            @pl.when(self.has(-dy, -dz))
            def _():
                self.copy(k, self.me).wait_recv()

            @pl.when(self.has(dy, dz))
            def _():
                self.copy(k, self.me).wait_send()


def greet(n, me, sample):
    barrier = pltpu.get_barrier_semaphore()

    def space_peer(d, _):
        pl.semaphore_signal(barrier, 1, device_id={"space": lax.rem(me + d, n)}, device_id_type=MESH)
        return 0

    lax.fori_loop(1, n, space_peer, 0)
    for d in range(1, 4):
        pl.semaphore_signal(barrier, 1, device_id={"sample": lax.rem(sample + d, 4)}, device_id_type=MESH)
    pl.semaphore_wait(barrier, n + 2)


def remote(src, dst, send, recv, **to):
    return pltpu.make_async_remote_copy(
        src_ref=src, dst_ref=dst, send_sem=send, recv_sem=recv, device_id=to, device_id_type=MESH
    )


LAG = 6


def gather_kernel(n, w, zi, yi, ci, out, zo, yo, co, hs, hr, as_, ar, bs, br, cs, cr):
    me, sample = lax.axis_index("space"), lax.axis_index("sample")
    core, x = lax.rem(sample, 2), sample // 2
    across, partner = (1 - x) * 2 + core, x * 2 + 1 - core
    greet(n, me, sample)
    halo = Halo((zi, yi, ci), (zo, yo, co), hs, hr)
    halo.start()

    def first(d, _):
        o = lax.rem(me + d, n)
        remote(w.at[core, x], out.at[me, core, x], as_.at[o], ar.at[me], space=o).start()
        return 0

    lax.fori_loop(1, n, first, 0)
    out[me] = w[...]

    def rest(t, _):
        @pl.when(t < n)
        def _():
            j = lax.rem(me - t + n, n)
            slot = out.at[j, core, x]
            remote(slot, slot, as_.at[j], ar.at[j], space=me).wait_recv()
            remote(slot, slot, bs.at[j], br.at[j], sample=across).start()

        @pl.when(t > LAG)
        def _():
            j = lax.rem(me - t + LAG + n, n)
            slot = out.at[j, core, 1 - x]
            remote(slot, slot, bs.at[j], br.at[j], sample=across).wait_recv()
            pair = out.at[j, core]
            remote(pair, pair, cs.at[j], cr.at[j], sample=partner).start()

        return 0

    lax.fori_loop(1, n + LAG, rest, 0)

    def last(d, _):
        o = lax.rem(me + d, n)
        pair = out.at[o, 1 - core]
        remote(pair, pair, cs.at[o], cr.at[o], sample=partner).wait_recv()
        remote(w.at[core, x], out.at[me, core, x], as_.at[o], ar.at[me], space=o).wait_send()
        slot = out.at[o, core, x]
        remote(slot, slot, bs.at[o], br.at[o], sample=across).wait_send()
        mine = out.at[o, core]
        remote(mine, mine, cs.at[o], cr.at[o], sample=partner).wait_send()
        return 0

    lax.fori_loop(1, n, last, 0)
    halo.finish()


def reduce_kernel(n, g, zi, yi, ci, out, zo, yo, co, r1, s2, r2, s3, r3, hs, hr, as_, ar, bs, br, cs, cr, ds, dr):
    me, sample = lax.axis_index("space"), lax.axis_index("sample")
    core, x = lax.rem(sample, 2), sample // 2
    across, partner = (1 - x) * 2 + core, x * 2 + 1 - core
    f32, bf16 = jnp.float32, jnp.bfloat16
    greet(n, me, sample)
    halo = Halo((zi, yi, ci), (zo, yo, co), hs, hr)
    halo.start()

    def owner(d):
        return lax.rem(me + 1 + d, n)

    def copy1(o):
        return remote(g.at[o, 1 - core], r1.at[o], as_.at[o], ar.at[o], sample=partner)

    def copy2(o):
        return remote(s2.at[o, 1 - x], r2.at[o], bs.at[o], br.at[o], sample=across)

    def copy3(o):
        return remote(s3.at[o], r3.at[me], cs.at[o], cr.at[me], space=o)

    def first(d, _):
        copy1(owner(d)).start()
        return 0

    lax.fori_loop(0, n, first, 0)

    def rest(t, _):
        @pl.when(t < n)
        def _():
            o = owner(t)
            copy1(o).wait_recv()
            s2[o] = (g[o, core].astype(f32) + r1[o].astype(f32)).astype(bf16)
            copy2(o).start()

        @pl.when(t >= LAG)
        def _():
            o = owner(t - LAG)
            copy2(o).wait_recv()
            s3[o] = (s2[o, x].astype(f32) + r2[o].astype(f32)).astype(bf16)

            @pl.when(t < n + LAG - 1)
            def _():
                copy3(o).start()

        return 0

    lax.fori_loop(0, n + LAG, rest, 0)

    def gather(d, total):
        j = lax.rem(me + n - d, n)
        remote(s3.at[j], r3.at[j], cs.at[j], cr.at[j], space=j).wait_recv()
        return total + r3[j].astype(f32)

    out[core, x] = lax.fori_loop(1, n, gather, s3[me].astype(f32))

    def copy4(d):
        mine = out.at[core, x]
        return remote(mine, mine, ds.at[d], dr.at[d], sample=lax.rem(sample + 1 + d, 4))

    for d in range(3):
        copy4(d).start()
    for d in range(3):
        copy4(d).wait()

    def drain(d, _):
        o = owner(d)
        copy1(o).wait_send()
        copy2(o).wait_send()

        @pl.when(d < n - 1)
        def _():
            copy3(o).wait_send()

        return 0

    lax.fori_loop(0, n, drain, 0)
    halo.finish()


def quarters(value, lead):
    rows = value.shape[-2]
    q = -(-rows // 4)
    if rows != 4 * q:
        value = jnp.pad(value, [(0, 0)] * (value.ndim - 2) + [(0, 4 * q - rows), (0, 0)])
    return value.reshape(*lead, 2, 2, q, value.shape[-1])


def whole_rows(value, rows):
    lead = value.shape[:-4]
    return value.reshape(*lead, -1, value.shape[-1])[..., :rows, :]


def like(arrays):
    return [jax.ShapeDtypeStruct(a.shape, a.dtype) for a in arrays]


def sems(*counts):
    return [pltpu.SemaphoreType.DMA((c,)) for c in counts]


def gather_weights(rows_bf, field):
    n = lax.axis_size("space")
    halo = faces(field)
    w = quarters(rows_bf, ())
    whole, zf, yf, cf = pl.pallas_call(
        functools.partial(gather_kernel, n),
        name="gather_and_halo",
        out_shape=[jax.ShapeDtypeStruct((n, *w.shape), w.dtype), *like(halo)],
        in_specs=[VM] * 4,
        out_specs=[VM] * 4,
        scratch_shapes=sems(8, 8, n, n, n, n, n, n),
        compiler_params=pltpu.CompilerParams(collective_id=0, has_side_effects=True),
    )(w, *halo)
    whole = whole_rows(whole, rows_bf.shape[0]).reshape(-1, rows_bf.shape[1])
    return whole, assemble(field, zf, yf, cf)


def reduce_grads(terms, rows, field):
    n = lax.axis_size("space")
    halo = faces(field)
    channels = terms.shape[-1]
    g = quarters(terms.reshape(n, rows, channels), (n,)).astype(jnp.bfloat16)
    q = g.shape[3]
    bf16 = jnp.bfloat16
    total, zf, yf, cf = pl.pallas_call(
        functools.partial(reduce_kernel, n),
        name="reduce_and_halo",
        out_shape=[jax.ShapeDtypeStruct((2, 2, q, channels), jnp.float32), *like(halo)],
        in_specs=[VM] * 4,
        out_specs=[VM] * 4,
        scratch_shapes=[
            pltpu.VMEM((n, 2, q, channels), bf16),
            pltpu.VMEM((n, 2, q, channels), bf16),
            pltpu.VMEM((n, q, channels), bf16),
            pltpu.VMEM((n, q, channels), bf16),
            pltpu.VMEM((n, q, channels), bf16),
            *sems(8, 8, n, n, n, n, n, n, 3, 3),
        ],
        compiler_params=pltpu.CompilerParams(collective_id=1, has_side_effects=True),
    )(g, *halo)
    return whole_rows(total, rows), assemble(field, zf, yf, cf)


def kernel_terms(padded, grad_pre):
    terms = lax.conv_general_dilated(
        padded,
        grad_pre,
        (1, 1, 1),
        "VALID",
        dimension_numbers=("CDHWN", "IDHWO", "DHWNC"),
        preferred_element_type=jnp.float32,
    )
    return terms.reshape(-1, terms.shape[-1])


def plain(acts, weight, moment, second, cotangent):
    field = acts[:, 0]
    grad_out = cotangent[:, 0]
    channels = weight.shape[1]
    rows_bf = weight.astype(jnp.bfloat16)
    whole, padded = gather_weights(rows_bf, extend_x(field))
    kernel = whole.reshape(3, 3, 3, channels, channels)
    pre = convolve(padded, kernel)
    value, slope = activate(pre)
    output = value.astype(jnp.bfloat16)
    grad_pre = (grad_out.astype(jnp.float32) * slope).astype(jnp.bfloat16)
    flipped = jnp.flip(kernel, (0, 1, 2)).transpose(0, 1, 2, 4, 3)
    total = (
        field.shape[0]
        * lax.axis_size("sample")
        * lax.axis_size("space")
        * field.shape[1]
        * field.shape[2]
        * field.shape[3]
    )
    local_terms = kernel_terms(padded, grad_pre)
    summed, grad_padded = reduce_grads(local_terms, weight.shape[0], extend_x(grad_pre))
    input_grad = convolve(grad_padded, flipped).astype(jnp.bfloat16)
    weight_grad = summed * float(total) ** (-0.5)
    new_moment = 0.9 * moment + 0.1 * weight_grad
    new_second = 0.999 * second + 0.001 * weight_grad * weight_grad
    first_fix = 1.0 - 0.9**10
    second_fix = 1.0 - 0.999**10
    new_weight = weight - 0.001 * (new_moment / first_fix) / (
        jnp.sqrt(new_second / second_fix) + 1e-08
    )
    return (output[:, None], input_grad[:, None], weight_grad, new_weight, new_moment, new_second)


TILE = 16


def peers(n):
    me, sample = lax.axis_index("space"), lax.axis_index("sample")
    core, x = lax.rem(sample, 2), sample // 2
    return me, sample, core, x


class Field:
    def __init__(self, block, ends, faces, shifts, send, recv):
        self.block, self.ends, self.faces, self.shifts = block, ends, faces, shifts
        self.send, self.recv = send, recv
        me = lax.axis_index("space")
        self.me, self.cz, self.cy = me, lax.rem(me, GZ), lax.rem(me // GZ, GY)
        self.ny = block.shape[2] - 2

    def has(self, dy, dz):
        y, z = self.cy + dy, self.cz + dz
        return (y >= 0) & (y < GY) & (z >= 0) & (z < GZ)

    def extract(self):
        crops, nx, _, nz, _ = self.block.shape
        row = lax.broadcasted_iota(jnp.int32, (2 * nx, nx * nz), 0)
        col = lax.broadcasted_iota(jnp.int32, (2 * nx, nx * nz), 1)
        want = jnp.where(row < nx, row * nz + nz - 1, (row - nx) * nz)
        pick = jnp.where(col == want, 1.0, 0.0).astype(jnp.bfloat16)

        for y in range(self.ny):
            for c in range(crops):
                rows = self.block[c, :, y + 1].reshape(nx * nz, -1)
                both = jnp.dot(pick, rows, preferred_element_type=jnp.float32).astype(jnp.bfloat16)
                self.faces[0, y, c] = both[:nx]
                self.faces[1, y, c] = both[nx:]

    def refs(self, dy, dz):
        last = self.ny - 1
        if dz == 0:
            src = self.block.at[:, :, last + 1 if dy > 0 else 1]
            dst = self.block.at[:, :, 0 if dy > 0 else last + 2]
            return src, dst
        side = 0 if dz > 0 else 1
        if dy == 0:
            return self.faces.at[side], self.ends.at[side, pl.ds(1, self.ny)]
        src = self.faces.at[side, last if dy > 0 else 0]
        return src, self.ends.at[side, 0 if dy > 0 else last + 2]

    def copy(self, k, to):
        src, dst = self.refs(*DIRS[k])
        return remote(src, dst, self.send.at[k], self.recv.at[k], space=to)

    def clear(self):
        for k, (dy, dz) in enumerate(DIRS):
            dst = self.refs(dy, dz)[1]

            @pl.when(jnp.logical_not(self.has(-dy, -dz)))
            def _():
                dst[...] = jnp.zeros(dst.shape, dst.dtype)

        nx = self.block.shape[1]
        for edge in (0, nx + 1):
            self.shifts[edge] = jnp.zeros(self.shifts.shape[1:], self.shifts.dtype)

    def start(self, faces_only):
        for k, (dy, dz) in enumerate(DIRS):
            if (dz == 0) == faces_only:

                @pl.when(self.has(dy, dz))
                def _():
                    self.copy(k, self.me + dy * GZ + dz).start()

    def finish(self):
        for k, (dy, dz) in enumerate(DIRS):

            @pl.when(self.has(-dy, -dz))
            def _():
                self.copy(k, self.me).wait_recv()

    def drain(self):
        for k, (dy, dz) in enumerate(DIRS):

            @pl.when(self.has(dy, dz))
            def _():
                self.copy(k, self.me).wait_send()

    def build(self):
        crops, nx, _, nz, ch = self.block.shape
        f32 = jnp.float32

        def step(y, _):
            out = ([], [], [])
            for c in range(crops):
                mid = self.block[c, :, y].astype(f32)
                low = self.ends[0, y, c].astype(f32)[:, None, :]
                high = self.ends[1, y, c].astype(f32)[:, None, :]
                z = lax.broadcasted_iota(jnp.int32, mid.shape, 1)
                out[0].append(jnp.where(z == 0, low, pltpu.roll(mid, 1, 1)))
                out[1].append(mid)
                out[2].append(jnp.where(z == nz - 1, high, pltpu.roll(mid, nz - 1, 1)))
            for kz in range(3):
                value = jnp.concatenate(out[kz], 1).astype(jnp.bfloat16)
                self.shifts[pl.ds(1, nx), y, :, kz * ch : (kz + 1) * ch] = value
            return 0

        lax.fori_loop(0, self.ny + 2, step, 0)

    def window(self, x0, kx, ky, step):
        rows = [
            self.shifts[pl.ds(x0 + kx, step), 2 * p + ky].reshape(-1, self.shifts.shape[-1])
            for p in range(self.ny // 2)
        ]
        return jnp.concatenate(rows, 0)

    def patch(self, x0, step):
        return jnp.concatenate([self.window(x0, kx, ky, step) for kx in range(3) for ky in range(4)], 1)


STEP = 8


def fused_kernel(
    n, scale,
    acts, cot, weight, moment_in, second_in,
    output, igrad, wgrad, nweight, nmoment, nsecond,
    xb, xe, xf, xs, zb, ze, zf, zs, cotv, w, moment, second,
    wall, w2, wt, dzt, g, r1, s2, p2, s3, p3, total,
    ls, xhs, xhr, zhs, zhr,
    gzs, gzr, gxs, gxr, gys, gyr, gds, gdr, gcs, gcr,
    c1s, c1r, c2s, c2r, c3s, c3r, c4s, c4r,
):
    f32, bf16 = jnp.float32, jnp.bfloat16
    me, sample, core, x = peers(n)
    na = n // 2
    a, b = me // 2, lax.rem(me, 2)
    across, partner = (1 - x) * 2 + core, x * 2 + 1 - core
    beside = a * 2 + 1 - b
    groups = w.shape[0]
    q = wall.shape[1] // 4
    ch = w.shape[2]
    crops, nx, _, nz, _ = xb.shape
    ny = xb.shape[2] - 2

    load_x = pltpu.make_async_copy(acts, xb.at[:, :, pl.ds(1, ny)], ls.at[0])
    load_c = pltpu.make_async_copy(cot, cotv, ls.at[1])
    load_w = pltpu.make_async_copy(weight, w, ls.at[2])
    load_m = pltpu.make_async_copy(moment_in, moment, ls.at[3])
    load_s = pltpu.make_async_copy(second_in, second, ls.at[4])
    for load in (load_w, load_x, load_c, load_m, load_s):
        load.start()

    barrier = pltpu.get_barrier_semaphore()

    def greet_space(d, _):
        pl.semaphore_signal(barrier, 1, device_id={"space": lax.rem(me + d, n)}, device_id_type=MESH)
        return 0

    lax.fori_loop(1, n, greet_space, 0)
    for d in range(1, 4):
        pl.semaphore_signal(barrier, 1, device_id={"sample": lax.rem(sample + d, 4)}, device_id_type=MESH)
    pl.semaphore_signal(barrier, 1, device_id={"sample": across, "space": beside}, device_id_type=MESH)

    wall[me, pl.ds(groups, 4 * q - groups)] = jnp.zeros((4 * q - groups, TILE, ch), bf16)
    field = Field(xb, xe, xf, xs, xhs, xhr)
    dfield = Field(zb, ze, zf, zs, zhs, zhr)
    load_w.wait()
    wall[me, pl.ds(0, groups)] = w[...].astype(bf16)
    pl.semaphore_wait(barrier, n + 3)

    def piece(s, c, h):
        return wall.at[s, pl.ds((c * 2 + h) * q, q)]

    def column(d):
        return lax.rem(a + na - d, na) * 2 + b

    def other(d):
        return lax.rem(a + na - d, na) * 2 + 1 - b

    def z_copy(d):
        part = piece(me, core, x)
        return remote(part, part, gzs.at[d], gzr.at[d], space=lax.rem(a + d, na) * 2 + b)

    def z_wait(d):
        part = piece(column(d), core, x)
        return remote(part, part, gzs.at[d], gzr.at[d], space=beside)

    def x_copy(d):
        part = piece(column(d), core, x)
        return remote(part, part, gxs.at[d], gxr.at[d], sample=across)

    def x_wait(d):
        part = piece(column(d), core, 1 - x)
        return remote(part, part, gxs.at[d], gxr.at[d], sample=across)

    def y_copy(d):
        part = piece(column(d), core, x)
        return remote(part, part, gys.at[d], gyr.at[d], space=beside)

    def y_wait(d):
        part = piece(other(d), core, x)
        return remote(part, part, gys.at[d], gyr.at[d], space=beside)

    def d_copy(d):
        part = piece(column(d), core, x)
        return remote(part, part, gds.at[d], gdr.at[d], sample=across, space=beside)

    def d_wait(d):
        part = piece(other(d), core, 1 - x)
        return remote(part, part, gds.at[d], gdr.at[d], sample=across, space=beside)

    def half(s, c):
        return wall.at[s, pl.ds(c * 2 * q, 2 * q)]

    def c_copy(i, s):
        part = half(s, core)
        return remote(part, part, gcs.at[i], gcr.at[i], sample=partner)

    def c_wait(i, s):
        part = half(s, 1 - core)
        return remote(part, part, gcs.at[i], gcr.at[i], sample=partner)

    for d in range(1, na):
        z_copy(d).start()
    y_copy(0).start()
    d_copy(0).start()
    load_x.wait()
    field.extract()
    field.start(False)
    field.clear()
    dfield.clear()
    for kx in range(3):
        w2[pl.ds((kx * 4 + 3) * 24, 24), :, 0:ch] = jnp.zeros((24, TILE, ch), bf16)
        w2[pl.ds(kx * 96, 24), :, ch : 2 * ch] = jnp.zeros((24, TILE, ch), bf16)
        wt[pl.ds(kx * 12 + 9, 3), pl.ds(0, 8)] = jnp.zeros((3, 8, TILE, ch), bf16)
        wt[pl.ds(kx * 12, 3), pl.ds(8, 8)] = jnp.zeros((3, 8, TILE, ch), bf16)
    g[:, pl.ds(groups, 4 * q - groups)] = jnp.zeros((n, 4 * q - groups, TILE, ch), bf16)


    def place(s):
        for i in range(groups):
            r = s * groups + i
            at = r + (r // 72) * 24
            tile = wall[s, i]
            w2[at, :, 0:ch] = tile
            w2[at + 24, :, ch : 2 * ch] = tile

    low_end = 2 * a < na

    def rank(j):
        return jnp.where(low_end, j, na - 1 - j)

    def forward(j, _):
        d = lax.rem(a - rank(j) + na, na)

        @pl.when(d > 0)
        def _():
            z_wait(d).wait_recv()
            y_copy(d).start()
            d_copy(d).start()
            x_copy(d).start()

        return 0

    lax.fori_loop(0, 2, forward, 0)
    field.start(True)
    lax.fori_loop(2, na, forward, 0)

    def relay(j, _):
        d = lax.rem(a - rank(j) + na, na)
        y_wait(d).wait_recv()
        d_wait(d).wait_recv()
        c_copy(na + d, other(d)).start()

        @pl.when(d > 0)
        def _():
            x_wait(d).wait_recv()
            c_copy(d, column(d)).start()

        return 0

    def arrive(j, _):
        d = lax.rem(a - rank(j) + na, na)

        @pl.when(d > 0)
        def _():
            c_wait(d, column(d)).wait_recv()

        place(column(d))
        c_wait(na + d, other(d)).wait_recv()
        place(other(d))
        return 0

    lax.fori_loop(0, na, relay, 0)
    field.finish()
    field.build()
    lax.fori_loop(0, na, arrive, 0)
    load_c.wait()
    rows = w2.shape[0] * TILE
    m = STEP * TILE

    def chunk(i, _):
        x0 = i * STEP
        pre = jnp.dot(field.patch(x0, STEP), w2[...].reshape(rows, 2 * ch), preferred_element_type=f32)
        square = pre * pre
        tval = jnp.tanh(pre * (root_coef + root_coef * cubic_coef * square))
        gate = 0.5 * (1.0 + tval)
        value = (pre * gate).astype(bf16)
        slope = gate + (0.5 * pre) * (1.0 - tval * tval) * (root_coef + 3.0 * root_coef * cubic_coef * square)
        pieces = []
        for p in range(ny // 2):
            line = []
            for h in range(2):
                up = jnp.concatenate([cotv[c, pl.ds(x0, STEP), 2 * p + h].astype(f32) for c in range(crops)], 1)
                dz = up.reshape(m, ch) * slope[p * m : (p + 1) * m, h * ch : (h + 1) * ch]
                line.append(dz)
                out = value[p * m : (p + 1) * m, h * ch : (h + 1) * ch].reshape(STEP, TILE, ch)
                dzr = dz.astype(bf16).reshape(STEP, TILE, ch)
                for c in range(crops):
                    output[c, pl.ds(x0, STEP), 2 * p + h] = out[:, c * nz : (c + 1) * nz]
                    zb[c, pl.ds(x0, STEP), 2 * p + h + 1] = dzr[:, c * nz : (c + 1) * nz]
            pieces.append(jnp.concatenate(line, 1))
        dzm = jnp.concatenate(pieces, 0)
        cols = dzm.shape[0]
        dzt[:, pl.ds(i * cols, cols)] = dzm.T.astype(bf16)
        return 0

    for i in range(nx // STEP):
        chunk(i, 0)

    dfield.start(True)

    def one(o):
        return remote(g.at[o, pl.ds((1 - core) * 2 * q, 2 * q)], r1.at[o], c1s.at[o], c1r.at[o], sample=partner)

    def two(k, j):
        own = j * 2 + (b if k == 0 else 1 - b)
        side = x if k == 1 else 1 - x
        to = {"sample": across} if k == 0 else {"space": beside}
        if k == 2:
            to = {"sample": across, "space": beside}
        return remote(s2.at[own, pl.ds(side * q, q)], p2.at[k, j], c2s.at[k, j], c2r.at[k, j], **to)

    def three(d):
        j = lax.rem(a + d, na)
        return remote(s3.at[j], p3.at[d], c3s.at[d], c3r.at[d], space=j * 2 + b)

    def four(d):
        mine = total.at[core * 2 + x]
        return remote(mine, mine, c4s.at[d], c4r.at[d], sample=lax.rem(sample + 1 + d, 4))

    def send_one(o, _):
        one(o).start()
        return 0

    def send_two(o, _):
        one(o).wait_recv()
        s2[o] = (g[o, pl.ds(core * 2 * q, 2 * q)].astype(f32) + r1[o].astype(f32)).astype(bf16)
        j = o // 2

        @pl.when(lax.rem(o, 2) == b)
        def _():
            two(0, j).start()

        @pl.when(lax.rem(o, 2) != b)
        def _():
            two(2, j).start()
            two(1, j).start()

        return 0

    def done(kx):
        return (kx * 72) // groups

    def terms(kx):
        window = [
            jnp.concatenate([field.window(i * STEP, kx, ky, STEP) for ky in range(4)], 1)
            for i in range(nx // STEP)
        ]
        pair = jnp.dot(dzt[...], jnp.concatenate(window, 0), preferred_element_type=f32)
        for ky in range(3):
            k = 3 * ch
            both = pair[:ch, ky * k : (ky + 1) * k] + pair[ch:, (ky + 1) * k : (ky + 2) * k]
            for kz in range(3):
                tap = both[:, kz * ch : (kz + 1) * ch].T.astype(bf16).reshape(ch // TILE, TILE, ch)
                for t in range(ch // TILE):
                    r = kx * 72 + (ky * 3 + kz) * (ch // TILE) + t
                    g[r // groups, r % groups] = tap[t]
            k = kx * 3 + ky
            for o in range(k * 24 // groups, (k + 1) * 24 // groups):
                send_one(o, 0)

    terms(0)
    dfield.extract()
    dfield.start(False)
    lax.fori_loop(0, done(1), send_two, 0)
    terms(1)
    terms(2)
    lax.fori_loop(done(1), done(2), send_two, 0)

    def flip(t, _):
        kx = t // 9
        src = kx * 96 + (t - kx * 9) * 8
        tap = w2[pl.ds(src, 8), :, 0:ch]
        back_t = 26 - t
        col = back_t + (back_t // 9) * 3
        wt[col, pl.ds(0, 8)] = tap
        wt[col + 3, pl.ds(8, 8)] = tap
        return 0

    lax.fori_loop(0, 14, flip, 0)
    lax.fori_loop(done(2), n, send_two, 0)
    lax.fori_loop(14, 27, flip, 0)

    def sum_two(j, _):
        for k in range(3):
            two(k, j).wait_recv()
        own = s2[j * 2 + b, pl.ds(x * q, q)].astype(f32)
        s3[j] = (own + p2[0, j].astype(f32) + p2[1, j].astype(f32) + p2[2, j].astype(f32)).astype(bf16)

        @pl.when(j != a)
        def _():
            three(lax.rem(j - a + na, na)).start()

        return 0

    dfield.finish()
    dfield.build()
    sum_two(0, 0)

    def back(i, _):
        x0 = i * STEP
        taps = jnp.concatenate([wt[k].reshape(2 * ch, ch) for k in range(wt.shape[0])], 1)
        grad = lax.dot_general(
            dfield.patch(x0, STEP), taps, (((1,), (1,)), ((), ())), preferred_element_type=f32
        ).astype(bf16)
        for p in range(ny // 2):
            for h in range(2):
                out = grad[p * m : (p + 1) * m, h * ch : (h + 1) * ch].reshape(STEP, TILE, ch)
                for c in range(crops):
                    igrad[c, pl.ds(x0, STEP), 2 * p + h] = out[:, c * nz : (c + 1) * nz]

        lax.fori_loop(i + 1, jnp.where(i == 0, 2, na), sum_two, 0)

        return 0

    lax.fori_loop(0, nx // STEP, back, 0)

    result = s3[a].astype(f32)
    for d in range(1, na):
        three(d).wait_recv()
        result = result + p3[d].astype(f32)
    total[core * 2 + x] = result.astype(bf16)
    for d in range(3):
        four(d).start()
    for d in range(3):
        four(d).wait()
    load_m.wait()
    load_s.wait()
    grad = total[...].reshape(4 * q, TILE, ch)[:groups].astype(f32) * scale
    mom = 0.9 * moment[...] + 0.1 * grad
    sec = 0.999 * second[...] + 0.001 * grad * grad
    first_fix = 1.0 - 0.9**10
    second_fix = 1.0 - 0.999**10
    wgrad[...] = grad
    nmoment[...] = mom
    nsecond[...] = sec
    nweight[...] = w[...] - 0.001 * (mom / first_fix) / (jnp.sqrt(sec / second_fix) + 1e-08)

    field.drain()
    dfield.drain()
    y_copy(0).wait_send()
    d_copy(0).wait_send()

    def drain_gather(d, _):
        z_copy(d).wait_send()
        y_copy(d).wait_send()
        d_copy(d).wait_send()
        x_copy(d).wait_send()
        c_copy(d, column(d)).wait_send()
        three(d).wait_send()
        return 0

    lax.fori_loop(1, na, drain_gather, 0)

    def drain_plane(d, _):
        c_copy(na + d, other(d)).wait_send()
        for k in range(3):
            two(k, d).wait_send()
        return 0

    lax.fori_loop(0, na, drain_plane, 0)

    def drain_one(o, _):
        one(o).wait_send()
        return 0

    lax.fori_loop(0, n, drain_one, 0)


def put_kernel(*refs):
    k = len(refs) // 2
    copies = [pltpu.make_async_copy(refs[i], refs[k + i], refs[-1].at[i]) for i in range(k)]
    for copy in copies:
        copy.start()
    for copy in copies:
        copy.wait()


def fused(acts, weight, moment, second, cotangent, scale):
    n = lax.axis_size("space")
    na = n // 2
    bf16, f32 = jnp.bfloat16, jnp.float32
    crops, nx, ny, nz, ch = acts.shape
    groups = weight.shape[0] // TILE
    q = -(-groups // 4)
    tiles = [v.reshape(groups, TILE, ch) for v in (weight, moment, second)]
    state = jax.ShapeDtypeStruct((groups, TILE, ch), f32)
    block = pltpu.VMEM((crops, nx, ny + 2, nz, ch), bf16)
    ends = pltpu.VMEM((2, ny + 2, crops, nx, ch), bf16)
    face = pltpu.VMEM((2, ny, crops, nx, ch), bf16)
    shifts = pltpu.VMEM((nx + 2, ny + 2, crops * nz, 3 * ch), bf16)
    wide = pltpu.VMEM((3 * 4 * 3 * ch // TILE, TILE, 2 * ch), bf16)
    HBM = pl.BlockSpec(memory_space=pltpu.HBM)

    def sem(*shape):
        return pltpu.SemaphoreType.DMA(shape)

    outs = pl.pallas_call(
        functools.partial(fused_kernel, n, scale),
        name="whole_step",
        out_shape=[jax.ShapeDtypeStruct(acts.shape, bf16), jax.ShapeDtypeStruct(acts.shape, bf16)] + [state] * 4,
        in_specs=[HBM] * 5,
        out_specs=[VM] * 6,
        scratch_shapes=[
            block, ends, face, shifts, block, ends, face, shifts,
            pltpu.VMEM((crops, nx, ny, nz, ch), bf16),
            pltpu.VMEM((groups, TILE, ch), f32), pltpu.VMEM((groups, TILE, ch), f32), pltpu.VMEM((groups, TILE, ch), f32),
            pltpu.VMEM((n, 4 * q, TILE, ch), bf16),
            wide, pltpu.VMEM((36, 2 * ch // TILE, TILE, ch), bf16),
            pltpu.VMEM((2 * ch, crops * nx * ny * nz // 2), bf16),
            pltpu.VMEM((n, 4 * q, TILE, ch), bf16),
            pltpu.VMEM((n, 2 * q, TILE, ch), bf16),
            pltpu.VMEM((n, 2 * q, TILE, ch), bf16),
            pltpu.VMEM((3, na, q, TILE, ch), bf16),
            pltpu.VMEM((na, q, TILE, ch), bf16),
            pltpu.VMEM((na, q, TILE, ch), bf16),
            pltpu.VMEM((4, q, TILE, ch), bf16),
            sem(5), sem(8), sem(8), sem(8), sem(8),
            sem(na), sem(na), sem(na), sem(na), sem(na), sem(na), sem(na), sem(na), sem(n), sem(n),
            sem(n), sem(n), sem(3, na), sem(3, na), sem(na), sem(na), sem(3), sem(3),
        ],
        compiler_params=pltpu.CompilerParams(
            collective_id=2, has_side_effects=True, vmem_limit_bytes=32 * 1024 * 1024
        ),
    )(*[pltpu.with_memory_space_constraint(v, pltpu.HBM) for v in (acts, cotangent, *tiles)])
    outs = pl.pallas_call(
        put_kernel,
        name="put",
        out_shape=like(outs),
        in_specs=[VM] * 6,
        out_specs=[HBM] * 6,
        scratch_shapes=[sem(6)],
        compiler_params=pltpu.CompilerParams(vmem_limit_bytes=2 * 1024 * 1024),
    )(*outs)
    return list(outs[:2]) + [v.reshape(weight.shape) for v in outs[2:]]


def local(acts, weight, moment, second, cotangent):
    n = lax.axis_size("space")
    crops, _, nx, ny, nz, channels = acts.shape
    total = crops * lax.axis_size("sample") * n * nx * ny * nz
    alone = n == GY * GZ and lax.axis_size("sample") == 4
    fits = crops * nz == TILE and nx == TILE and ny % 2 == 0 and channels == 128 and weight.shape[0] % TILE == 0
    if not (alone and fits):
        return plain(acts, weight, moment, second, cotangent)
    value, grad, *rest = fused(
        acts[:, 0], weight, moment, second, cotangent[:, 0], float(total) ** (-0.5)
    )
    return (value[:, None], grad[:, None], *rest)


def solution(mesh):
    in_specs = (
        P("sample", "space", None, None, None, None),
        P("space", None),
        P("space", None),
        P("space", None),
        P("sample", "space", None, None, None, None),
    )
    out_specs = (
        P("sample", "space", None, None, None, None),
        P("sample", "space", None, None, None, None),
        P("space", None),
        P("space", None),
        P("space", None),
        P("space", None),
    )
    return jax.shard_map(local, mesh=mesh, in_specs=in_specs, out_specs=out_specs, check_vma=False)
```

```python
import functools

import jax
import jax.numpy as jnp
from jax import lax
from jax.experimental import pallas as pl
from jax.experimental.pallas import tpu as pltpu
from jax.sharding import PartitionSpec as P

GY = 2
GZ = 4
MESH = pl.DeviceIdType.MESH
VM = pl.BlockSpec(memory_space=pltpu.VMEM)

root_coef = 0.7978845608
cubic_coef = 0.044715

SIDES = (1, -1)
DIRS = [(0, 1), (0, -1), (1, 0), (-1, 0)] + [(dy, dz) for dy in SIDES for dz in SIDES]


def shifted(value, axis, by):
    devices = lax.axis_size(axis)
    pairs = [(i, i + by) for i in range(devices) if 0 <= i + by < devices]
    return lax.ppermute(value, axis, pairs)


def convolve(field, kernel):
    return lax.conv_general_dilated(
        field,
        kernel,
        (1, 1, 1),
        "VALID",
        dimension_numbers=("NDHWC", "DHWIO", "NDHWC"),
        preferred_element_type=jnp.float32,
    )


def activate(pre):
    inner = root_coef * (pre + cubic_coef * pre * pre * pre)
    tval = jnp.tanh(inner)
    value = 0.5 * pre * (1.0 + tval)
    slope = 0.5 * (1.0 + tval) + 0.5 * pre * (1.0 - tval * tval) * root_coef * (
        1.0 + 3.0 * cubic_coef * pre * pre
    )
    return (value, slope)


def extend_x(field):
    groups = lax.axis_size("space") // (GY * GZ)
    if groups == 1:
        return jnp.pad(field, ((0, 0), (1, 1), (0, 0), (0, 0), (0, 0)))
    coord = lax.axis_index("space") // (GZ * GY)
    length = field.shape[1]
    below = shifted(field[:, length - 1 : length], "space", GY * GZ)
    above = shifted(field[:, :1], "space", -GY * GZ)
    below = jnp.where(coord > 0, below, jnp.zeros_like(below))
    above = jnp.where(coord < groups - 1, above, jnp.zeros_like(above))
    return jnp.concatenate([below, field, above], 1)


def faces(field):
    ends = {1: field.shape[2] - 1, -1: 0}
    endz = {1: field.shape[3] - 1, -1: 0}
    zf = jnp.stack([field[:, :, :, endz[d], :] for d in SIDES])
    yf = jnp.stack([field[:, :, ends[d], :, :] for d in SIDES])
    cf = jnp.stack([field[:, :, ends[dy], endz[dz], :] for dy in SIDES for dz in SIDES])
    return (zf, yf, cf)


def assemble(field, zf, yf, cf):
    mid = jnp.concatenate([zf[0][:, :, :, None], field, zf[1][:, :, :, None]], 3)
    rows = []
    for i in range(2):
        low, high = cf[2 * i][:, :, None, :], cf[2 * i + 1][:, :, None, :]
        rows.append(jnp.concatenate([low, yf[i], high], 2)[:, :, None])
    return jnp.concatenate([rows[0], mid, rows[1]], 2)


class Halo:
    def __init__(self, ins, outs, send, recv):
        me = lax.axis_index("space")
        self.me, self.send, self.recv = me, send, recv
        self.cz, self.cy = lax.rem(me, GZ), lax.rem(me // GZ, GY)
        self.src = [ins[k // 2].at[k % 2] if k < 4 else ins[2].at[k - 4] for k in range(8)]
        self.dst = [outs[k // 2].at[k % 2] if k < 4 else outs[2].at[k - 4] for k in range(8)]

    def has(self, dy, dz):
        y, z = self.cy + dy, self.cz + dz
        return (y >= 0) & (y < GY) & (z >= 0) & (z < GZ)

    def copy(self, k, to):
        return pltpu.make_async_remote_copy(
            src_ref=self.src[k],
            dst_ref=self.dst[k],
            send_sem=self.send.at[k],
            recv_sem=self.recv.at[k],
            device_id={"space": to},
            device_id_type=MESH,
        )

    def start(self):
        for k, (dy, dz) in enumerate(DIRS):

            @pl.when(self.has(dy, dz))
            def _():
                self.copy(k, self.me + dy * GZ + dz).start()

            @pl.when(jnp.logical_not(self.has(-dy, -dz)))
            def _():
                self.dst[k][...] = jnp.zeros(self.dst[k].shape, self.dst[k].dtype)

    def finish(self):
        for k, (dy, dz) in enumerate(DIRS):

            @pl.when(self.has(-dy, -dz))
            def _():
                self.copy(k, self.me).wait_recv()

            @pl.when(self.has(dy, dz))
            def _():
                self.copy(k, self.me).wait_send()


def greet(n, me, sample):
    barrier = pltpu.get_barrier_semaphore()

    def space_peer(d, _):
        pl.semaphore_signal(barrier, 1, device_id={"space": lax.rem(me + d, n)}, device_id_type=MESH)
        return 0

    lax.fori_loop(1, n, space_peer, 0)
    for d in range(1, 4):
        pl.semaphore_signal(barrier, 1, device_id={"sample": lax.rem(sample + d, 4)}, device_id_type=MESH)
    pl.semaphore_wait(barrier, n + 2)


def remote(src, dst, send, recv, **to):
    return pltpu.make_async_remote_copy(
        src_ref=src, dst_ref=dst, send_sem=send, recv_sem=recv, device_id=to, device_id_type=MESH
    )


LAG = 6


def gather_kernel(n, w, zi, yi, ci, out, zo, yo, co, hs, hr, as_, ar, bs, br, cs, cr):
    me, sample = lax.axis_index("space"), lax.axis_index("sample")
    core, x = lax.rem(sample, 2), sample // 2
    across, partner = (1 - x) * 2 + core, x * 2 + 1 - core
    greet(n, me, sample)
    halo = Halo((zi, yi, ci), (zo, yo, co), hs, hr)
    halo.start()

    def first(d, _):
        o = lax.rem(me + d, n)
        remote(w.at[core, x], out.at[me, core, x], as_.at[o], ar.at[me], space=o).start()
        return 0

    lax.fori_loop(1, n, first, 0)
    out[me] = w[...]

    def rest(t, _):
        @pl.when(t < n)
        def _():
            j = lax.rem(me - t + n, n)
            slot = out.at[j, core, x]
            remote(slot, slot, as_.at[j], ar.at[j], space=me).wait_recv()
            remote(slot, slot, bs.at[j], br.at[j], sample=across).start()

        @pl.when(t > LAG)
        def _():
            j = lax.rem(me - t + LAG + n, n)
            slot = out.at[j, core, 1 - x]
            remote(slot, slot, bs.at[j], br.at[j], sample=across).wait_recv()
            pair = out.at[j, core]
            remote(pair, pair, cs.at[j], cr.at[j], sample=partner).start()

        return 0

    lax.fori_loop(1, n + LAG, rest, 0)

    def last(d, _):
        o = lax.rem(me + d, n)
        pair = out.at[o, 1 - core]
        remote(pair, pair, cs.at[o], cr.at[o], sample=partner).wait_recv()
        remote(w.at[core, x], out.at[me, core, x], as_.at[o], ar.at[me], space=o).wait_send()
        slot = out.at[o, core, x]
        remote(slot, slot, bs.at[o], br.at[o], sample=across).wait_send()
        mine = out.at[o, core]
        remote(mine, mine, cs.at[o], cr.at[o], sample=partner).wait_send()
        return 0

    lax.fori_loop(1, n, last, 0)
    halo.finish()


def reduce_kernel(n, g, zi, yi, ci, out, zo, yo, co, r1, s2, r2, s3, r3, hs, hr, as_, ar, bs, br, cs, cr, ds, dr):
    me, sample = lax.axis_index("space"), lax.axis_index("sample")
    core, x = lax.rem(sample, 2), sample // 2
    across, partner = (1 - x) * 2 + core, x * 2 + 1 - core
    f32, bf16 = jnp.float32, jnp.bfloat16
    greet(n, me, sample)
    halo = Halo((zi, yi, ci), (zo, yo, co), hs, hr)
    halo.start()

    def owner(d):
        return lax.rem(me + 1 + d, n)

    def copy1(o):
        return remote(g.at[o, 1 - core], r1.at[o], as_.at[o], ar.at[o], sample=partner)

    def copy2(o):
        return remote(s2.at[o, 1 - x], r2.at[o], bs.at[o], br.at[o], sample=across)

    def copy3(o):
        return remote(s3.at[o], r3.at[me], cs.at[o], cr.at[me], space=o)

    def first(d, _):
        copy1(owner(d)).start()
        return 0

    lax.fori_loop(0, n, first, 0)

    def rest(t, _):
        @pl.when(t < n)
        def _():
            o = owner(t)
            copy1(o).wait_recv()
            s2[o] = (g[o, core].astype(f32) + r1[o].astype(f32)).astype(bf16)
            copy2(o).start()

        @pl.when(t >= LAG)
        def _():
            o = owner(t - LAG)
            copy2(o).wait_recv()
            s3[o] = (s2[o, x].astype(f32) + r2[o].astype(f32)).astype(bf16)

            @pl.when(t < n + LAG - 1)
            def _():
                copy3(o).start()

        return 0

    lax.fori_loop(0, n + LAG, rest, 0)

    def gather(d, total):
        j = lax.rem(me + n - d, n)
        remote(s3.at[j], r3.at[j], cs.at[j], cr.at[j], space=j).wait_recv()
        return total + r3[j].astype(f32)

    out[core, x] = lax.fori_loop(1, n, gather, s3[me].astype(f32))

    def copy4(d):
        mine = out.at[core, x]
        return remote(mine, mine, ds.at[d], dr.at[d], sample=lax.rem(sample + 1 + d, 4))

    for d in range(3):
        copy4(d).start()
    for d in range(3):
        copy4(d).wait()

    def drain(d, _):
        o = owner(d)
        copy1(o).wait_send()
        copy2(o).wait_send()

        @pl.when(d < n - 1)
        def _():
            copy3(o).wait_send()

        return 0

    lax.fori_loop(0, n, drain, 0)
    halo.finish()


def quarters(value, lead):
    rows = value.shape[-2]
    q = -(-rows // 4)
    if rows != 4 * q:
        value = jnp.pad(value, [(0, 0)] * (value.ndim - 2) + [(0, 4 * q - rows), (0, 0)])
    return value.reshape(*lead, 2, 2, q, value.shape[-1])


def whole_rows(value, rows):
    lead = value.shape[:-4]
    return value.reshape(*lead, -1, value.shape[-1])[..., :rows, :]


def like(arrays):
    return [jax.ShapeDtypeStruct(a.shape, a.dtype) for a in arrays]


def sems(*counts):
    return [pltpu.SemaphoreType.DMA((c,)) for c in counts]


def gather_weights(rows_bf, field):
    n = lax.axis_size("space")
    halo = faces(field)
    w = quarters(rows_bf, ())
    whole, zf, yf, cf = pl.pallas_call(
        functools.partial(gather_kernel, n),
        name="gather_and_halo",
        out_shape=[jax.ShapeDtypeStruct((n, *w.shape), w.dtype), *like(halo)],
        in_specs=[VM] * 4,
        out_specs=[VM] * 4,
        scratch_shapes=sems(8, 8, n, n, n, n, n, n),
        compiler_params=pltpu.CompilerParams(collective_id=0, has_side_effects=True),
    )(w, *halo)
    whole = whole_rows(whole, rows_bf.shape[0]).reshape(-1, rows_bf.shape[1])
    return whole, assemble(field, zf, yf, cf)


def reduce_grads(terms, rows, field):
    n = lax.axis_size("space")
    halo = faces(field)
    channels = terms.shape[-1]
    g = quarters(terms.reshape(n, rows, channels), (n,)).astype(jnp.bfloat16)
    q = g.shape[3]
    bf16 = jnp.bfloat16
    total, zf, yf, cf = pl.pallas_call(
        functools.partial(reduce_kernel, n),
        name="reduce_and_halo",
        out_shape=[jax.ShapeDtypeStruct((2, 2, q, channels), jnp.float32), *like(halo)],
        in_specs=[VM] * 4,
        out_specs=[VM] * 4,
        scratch_shapes=[
            pltpu.VMEM((n, 2, q, channels), bf16),
            pltpu.VMEM((n, 2, q, channels), bf16),
            pltpu.VMEM((n, q, channels), bf16),
            pltpu.VMEM((n, q, channels), bf16),
            pltpu.VMEM((n, q, channels), bf16),
            *sems(8, 8, n, n, n, n, n, n, 3, 3),
        ],
        compiler_params=pltpu.CompilerParams(collective_id=1, has_side_effects=True),
    )(g, *halo)
    return whole_rows(total, rows), assemble(field, zf, yf, cf)


def kernel_terms(padded, grad_pre):
    terms = lax.conv_general_dilated(
        padded,
        grad_pre,
        (1, 1, 1),
        "VALID",
        dimension_numbers=("CDHWN", "IDHWO", "DHWNC"),
        preferred_element_type=jnp.float32,
    )
    return terms.reshape(-1, terms.shape[-1])


def plain(acts, weight, moment, second, cotangent):
    field = acts[:, 0]
    grad_out = cotangent[:, 0]
    channels = weight.shape[1]
    rows_bf = weight.astype(jnp.bfloat16)
    whole, padded = gather_weights(rows_bf, extend_x(field))
    kernel = whole.reshape(3, 3, 3, channels, channels)
    pre = convolve(padded, kernel)
    value, slope = activate(pre)
    output = value.astype(jnp.bfloat16)
    grad_pre = (grad_out.astype(jnp.float32) * slope).astype(jnp.bfloat16)
    flipped = jnp.flip(kernel, (0, 1, 2)).transpose(0, 1, 2, 4, 3)
    total = (
        field.shape[0]
        * lax.axis_size("sample")
        * lax.axis_size("space")
        * field.shape[1]
        * field.shape[2]
        * field.shape[3]
    )
    local_terms = kernel_terms(padded, grad_pre)
    summed, grad_padded = reduce_grads(local_terms, weight.shape[0], extend_x(grad_pre))
    input_grad = convolve(grad_padded, flipped).astype(jnp.bfloat16)
    weight_grad = summed * float(total) ** (-0.5)
    new_moment = 0.9 * moment + 0.1 * weight_grad
    new_second = 0.999 * second + 0.001 * weight_grad * weight_grad
    first_fix = 1.0 - 0.9**10
    second_fix = 1.0 - 0.999**10
    new_weight = weight - 0.001 * (new_moment / first_fix) / (
        jnp.sqrt(new_second / second_fix) + 1e-08
    )
    return (output[:, None], input_grad[:, None], weight_grad, new_weight, new_moment, new_second)


TILE = 16


def peers(n):
    me, sample = lax.axis_index("space"), lax.axis_index("sample")
    core, x = lax.rem(sample, 2), sample // 2
    return me, sample, core, x


class Field:
    def __init__(self, block, ends, faces, shifts, send, recv):
        self.block, self.ends, self.faces, self.shifts = block, ends, faces, shifts
        self.send, self.recv = send, recv
        me = lax.axis_index("space")
        self.me, self.cz, self.cy = me, lax.rem(me, GZ), lax.rem(me // GZ, GY)
        self.ny = block.shape[2] - 2

    def has(self, dy, dz):
        y, z = self.cy + dy, self.cz + dz
        return (y >= 0) & (y < GY) & (z >= 0) & (z < GZ)

    def extract(self):
        crops, nx, _, nz, _ = self.block.shape
        row = lax.broadcasted_iota(jnp.int32, (2 * nx, nx * nz), 0)
        col = lax.broadcasted_iota(jnp.int32, (2 * nx, nx * nz), 1)
        want = jnp.where(row < nx, row * nz + nz - 1, (row - nx) * nz)
        pick = jnp.where(col == want, 1.0, 0.0).astype(jnp.bfloat16)

        for y in range(self.ny):
            for c in range(crops):
                rows = self.block[c, :, y + 1].reshape(nx * nz, -1)
                both = jnp.dot(pick, rows, preferred_element_type=jnp.float32).astype(jnp.bfloat16)
                self.faces[0, y, c] = both[:nx]
                self.faces[1, y, c] = both[nx:]

    def refs(self, dy, dz):
        last = self.ny - 1
        if dz == 0:
            src = self.block.at[:, :, last + 1 if dy > 0 else 1]
            dst = self.block.at[:, :, 0 if dy > 0 else last + 2]
            return src, dst
        side = 0 if dz > 0 else 1
        if dy == 0:
            return self.faces.at[side], self.ends.at[side, pl.ds(1, self.ny)]
        src = self.faces.at[side, last if dy > 0 else 0]
        return src, self.ends.at[side, 0 if dy > 0 else last + 2]

    def copy(self, k, to):
        src, dst = self.refs(*DIRS[k])
        return remote(src, dst, self.send.at[k], self.recv.at[k], space=to)

    def clear(self):
        for k, (dy, dz) in enumerate(DIRS):
            dst = self.refs(dy, dz)[1]

            @pl.when(jnp.logical_not(self.has(-dy, -dz)))
            def _():
                dst[...] = jnp.zeros(dst.shape, dst.dtype)

        nx = self.block.shape[1]
        for edge in (0, nx + 1):
            self.shifts[edge] = jnp.zeros(self.shifts.shape[1:], self.shifts.dtype)

    def start(self, faces_only):
        for k, (dy, dz) in enumerate(DIRS):
            if (dz == 0) == faces_only:

                @pl.when(self.has(dy, dz))
                def _():
                    self.copy(k, self.me + dy * GZ + dz).start()

    def finish(self):
        for k, (dy, dz) in enumerate(DIRS):

            @pl.when(self.has(-dy, -dz))
            def _():
                self.copy(k, self.me).wait_recv()

    def drain(self):
        for k, (dy, dz) in enumerate(DIRS):

            @pl.when(self.has(dy, dz))
            def _():
                self.copy(k, self.me).wait_send()

    def build(self):
        crops, nx, _, nz, ch = self.block.shape
        f32 = jnp.float32

        def step(y, _):
            out = ([], [], [])
            for c in range(crops):
                mid = self.block[c, :, y].astype(f32)
                low = self.ends[0, y, c].astype(f32)[:, None, :]
                high = self.ends[1, y, c].astype(f32)[:, None, :]
                z = lax.broadcasted_iota(jnp.int32, mid.shape, 1)
                out[0].append(jnp.where(z == 0, low, pltpu.roll(mid, 1, 1)))
                out[1].append(mid)
                out[2].append(jnp.where(z == nz - 1, high, pltpu.roll(mid, nz - 1, 1)))
            for kz in range(3):
                value = jnp.concatenate(out[kz], 1).astype(jnp.bfloat16)
                self.shifts[pl.ds(1, nx), y, :, kz * ch : (kz + 1) * ch] = value
            return 0

        lax.fori_loop(0, self.ny + 2, step, 0)

    def window(self, x0, kx, ky, step):
        rows = [
            self.shifts[pl.ds(x0 + kx, step), 2 * p + ky].reshape(-1, self.shifts.shape[-1])
            for p in range(self.ny // 2)
        ]
        return jnp.concatenate(rows, 0)

    def patch(self, x0, step):
        return jnp.concatenate([self.window(x0, kx, ky, step) for kx in range(3) for ky in range(4)], 1)


STEP = 8


def fused_kernel(
    n, scale,
    acts, cot, weight, moment_in, second_in,
    output, igrad, wgrad, nweight, nmoment, nsecond,
    xb, xe, xf, xs, zb, ze, zf, zs, cotv, w, moment, second,
    wall, w2, wt, dzt, g, r1, s2, p2, s3, p3, total,
    ls, xhs, xhr, zhs, zhr,
    gzs, gzr, gxs, gxr, gys, gyr, gds, gdr, gcs, gcr,
    c1s, c1r, c2s, c2r, c3s, c3r, c4s, c4r,
):
    f32, bf16 = jnp.float32, jnp.bfloat16
    me, sample, core, x = peers(n)
    na = n // 2
    a, b = me // 2, lax.rem(me, 2)
    across, partner = (1 - x) * 2 + core, x * 2 + 1 - core
    beside = a * 2 + 1 - b
    groups = w.shape[0]
    q = wall.shape[1] // 4
    ch = w.shape[2]
    crops, nx, _, nz, _ = xb.shape
    ny = xb.shape[2] - 2

    load_x = pltpu.make_async_copy(acts, xb.at[:, :, pl.ds(1, ny)], ls.at[0])
    load_c = pltpu.make_async_copy(cot, cotv, ls.at[1])
    load_w = pltpu.make_async_copy(weight, w, ls.at[2])
    load_m = pltpu.make_async_copy(moment_in, moment, ls.at[3])
    load_s = pltpu.make_async_copy(second_in, second, ls.at[4])
    for load in (load_w, load_x, load_c, load_m, load_s):
        load.start()

    barrier = pltpu.get_barrier_semaphore()

    def greet_space(d, _):
        pl.semaphore_signal(barrier, 1, device_id={"space": lax.rem(me + d, n)}, device_id_type=MESH)
        return 0

    lax.fori_loop(1, n, greet_space, 0)
    for d in range(1, 4):
        pl.semaphore_signal(barrier, 1, device_id={"sample": lax.rem(sample + d, 4)}, device_id_type=MESH)
    pl.semaphore_signal(barrier, 1, device_id={"sample": across, "space": beside}, device_id_type=MESH)

    wall[me, pl.ds(groups, 4 * q - groups)] = jnp.zeros((4 * q - groups, TILE, ch), bf16)
    field = Field(xb, xe, xf, xs, xhs, xhr)
    dfield = Field(zb, ze, zf, zs, zhs, zhr)
    load_w.wait()
    wall[me, pl.ds(0, groups)] = w[...].astype(bf16)
    pl.semaphore_wait(barrier, n + 3)

    def piece(s, c, h):
        return wall.at[s, pl.ds((c * 2 + h) * q, q)]

    def column(d):
        return lax.rem(a + na - d, na) * 2 + b

    def other(d):
        return lax.rem(a + na - d, na) * 2 + 1 - b

    def z_copy(d):
        part = piece(me, core, x)
        return remote(part, part, gzs.at[d], gzr.at[d], space=lax.rem(a + d, na) * 2 + b)

    def z_wait(d):
        part = piece(column(d), core, x)
        return remote(part, part, gzs.at[d], gzr.at[d], space=beside)

    def x_copy(d):
        part = piece(column(d), core, x)
        return remote(part, part, gxs.at[d], gxr.at[d], sample=across)

    def x_wait(d):
        part = piece(column(d), core, 1 - x)
        return remote(part, part, gxs.at[d], gxr.at[d], sample=across)

    def y_copy(d):
        part = piece(column(d), core, x)
        return remote(part, part, gys.at[d], gyr.at[d], space=beside)

    def y_wait(d):
        part = piece(other(d), core, x)
        return remote(part, part, gys.at[d], gyr.at[d], space=beside)

    def d_copy(d):
        part = piece(column(d), core, x)
        return remote(part, part, gds.at[d], gdr.at[d], sample=across, space=beside)

    def d_wait(d):
        part = piece(other(d), core, 1 - x)
        return remote(part, part, gds.at[d], gdr.at[d], sample=across, space=beside)

    def half(s, c):
        return wall.at[s, pl.ds(c * 2 * q, 2 * q)]

    def c_copy(i, s):
        part = half(s, core)
        return remote(part, part, gcs.at[i], gcr.at[i], sample=partner)

    def c_wait(i, s):
        part = half(s, 1 - core)
        return remote(part, part, gcs.at[i], gcr.at[i], sample=partner)

    for d in range(1, na):
        z_copy(d).start()
    y_copy(0).start()
    d_copy(0).start()
    load_x.wait()
    field.extract()
    field.start(False)
    field.clear()
    dfield.clear()
    for kx in range(3):
        w2[pl.ds((kx * 4 + 3) * 24, 24), :, 0:ch] = jnp.zeros((24, TILE, ch), bf16)
        w2[pl.ds(kx * 96, 24), :, ch : 2 * ch] = jnp.zeros((24, TILE, ch), bf16)
        wt[pl.ds(kx * 12 + 9, 3), pl.ds(0, 8)] = jnp.zeros((3, 8, TILE, ch), bf16)
        wt[pl.ds(kx * 12, 3), pl.ds(8, 8)] = jnp.zeros((3, 8, TILE, ch), bf16)
    g[:, pl.ds(groups, 4 * q - groups)] = jnp.zeros((n, 4 * q - groups, TILE, ch), bf16)


    def place(s):
        for i in range(groups):
            r = s * groups + i
            at = r + jnp.where(r >= 144, 48, jnp.where(r >= 72, 24, 0))
            tile = wall[s, i]
            w2[at, :, 0:ch] = tile
            w2[at + 24, :, ch : 2 * ch] = tile

    low_end = 2 * a < na

    def rank(j):
        return jnp.where(low_end, j, na - 1 - j)

    def forward(j, _):
        d = lax.rem(a - rank(j) + na, na)

        @pl.when(d > 0)
        def _():
            z_wait(d).wait_recv()
            y_copy(d).start()
            d_copy(d).start()
            x_copy(d).start()

        return 0

    lax.fori_loop(0, 2, forward, 0)
    field.start(True)
    lax.fori_loop(2, na, forward, 0)

    def relay(j, _):
        d = lax.rem(a - rank(j) + na, na)

        @pl.when(d > 0)
        def _():
            x_wait(d).wait_recv()
            c_copy(d, column(d)).start()

        y_wait(d).wait_recv()
        d_wait(d).wait_recv()
        c_copy(na + d, other(d)).start()
        return 0

    def arrive(j, _):
        d = lax.rem(a - rank(j) + na, na)

        @pl.when(d > 0)
        def _():
            c_wait(d, column(d)).wait_recv()

        place(column(d))
        c_wait(na + d, other(d)).wait_recv()
        place(other(d))
        return 0

    lax.fori_loop(0, na, relay, 0)
    field.finish()
    field.build()
    lax.fori_loop(0, na, arrive, 0)
    load_c.wait()
    rows = w2.shape[0] * TILE
    m = STEP * TILE

    def chunk(i, _):
        x0 = i * STEP
        pre = jnp.dot(field.patch(x0, STEP), w2[...].reshape(rows, 2 * ch), preferred_element_type=f32)
        square = pre * pre
        tval = jnp.tanh(pre * (root_coef + root_coef * cubic_coef * square))
        gate = 0.5 * (1.0 + tval)
        value = (pre * gate).astype(bf16)
        slope = gate + (0.5 * pre) * (1.0 - tval * tval) * (root_coef + 3.0 * root_coef * cubic_coef * square)
        pieces = []
        for p in range(ny // 2):
            line = []
            for h in range(2):
                up = jnp.concatenate([cotv[c, pl.ds(x0, STEP), 2 * p + h].astype(f32) for c in range(crops)], 1)
                dz = up.reshape(m, ch) * slope[p * m : (p + 1) * m, h * ch : (h + 1) * ch]
                line.append(dz)
                out = value[p * m : (p + 1) * m, h * ch : (h + 1) * ch].reshape(STEP, TILE, ch)
                dzr = dz.astype(bf16).reshape(STEP, TILE, ch)
                for c in range(crops):
                    output[c, pl.ds(x0, STEP), 2 * p + h] = out[:, c * nz : (c + 1) * nz]
                    zb[c, pl.ds(x0, STEP), 2 * p + h + 1] = dzr[:, c * nz : (c + 1) * nz]
            pieces.append(jnp.concatenate(line, 1))
        dzm = jnp.concatenate(pieces, 0)
        cols = dzm.shape[0]
        dzt[:, pl.ds(i * cols, cols)] = dzm.T.astype(bf16)
        return 0

    for i in range(nx // STEP):
        chunk(i, 0)

    dfield.start(True)

    def one(o):
        return remote(g.at[o, pl.ds((1 - core) * 2 * q, 2 * q)], r1.at[o], c1s.at[o], c1r.at[o], sample=partner)

    def two(k, j):
        own = j * 2 + (b if k == 0 else 1 - b)
        side = x if k == 1 else 1 - x
        to = {"sample": across} if k == 0 else {"space": beside}
        if k == 2:
            to = {"sample": across, "space": beside}
        return remote(s2.at[own, pl.ds(side * q, q)], p2.at[k, j], c2s.at[k, j], c2r.at[k, j], **to)

    def three(d):
        j = lax.rem(a + d, na)
        return remote(s3.at[j], p3.at[d], c3s.at[d], c3r.at[d], space=j * 2 + b)

    def four(d):
        mine = total.at[core * 2 + x]
        return remote(mine, mine, c4s.at[d], c4r.at[d], sample=lax.rem(sample + 1 + d, 4))

    def send_one(o, _):
        one(o).start()
        return 0

    def send_two(o, _):
        one(o).wait_recv()
        s2[o] = (g[o, pl.ds(core * 2 * q, 2 * q)].astype(f32) + r1[o].astype(f32)).astype(bf16)
        j = o // 2

        @pl.when(lax.rem(o, 2) == b)
        def _():
            two(0, j).start()

        @pl.when(lax.rem(o, 2) != b)
        def _():
            two(2, j).start()
            two(1, j).start()

        return 0

    def done(kx):
        return (kx * 72) // groups

    def terms(kx):
        window = [
            jnp.concatenate([field.window(i * STEP, kx, ky, STEP) for ky in range(4)], 1)
            for i in range(nx // STEP)
        ]
        pair = jnp.dot(dzt[...], jnp.concatenate(window, 0), preferred_element_type=f32)
        for ky in range(3):
            k = 3 * ch
            both = pair[:ch, ky * k : (ky + 1) * k] + pair[ch:, (ky + 1) * k : (ky + 2) * k]
            for kz in range(3):
                tap = both[:, kz * ch : (kz + 1) * ch].T.astype(bf16).reshape(ch // TILE, TILE, ch)
                for t in range(ch // TILE):
                    r = kx * 72 + (ky * 3 + kz) * (ch // TILE) + t
                    g[r // groups, r % groups] = tap[t]
            k = kx * 3 + ky
            for o in range(k * 24 // groups, (k + 1) * 24 // groups):
                send_one(o, 0)

    terms(0)
    dfield.extract()
    dfield.start(False)
    lax.fori_loop(0, done(1), send_two, 0)
    terms(1)
    terms(2)
    lax.fori_loop(done(1), done(2), send_two, 0)

    def flip(t, _):
        kx = t // 9
        src = kx * 96 + (t - kx * 9) * 8
        tap = w2[pl.ds(src, 8), :, 0:ch]
        back_t = 26 - t
        col = back_t + (back_t // 9) * 3
        wt[col, pl.ds(0, 8)] = tap
        wt[col + 3, pl.ds(8, 8)] = tap
        return 0

    lax.fori_loop(0, 14, flip, 0)
    lax.fori_loop(done(2), n, send_two, 0)
    lax.fori_loop(14, 27, flip, 0)

    def sum_two(j, _):
        for k in range(3):
            two(k, j).wait_recv()
        own = s2[j * 2 + b, pl.ds(x * q, q)].astype(f32)
        s3[j] = (own + p2[0, j].astype(f32) + p2[1, j].astype(f32) + p2[2, j].astype(f32)).astype(bf16)

        @pl.when(j != a)
        def _():
            three(lax.rem(j - a + na, na)).start()

        return 0

    dfield.finish()
    dfield.build()
    sum_two(0, 0)

    def back(i, _):
        x0 = i * STEP
        taps = jnp.concatenate([wt[k].reshape(2 * ch, ch) for k in range(wt.shape[0])], 1)
        grad = lax.dot_general(
            dfield.patch(x0, STEP), taps, (((1,), (1,)), ((), ())), preferred_element_type=f32
        ).astype(bf16)
        for p in range(ny // 2):
            for h in range(2):
                out = grad[p * m : (p + 1) * m, h * ch : (h + 1) * ch].reshape(STEP, TILE, ch)
                for c in range(crops):
                    igrad[c, pl.ds(x0, STEP), 2 * p + h] = out[:, c * nz : (c + 1) * nz]

        lax.fori_loop(i + 1, jnp.where(i == 0, 2, na), sum_two, 0)

        return 0

    lax.fori_loop(0, nx // STEP, back, 0)

    result = s3[a].astype(f32)
    for d in range(1, na):
        three(d).wait_recv()
        result = result + p3[d].astype(f32)
    total[core * 2 + x] = result.astype(bf16)
    for d in range(3):
        four(d).start()
    for d in range(3):
        four(d).wait()
    load_m.wait()
    load_s.wait()
    grad = total[...].reshape(4 * q, TILE, ch)[:groups].astype(f32) * scale
    mom = 0.9 * moment[...] + 0.1 * grad
    sec = 0.999 * second[...] + 0.001 * grad * grad
    first_fix = 1.0 - 0.9**10
    second_fix = 1.0 - 0.999**10
    wgrad[...] = grad
    nmoment[...] = mom
    nsecond[...] = sec
    nweight[...] = w[...] - 0.001 * (mom / first_fix) / (jnp.sqrt(sec / second_fix) + 1e-08)

    field.drain()
    dfield.drain()
    y_copy(0).wait_send()
    d_copy(0).wait_send()

    def drain_gather(d, _):
        z_copy(d).wait_send()
        y_copy(d).wait_send()
        d_copy(d).wait_send()
        x_copy(d).wait_send()
        c_copy(d, column(d)).wait_send()
        three(d).wait_send()
        return 0

    lax.fori_loop(1, na, drain_gather, 0)

    def drain_plane(d, _):
        c_copy(na + d, other(d)).wait_send()
        for k in range(3):
            two(k, d).wait_send()
        return 0

    lax.fori_loop(0, na, drain_plane, 0)

    def drain_one(o, _):
        one(o).wait_send()
        return 0

    lax.fori_loop(0, n, drain_one, 0)


def put_kernel(*refs):
    k = len(refs) // 2
    copies = [pltpu.make_async_copy(refs[i], refs[k + i], refs[-1].at[i]) for i in range(k)]
    for copy in copies:
        copy.start()
    for copy in copies:
        copy.wait()


def fused(acts, weight, moment, second, cotangent, scale):
    n = lax.axis_size("space")
    na = n // 2
    bf16, f32 = jnp.bfloat16, jnp.float32
    crops, nx, ny, nz, ch = acts.shape
    groups = weight.shape[0] // TILE
    q = -(-groups // 4)
    tiles = [v.reshape(groups, TILE, ch) for v in (weight, moment, second)]
    state = jax.ShapeDtypeStruct((groups, TILE, ch), f32)
    block = pltpu.VMEM((crops, nx, ny + 2, nz, ch), bf16)
    ends = pltpu.VMEM((2, ny + 2, crops, nx, ch), bf16)
    face = pltpu.VMEM((2, ny, crops, nx, ch), bf16)
    shifts = pltpu.VMEM((nx + 2, ny + 2, crops * nz, 3 * ch), bf16)
    wide = pltpu.VMEM((3 * 4 * 3 * ch // TILE, TILE, 2 * ch), bf16)
    HBM = pl.BlockSpec(memory_space=pltpu.HBM)

    def sem(*shape):
        return pltpu.SemaphoreType.DMA(shape)

    outs = pl.pallas_call(
        functools.partial(fused_kernel, n, scale),
        name="whole_step",
        out_shape=[jax.ShapeDtypeStruct(acts.shape, bf16), jax.ShapeDtypeStruct(acts.shape, bf16)] + [state] * 4,
        in_specs=[HBM] * 5,
        out_specs=[VM] * 6,
        scratch_shapes=[
            block, ends, face, shifts, block, ends, face, shifts,
            pltpu.VMEM((crops, nx, ny, nz, ch), bf16),
            pltpu.VMEM((groups, TILE, ch), f32), pltpu.VMEM((groups, TILE, ch), f32), pltpu.VMEM((groups, TILE, ch), f32),
            pltpu.VMEM((n, 4 * q, TILE, ch), bf16),
            wide, pltpu.VMEM((36, 2 * ch // TILE, TILE, ch), bf16),
            pltpu.VMEM((2 * ch, crops * nx * ny * nz // 2), bf16),
            pltpu.VMEM((n, 4 * q, TILE, ch), bf16),
            pltpu.VMEM((n, 2 * q, TILE, ch), bf16),
            pltpu.VMEM((n, 2 * q, TILE, ch), bf16),
            pltpu.VMEM((3, na, q, TILE, ch), bf16),
            pltpu.VMEM((na, q, TILE, ch), bf16),
            pltpu.VMEM((na, q, TILE, ch), bf16),
            pltpu.VMEM((4, q, TILE, ch), bf16),
            sem(5), sem(8), sem(8), sem(8), sem(8),
            sem(na), sem(na), sem(na), sem(na), sem(na), sem(na), sem(na), sem(na), sem(n), sem(n),
            sem(n), sem(n), sem(3, na), sem(3, na), sem(na), sem(na), sem(3), sem(3),
        ],
        compiler_params=pltpu.CompilerParams(
            collective_id=2, has_side_effects=True, vmem_limit_bytes=32 * 1024 * 1024
        ),
    )(*[pltpu.with_memory_space_constraint(v, pltpu.HBM) for v in (acts, cotangent, *tiles)])
    outs = pl.pallas_call(
        put_kernel,
        name="put",
        out_shape=like(outs),
        in_specs=[VM] * 6,
        out_specs=[HBM] * 6,
        scratch_shapes=[sem(6)],
        compiler_params=pltpu.CompilerParams(vmem_limit_bytes=2 * 1024 * 1024),
    )(*outs)
    return list(outs[:2]) + [v.reshape(weight.shape) for v in outs[2:]]


def local(acts, weight, moment, second, cotangent):
    n = lax.axis_size("space")
    crops, _, nx, ny, nz, channels = acts.shape
    total = crops * lax.axis_size("sample") * n * nx * ny * nz
    alone = n == GY * GZ and lax.axis_size("sample") == 4
    fits = crops * nz == TILE and nx == TILE and ny % 2 == 0 and channels == 128 and weight.shape[0] % TILE == 0
    if not (alone and fits):
        return plain(acts, weight, moment, second, cotangent)
    value, grad, *rest = fused(
        acts[:, 0], weight, moment, second, cotangent[:, 0], float(total) ** (-0.5)
    )
    return (value[:, None], grad[:, None], *rest)


def solution(mesh):
    in_specs = (
        P("sample", "space", None, None, None, None),
        P("space", None),
        P("space", None),
        P("space", None),
        P("sample", "space", None, None, None, None),
    )
    out_specs = (
        P("sample", "space", None, None, None, None),
        P("sample", "space", None, None, None, None),
        P("space", None),
        P("space", None),
        P("space", None),
        P("space", None),
    )
    return jax.shard_map(local, mesh=mesh, in_specs=in_specs, out_specs=out_specs, check_vma=False)
```

```python
import functools

import jax
import jax.numpy as jnp
from jax import lax
from jax.experimental import pallas as pl
from jax.experimental.pallas import tpu as pltpu
from jax.sharding import PartitionSpec as P

GY = 2
GZ = 4
MESH = pl.DeviceIdType.MESH
VM = pl.BlockSpec(memory_space=pltpu.VMEM)

root_coef = 0.7978845608
cubic_coef = 0.044715

SIDES = (1, -1)
DIRS = [(0, 1), (0, -1), (1, 0), (-1, 0)] + [(dy, dz) for dy in SIDES for dz in SIDES]


def shifted(value, axis, by):
    devices = lax.axis_size(axis)
    pairs = [(i, i + by) for i in range(devices) if 0 <= i + by < devices]
    return lax.ppermute(value, axis, pairs)


def convolve(field, kernel):
    return lax.conv_general_dilated(
        field,
        kernel,
        (1, 1, 1),
        "VALID",
        dimension_numbers=("NDHWC", "DHWIO", "NDHWC"),
        preferred_element_type=jnp.float32,
    )


def activate(pre):
    inner = root_coef * (pre + cubic_coef * pre * pre * pre)
    tval = jnp.tanh(inner)
    value = 0.5 * pre * (1.0 + tval)
    slope = 0.5 * (1.0 + tval) + 0.5 * pre * (1.0 - tval * tval) * root_coef * (
        1.0 + 3.0 * cubic_coef * pre * pre
    )
    return (value, slope)


def extend_x(field):
    groups = lax.axis_size("space") // (GY * GZ)
    if groups == 1:
        return jnp.pad(field, ((0, 0), (1, 1), (0, 0), (0, 0), (0, 0)))
    coord = lax.axis_index("space") // (GZ * GY)
    length = field.shape[1]
    below = shifted(field[:, length - 1 : length], "space", GY * GZ)
    above = shifted(field[:, :1], "space", -GY * GZ)
    below = jnp.where(coord > 0, below, jnp.zeros_like(below))
    above = jnp.where(coord < groups - 1, above, jnp.zeros_like(above))
    return jnp.concatenate([below, field, above], 1)


def faces(field):
    ends = {1: field.shape[2] - 1, -1: 0}
    endz = {1: field.shape[3] - 1, -1: 0}
    zf = jnp.stack([field[:, :, :, endz[d], :] for d in SIDES])
    yf = jnp.stack([field[:, :, ends[d], :, :] for d in SIDES])
    cf = jnp.stack([field[:, :, ends[dy], endz[dz], :] for dy in SIDES for dz in SIDES])
    return (zf, yf, cf)


def assemble(field, zf, yf, cf):
    mid = jnp.concatenate([zf[0][:, :, :, None], field, zf[1][:, :, :, None]], 3)
    rows = []
    for i in range(2):
        low, high = cf[2 * i][:, :, None, :], cf[2 * i + 1][:, :, None, :]
        rows.append(jnp.concatenate([low, yf[i], high], 2)[:, :, None])
    return jnp.concatenate([rows[0], mid, rows[1]], 2)


class Halo:
    def __init__(self, ins, outs, send, recv):
        me = lax.axis_index("space")
        self.me, self.send, self.recv = me, send, recv
        self.cz, self.cy = lax.rem(me, GZ), lax.rem(me // GZ, GY)
        self.src = [ins[k // 2].at[k % 2] if k < 4 else ins[2].at[k - 4] for k in range(8)]
        self.dst = [outs[k // 2].at[k % 2] if k < 4 else outs[2].at[k - 4] for k in range(8)]

    def has(self, dy, dz):
        y, z = self.cy + dy, self.cz + dz
        return (y >= 0) & (y < GY) & (z >= 0) & (z < GZ)

    def copy(self, k, to):
        return pltpu.make_async_remote_copy(
            src_ref=self.src[k],
            dst_ref=self.dst[k],
            send_sem=self.send.at[k],
            recv_sem=self.recv.at[k],
            device_id={"space": to},
            device_id_type=MESH,
        )

    def start(self):
        for k, (dy, dz) in enumerate(DIRS):

            @pl.when(self.has(dy, dz))
            def _():
                self.copy(k, self.me + dy * GZ + dz).start()

            @pl.when(jnp.logical_not(self.has(-dy, -dz)))
            def _():
                self.dst[k][...] = jnp.zeros(self.dst[k].shape, self.dst[k].dtype)

    def finish(self):
        for k, (dy, dz) in enumerate(DIRS):

            @pl.when(self.has(-dy, -dz))
            def _():
                self.copy(k, self.me).wait_recv()

            @pl.when(self.has(dy, dz))
            def _():
                self.copy(k, self.me).wait_send()


def greet(n, me, sample):
    barrier = pltpu.get_barrier_semaphore()

    def space_peer(d, _):
        pl.semaphore_signal(barrier, 1, device_id={"space": lax.rem(me + d, n)}, device_id_type=MESH)
        return 0

    lax.fori_loop(1, n, space_peer, 0)
    for d in range(1, 4):
        pl.semaphore_signal(barrier, 1, device_id={"sample": lax.rem(sample + d, 4)}, device_id_type=MESH)
    pl.semaphore_wait(barrier, n + 2)


def remote(src, dst, send, recv, **to):
    return pltpu.make_async_remote_copy(
        src_ref=src, dst_ref=dst, send_sem=send, recv_sem=recv, device_id=to, device_id_type=MESH
    )


LAG = 6


def gather_kernel(n, w, zi, yi, ci, out, zo, yo, co, hs, hr, as_, ar, bs, br, cs, cr):
    me, sample = lax.axis_index("space"), lax.axis_index("sample")
    core, x = lax.rem(sample, 2), sample // 2
    across, partner = (1 - x) * 2 + core, x * 2 + 1 - core
    greet(n, me, sample)
    halo = Halo((zi, yi, ci), (zo, yo, co), hs, hr)
    halo.start()

    def first(d, _):
        o = lax.rem(me + d, n)
        remote(w.at[core, x], out.at[me, core, x], as_.at[o], ar.at[me], space=o).start()
        return 0

    lax.fori_loop(1, n, first, 0)
    out[me] = w[...]

    def rest(t, _):
        @pl.when(t < n)
        def _():
            j = lax.rem(me - t + n, n)
            slot = out.at[j, core, x]
            remote(slot, slot, as_.at[j], ar.at[j], space=me).wait_recv()
            remote(slot, slot, bs.at[j], br.at[j], sample=across).start()

        @pl.when(t > LAG)
        def _():
            j = lax.rem(me - t + LAG + n, n)
            slot = out.at[j, core, 1 - x]
            remote(slot, slot, bs.at[j], br.at[j], sample=across).wait_recv()
            pair = out.at[j, core]
            remote(pair, pair, cs.at[j], cr.at[j], sample=partner).start()

        return 0

    lax.fori_loop(1, n + LAG, rest, 0)

    def last(d, _):
        o = lax.rem(me + d, n)
        pair = out.at[o, 1 - core]
        remote(pair, pair, cs.at[o], cr.at[o], sample=partner).wait_recv()
        remote(w.at[core, x], out.at[me, core, x], as_.at[o], ar.at[me], space=o).wait_send()
        slot = out.at[o, core, x]
        remote(slot, slot, bs.at[o], br.at[o], sample=across).wait_send()
        mine = out.at[o, core]
        remote(mine, mine, cs.at[o], cr.at[o], sample=partner).wait_send()
        return 0

    lax.fori_loop(1, n, last, 0)
    halo.finish()


def reduce_kernel(n, g, zi, yi, ci, out, zo, yo, co, r1, s2, r2, s3, r3, hs, hr, as_, ar, bs, br, cs, cr, ds, dr):
    me, sample = lax.axis_index("space"), lax.axis_index("sample")
    core, x = lax.rem(sample, 2), sample // 2
    across, partner = (1 - x) * 2 + core, x * 2 + 1 - core
    f32, bf16 = jnp.float32, jnp.bfloat16
    greet(n, me, sample)
    halo = Halo((zi, yi, ci), (zo, yo, co), hs, hr)
    halo.start()

    def owner(d):
        return lax.rem(me + 1 + d, n)

    def copy1(o):
        return remote(g.at[o, 1 - core], r1.at[o], as_.at[o], ar.at[o], sample=partner)

    def copy2(o):
        return remote(s2.at[o, 1 - x], r2.at[o], bs.at[o], br.at[o], sample=across)

    def copy3(o):
        return remote(s3.at[o], r3.at[me], cs.at[o], cr.at[me], space=o)

    def first(d, _):
        copy1(owner(d)).start()
        return 0

    lax.fori_loop(0, n, first, 0)

    def rest(t, _):
        @pl.when(t < n)
        def _():
            o = owner(t)
            copy1(o).wait_recv()
            s2[o] = (g[o, core].astype(f32) + r1[o].astype(f32)).astype(bf16)
            copy2(o).start()

        @pl.when(t >= LAG)
        def _():
            o = owner(t - LAG)
            copy2(o).wait_recv()
            s3[o] = (s2[o, x].astype(f32) + r2[o].astype(f32)).astype(bf16)

            @pl.when(t < n + LAG - 1)
            def _():
                copy3(o).start()

        return 0

    lax.fori_loop(0, n + LAG, rest, 0)

    def gather(d, total):
        j = lax.rem(me + n - d, n)
        remote(s3.at[j], r3.at[j], cs.at[j], cr.at[j], space=j).wait_recv()
        return total + r3[j].astype(f32)

    out[core, x] = lax.fori_loop(1, n, gather, s3[me].astype(f32))

    def copy4(d):
        mine = out.at[core, x]
        return remote(mine, mine, ds.at[d], dr.at[d], sample=lax.rem(sample + 1 + d, 4))

    for d in range(3):
        copy4(d).start()
    for d in range(3):
        copy4(d).wait()

    def drain(d, _):
        o = owner(d)
        copy1(o).wait_send()
        copy2(o).wait_send()

        @pl.when(d < n - 1)
        def _():
            copy3(o).wait_send()

        return 0

    lax.fori_loop(0, n, drain, 0)
    halo.finish()


def quarters(value, lead):
    rows = value.shape[-2]
    q = -(-rows // 4)
    if rows != 4 * q:
        value = jnp.pad(value, [(0, 0)] * (value.ndim - 2) + [(0, 4 * q - rows), (0, 0)])
    return value.reshape(*lead, 2, 2, q, value.shape[-1])


def whole_rows(value, rows):
    lead = value.shape[:-4]
    return value.reshape(*lead, -1, value.shape[-1])[..., :rows, :]


def like(arrays):
    return [jax.ShapeDtypeStruct(a.shape, a.dtype) for a in arrays]


def sems(*counts):
    return [pltpu.SemaphoreType.DMA((c,)) for c in counts]


def gather_weights(rows_bf, field):
    n = lax.axis_size("space")
    halo = faces(field)
    w = quarters(rows_bf, ())
    whole, zf, yf, cf = pl.pallas_call(
        functools.partial(gather_kernel, n),
        name="gather_and_halo",
        out_shape=[jax.ShapeDtypeStruct((n, *w.shape), w.dtype), *like(halo)],
        in_specs=[VM] * 4,
        out_specs=[VM] * 4,
        scratch_shapes=sems(8, 8, n, n, n, n, n, n),
        compiler_params=pltpu.CompilerParams(collective_id=0, has_side_effects=True),
    )(w, *halo)
    whole = whole_rows(whole, rows_bf.shape[0]).reshape(-1, rows_bf.shape[1])
    return whole, assemble(field, zf, yf, cf)


def reduce_grads(terms, rows, field):
    n = lax.axis_size("space")
    halo = faces(field)
    channels = terms.shape[-1]
    g = quarters(terms.reshape(n, rows, channels), (n,)).astype(jnp.bfloat16)
    q = g.shape[3]
    bf16 = jnp.bfloat16
    total, zf, yf, cf = pl.pallas_call(
        functools.partial(reduce_kernel, n),
        name="reduce_and_halo",
        out_shape=[jax.ShapeDtypeStruct((2, 2, q, channels), jnp.float32), *like(halo)],
        in_specs=[VM] * 4,
        out_specs=[VM] * 4,
        scratch_shapes=[
            pltpu.VMEM((n, 2, q, channels), bf16),
            pltpu.VMEM((n, 2, q, channels), bf16),
            pltpu.VMEM((n, q, channels), bf16),
            pltpu.VMEM((n, q, channels), bf16),
            pltpu.VMEM((n, q, channels), bf16),
            *sems(8, 8, n, n, n, n, n, n, 3, 3),
        ],
        compiler_params=pltpu.CompilerParams(collective_id=1, has_side_effects=True),
    )(g, *halo)
    return whole_rows(total, rows), assemble(field, zf, yf, cf)


def kernel_terms(padded, grad_pre):
    terms = lax.conv_general_dilated(
        padded,
        grad_pre,
        (1, 1, 1),
        "VALID",
        dimension_numbers=("CDHWN", "IDHWO", "DHWNC"),
        preferred_element_type=jnp.float32,
    )
    return terms.reshape(-1, terms.shape[-1])


def plain(acts, weight, moment, second, cotangent):
    field = acts[:, 0]
    grad_out = cotangent[:, 0]
    channels = weight.shape[1]
    rows_bf = weight.astype(jnp.bfloat16)
    whole, padded = gather_weights(rows_bf, extend_x(field))
    kernel = whole.reshape(3, 3, 3, channels, channels)
    pre = convolve(padded, kernel)
    value, slope = activate(pre)
    output = value.astype(jnp.bfloat16)
    grad_pre = (grad_out.astype(jnp.float32) * slope).astype(jnp.bfloat16)
    flipped = jnp.flip(kernel, (0, 1, 2)).transpose(0, 1, 2, 4, 3)
    total = (
        field.shape[0]
        * lax.axis_size("sample")
        * lax.axis_size("space")
        * field.shape[1]
        * field.shape[2]
        * field.shape[3]
    )
    local_terms = kernel_terms(padded, grad_pre)
    summed, grad_padded = reduce_grads(local_terms, weight.shape[0], extend_x(grad_pre))
    input_grad = convolve(grad_padded, flipped).astype(jnp.bfloat16)
    weight_grad = summed * float(total) ** (-0.5)
    new_moment = 0.9 * moment + 0.1 * weight_grad
    new_second = 0.999 * second + 0.001 * weight_grad * weight_grad
    first_fix = 1.0 - 0.9**10
    second_fix = 1.0 - 0.999**10
    new_weight = weight - 0.001 * (new_moment / first_fix) / (
        jnp.sqrt(new_second / second_fix) + 1e-08
    )
    return (output[:, None], input_grad[:, None], weight_grad, new_weight, new_moment, new_second)


TILE = 16


def peers(n):
    me, sample = lax.axis_index("space"), lax.axis_index("sample")
    core, x = lax.rem(sample, 2), sample // 2
    return me, sample, core, x


class Field:
    def __init__(self, block, ends, faces, shifts, send, recv):
        self.block, self.ends, self.faces, self.shifts = block, ends, faces, shifts
        self.send, self.recv = send, recv
        me = lax.axis_index("space")
        self.me, self.cz, self.cy = me, lax.rem(me, GZ), lax.rem(me // GZ, GY)
        self.ny = block.shape[2] - 2

    def has(self, dy, dz):
        y, z = self.cy + dy, self.cz + dz
        return (y >= 0) & (y < GY) & (z >= 0) & (z < GZ)

    def extract(self):
        crops, nx, _, nz, _ = self.block.shape
        row = lax.broadcasted_iota(jnp.int32, (2 * nx, nx * nz), 0)
        col = lax.broadcasted_iota(jnp.int32, (2 * nx, nx * nz), 1)
        want = jnp.where(row < nx, row * nz + nz - 1, (row - nx) * nz)
        pick = jnp.where(col == want, 1.0, 0.0).astype(jnp.bfloat16)

        for y in range(self.ny):
            for c in range(crops):
                rows = self.block[c, :, y + 1].reshape(nx * nz, -1)
                both = jnp.dot(pick, rows, preferred_element_type=jnp.float32).astype(jnp.bfloat16)
                self.faces[0, y, c] = both[:nx]
                self.faces[1, y, c] = both[nx:]

    def refs(self, dy, dz):
        last = self.ny - 1
        if dz == 0:
            src = self.block.at[:, :, last + 1 if dy > 0 else 1]
            dst = self.block.at[:, :, 0 if dy > 0 else last + 2]
            return src, dst
        side = 0 if dz > 0 else 1
        if dy == 0:
            return self.faces.at[side], self.ends.at[side, pl.ds(1, self.ny)]
        src = self.faces.at[side, last if dy > 0 else 0]
        return src, self.ends.at[side, 0 if dy > 0 else last + 2]

    def copy(self, k, to):
        src, dst = self.refs(*DIRS[k])
        return remote(src, dst, self.send.at[k], self.recv.at[k], space=to)

    def clear(self):
        for k, (dy, dz) in enumerate(DIRS):
            dst = self.refs(dy, dz)[1]

            @pl.when(jnp.logical_not(self.has(-dy, -dz)))
            def _():
                dst[...] = jnp.zeros(dst.shape, dst.dtype)

        nx = self.block.shape[1]
        for edge in (0, nx + 1):
            self.shifts[edge] = jnp.zeros(self.shifts.shape[1:], self.shifts.dtype)

    def start(self, faces_only):
        for k, (dy, dz) in enumerate(DIRS):
            if (dz == 0) == faces_only:

                @pl.when(self.has(dy, dz))
                def _():
                    self.copy(k, self.me + dy * GZ + dz).start()

    def finish(self):
        for k, (dy, dz) in enumerate(DIRS):

            @pl.when(self.has(-dy, -dz))
            def _():
                self.copy(k, self.me).wait_recv()

    def drain(self):
        for k, (dy, dz) in enumerate(DIRS):

            @pl.when(self.has(dy, dz))
            def _():
                self.copy(k, self.me).wait_send()

    def build(self):
        crops, nx, _, nz, ch = self.block.shape
        f32 = jnp.float32

        def step(y, _):
            out = ([], [], [])
            for c in range(crops):
                mid = self.block[c, :, y].astype(f32)
                low = self.ends[0, y, c].astype(f32)[:, None, :]
                high = self.ends[1, y, c].astype(f32)[:, None, :]
                z = lax.broadcasted_iota(jnp.int32, mid.shape, 1)
                out[0].append(jnp.where(z == 0, low, pltpu.roll(mid, 1, 1)))
                out[1].append(mid)
                out[2].append(jnp.where(z == nz - 1, high, pltpu.roll(mid, nz - 1, 1)))
            for kz in range(3):
                value = jnp.concatenate(out[kz], 1).astype(jnp.bfloat16)
                self.shifts[pl.ds(1, nx), y, :, kz * ch : (kz + 1) * ch] = value
            return 0

        lax.fori_loop(0, self.ny + 2, step, 0)

    def window(self, x0, kx, ky, step):
        rows = [
            self.shifts[pl.ds(x0 + kx, step), 2 * p + ky].reshape(-1, self.shifts.shape[-1])
            for p in range(self.ny // 2)
        ]
        return jnp.concatenate(rows, 0)

    def patch(self, x0, step):
        return jnp.concatenate([self.window(x0, kx, ky, step) for kx in range(3) for ky in range(4)], 1)


STEP = 8


def fused_kernel(
    n, scale,
    acts, cot, weight, moment_in, second_in,
    output, igrad, wgrad, nweight, nmoment, nsecond,
    xb, xe, xf, xs, zb, ze, zf, zs, cotv, w, moment, second,
    wall, w2, wt, dzt, g, r1, s2, p2, s3, p3, total,
    ls, xhs, xhr, zhs, zhr,
    gzs, gzr, gxs, gxr, gys, gyr, gds, gdr, gcs, gcr,
    c1s, c1r, c2s, c2r, c3s, c3r, c4s, c4r,
):
    f32, bf16 = jnp.float32, jnp.bfloat16
    me, sample, core, x = peers(n)
    na = n // 2
    a, b = me // 2, lax.rem(me, 2)
    across, partner = (1 - x) * 2 + core, x * 2 + 1 - core
    beside = a * 2 + 1 - b
    groups = w.shape[0]
    q = wall.shape[1] // 4
    ch = w.shape[2]
    crops, nx, _, nz, _ = xb.shape
    ny = xb.shape[2] - 2

    load_x = pltpu.make_async_copy(acts, xb.at[:, :, pl.ds(1, ny)], ls.at[0])
    load_c = pltpu.make_async_copy(cot, cotv, ls.at[1])
    load_w = pltpu.make_async_copy(weight, w, ls.at[2])
    load_m = pltpu.make_async_copy(moment_in, moment, ls.at[3])
    load_s = pltpu.make_async_copy(second_in, second, ls.at[4])
    for load in (load_w, load_x, load_c, load_m, load_s):
        load.start()

    barrier = pltpu.get_barrier_semaphore()

    def greet_space(d, _):
        pl.semaphore_signal(barrier, 1, device_id={"space": lax.rem(me + d, n)}, device_id_type=MESH)
        return 0

    lax.fori_loop(1, n, greet_space, 0)
    for d in range(1, 4):
        pl.semaphore_signal(barrier, 1, device_id={"sample": lax.rem(sample + d, 4)}, device_id_type=MESH)
    pl.semaphore_signal(barrier, 1, device_id={"sample": across, "space": beside}, device_id_type=MESH)

    wall[me, pl.ds(groups, 4 * q - groups)] = jnp.zeros((4 * q - groups, TILE, ch), bf16)
    field = Field(xb, xe, xf, xs, xhs, xhr)
    dfield = Field(zb, ze, zf, zs, zhs, zhr)
    load_w.wait()
    wall[me, pl.ds(0, groups)] = w[...].astype(bf16)
    pl.semaphore_wait(barrier, n + 3)

    def piece(s, c, h):
        return wall.at[s, pl.ds((c * 2 + h) * q, q)]

    def column(d):
        return lax.rem(a + na - d, na) * 2 + b

    def other(d):
        return lax.rem(a + na - d, na) * 2 + 1 - b

    def z_copy(d):
        part = piece(me, core, x)
        return remote(part, part, gzs.at[d], gzr.at[d], space=lax.rem(a + d, na) * 2 + b)

    def z_wait(d):
        part = piece(column(d), core, x)
        return remote(part, part, gzs.at[d], gzr.at[d], space=beside)

    def x_copy(d):
        part = piece(column(d), core, x)
        return remote(part, part, gxs.at[d], gxr.at[d], sample=across)

    def x_wait(d):
        part = piece(column(d), core, 1 - x)
        return remote(part, part, gxs.at[d], gxr.at[d], sample=across)

    def y_copy(d):
        part = piece(column(d), core, x)
        return remote(part, part, gys.at[d], gyr.at[d], space=beside)

    def y_wait(d):
        part = piece(other(d), core, x)
        return remote(part, part, gys.at[d], gyr.at[d], space=beside)

    def d_copy(d):
        part = piece(column(d), core, x)
        return remote(part, part, gds.at[d], gdr.at[d], sample=across, space=beside)

    def d_wait(d):
        part = piece(other(d), core, 1 - x)
        return remote(part, part, gds.at[d], gdr.at[d], sample=across, space=beside)

    def half(s, c):
        return wall.at[s, pl.ds(c * 2 * q, 2 * q)]

    def c_copy(i, s):
        part = half(s, core)
        return remote(part, part, gcs.at[i], gcr.at[i], sample=partner)

    def c_wait(i, s):
        part = half(s, 1 - core)
        return remote(part, part, gcs.at[i], gcr.at[i], sample=partner)

    for d in range(1, na):
        z_copy(d).start()
    y_copy(0).start()
    d_copy(0).start()
    load_x.wait()
    field.extract()
    field.start(False)
    field.clear()
    dfield.clear()
    for kx in range(3):
        w2[pl.ds((kx * 4 + 3) * 24, 24), :, 0:ch] = jnp.zeros((24, TILE, ch), bf16)
        w2[pl.ds(kx * 96, 24), :, ch : 2 * ch] = jnp.zeros((24, TILE, ch), bf16)
        wt[pl.ds(kx * 12 + 9, 3), pl.ds(0, 8)] = jnp.zeros((3, 8, TILE, ch), bf16)
        wt[pl.ds(kx * 12, 3), pl.ds(8, 8)] = jnp.zeros((3, 8, TILE, ch), bf16)
    g[:, pl.ds(groups, 4 * q - groups)] = jnp.zeros((n, 4 * q - groups, TILE, ch), bf16)


    def place(s):
        for i in range(groups):
            r = s * groups + i
            at = r + jnp.where(r >= 144, 48, jnp.where(r >= 72, 24, 0))
            tile = wall[s, i]
            w2[at, :, 0:ch] = tile
            w2[at + 24, :, ch : 2 * ch] = tile

    low_end = 2 * a < na

    def rank(j):
        return jnp.where(low_end, j, na - 1 - j)

    def forward(j, _):
        d = lax.rem(a - rank(j) + na, na)

        @pl.when(d > 0)
        def _():
            z_wait(d).wait_recv()
            y_copy(d).start()
            d_copy(d).start()
            x_copy(d).start()

        return 0

    place(me)
    lax.fori_loop(0, 3, forward, 0)
    field.start(True)
    lax.fori_loop(3, na, forward, 0)

    def relay(j, _):
        d = lax.rem(a - rank(j) + na, na)

        @pl.when(d > 0)
        def _():
            x_wait(d).wait_recv()
            c_copy(d, column(d)).start()

        y_wait(d).wait_recv()
        d_wait(d).wait_recv()
        c_copy(na + d, other(d)).start()
        return 0

    def arrive(j, _):
        d = lax.rem(a - rank(j) + na, na)

        @pl.when(d > 0)
        def _():
            c_wait(d, column(d)).wait_recv()

            place(column(d))

        c_wait(na + d, other(d)).wait_recv()
        place(other(d))
        return 0

    lax.fori_loop(0, na, relay, 0)
    field.finish()
    field.build()
    lax.fori_loop(0, na, arrive, 0)
    load_c.wait()
    rows = w2.shape[0] * TILE
    m = STEP * TILE

    def chunk(i, _):
        x0 = i * STEP
        pre = jnp.dot(field.patch(x0, STEP), w2[...].reshape(rows, 2 * ch), preferred_element_type=f32)
        square = pre * pre
        tval = jnp.tanh(pre * (root_coef + root_coef * cubic_coef * square))
        gate = 0.5 * (1.0 + tval)
        value = (pre * gate).astype(bf16)
        slope = gate + (0.5 * pre) * (1.0 - tval * tval) * (root_coef + 3.0 * root_coef * cubic_coef * square)
        pieces = []
        for p in range(ny // 2):
            line = []
            for h in range(2):
                up = jnp.concatenate([cotv[c, pl.ds(x0, STEP), 2 * p + h].astype(f32) for c in range(crops)], 1)
                dz = up.reshape(m, ch) * slope[p * m : (p + 1) * m, h * ch : (h + 1) * ch]
                line.append(dz)
                out = value[p * m : (p + 1) * m, h * ch : (h + 1) * ch].reshape(STEP, TILE, ch)
                dzr = dz.astype(bf16).reshape(STEP, TILE, ch)
                for c in range(crops):
                    output[c, pl.ds(x0, STEP), 2 * p + h] = out[:, c * nz : (c + 1) * nz]
                    zb[c, pl.ds(x0, STEP), 2 * p + h + 1] = dzr[:, c * nz : (c + 1) * nz]
            pieces.append(jnp.concatenate(line, 1))
        dzm = jnp.concatenate(pieces, 0)
        cols = dzm.shape[0]
        dzt[:, pl.ds(i * cols, cols)] = dzm.T.astype(bf16)
        return 0

    for i in range(nx // STEP):
        chunk(i, 0)

    dfield.start(True)

    def one(o):
        return remote(g.at[o, pl.ds((1 - core) * 2 * q, 2 * q)], r1.at[o], c1s.at[o], c1r.at[o], sample=partner)

    def two(k, j):
        own = j * 2 + (b if k == 0 else 1 - b)
        side = x if k == 1 else 1 - x
        to = {"sample": across} if k == 0 else {"space": beside}
        if k == 2:
            to = {"sample": across, "space": beside}
        return remote(s2.at[own, pl.ds(side * q, q)], p2.at[k, j], c2s.at[k, j], c2r.at[k, j], **to)

    def three(d):
        j = lax.rem(a + d, na)
        return remote(s3.at[j], p3.at[d], c3s.at[d], c3r.at[d], space=j * 2 + b)

    def four(d):
        mine = total.at[core * 2 + x]
        return remote(mine, mine, c4s.at[d], c4r.at[d], sample=lax.rem(sample + 1 + d, 4))

    def send_one(o, _):
        one(o).start()
        return 0

    def send_two(o, _):
        one(o).wait_recv()
        s2[o] = (g[o, pl.ds(core * 2 * q, 2 * q)].astype(f32) + r1[o].astype(f32)).astype(bf16)
        j = o // 2

        @pl.when(lax.rem(o, 2) == b)
        def _():
            two(0, j).start()

        @pl.when(lax.rem(o, 2) != b)
        def _():
            two(2, j).start()
            two(1, j).start()

        return 0

    def done(kx):
        return (kx * 72) // groups

    def terms(kx):
        window = [
            jnp.concatenate([field.window(i * STEP, kx, ky, STEP) for ky in range(4)], 1)
            for i in range(nx // STEP)
        ]
        pair = jnp.dot(dzt[...], jnp.concatenate(window, 0), preferred_element_type=f32)
        for ky in range(3):
            k = 3 * ch
            both = pair[:ch, ky * k : (ky + 1) * k] + pair[ch:, (ky + 1) * k : (ky + 2) * k]
            for kz in range(3):
                tap = both[:, kz * ch : (kz + 1) * ch].T.astype(bf16).reshape(ch // TILE, TILE, ch)
                for t in range(ch // TILE):
                    r = kx * 72 + (ky * 3 + kz) * (ch // TILE) + t
                    g[r // groups, r % groups] = tap[t]
            k = kx * 3 + ky
            for o in range(k * 24 // groups, (k + 1) * 24 // groups):
                send_one(o, 0)

    terms(0)
    dfield.extract()
    dfield.start(False)
    lax.fori_loop(0, done(1), send_two, 0)
    terms(1)
    terms(2)
    lax.fori_loop(done(1), done(2), send_two, 0)

    def flip(t, _):
        kx = t // 9
        src = kx * 96 + (t - kx * 9) * 8
        tap = w2[pl.ds(src, 8), :, 0:ch]
        back_t = 26 - t
        col = back_t + (back_t // 9) * 3
        wt[col, pl.ds(0, 8)] = tap
        wt[col + 3, pl.ds(8, 8)] = tap
        return 0

    lax.fori_loop(0, 14, flip, 0)
    lax.fori_loop(done(2), n, send_two, 0)
    lax.fori_loop(14, 27, flip, 0)

    def sum_two(j, _):
        for k in range(3):
            two(k, j).wait_recv()
        own = s2[j * 2 + b, pl.ds(x * q, q)].astype(f32)
        s3[j] = (own + p2[0, j].astype(f32) + p2[1, j].astype(f32) + p2[2, j].astype(f32)).astype(bf16)

        @pl.when(j != a)
        def _():
            three(lax.rem(j - a + na, na)).start()

        return 0

    dfield.finish()
    dfield.build()
    sum_two(0, 0)

    def back(i, _):
        x0 = i * STEP
        taps = jnp.concatenate([wt[k].reshape(2 * ch, ch) for k in range(wt.shape[0])], 1)
        grad = lax.dot_general(
            dfield.patch(x0, STEP), taps, (((1,), (1,)), ((), ())), preferred_element_type=f32
        ).astype(bf16)
        for p in range(ny // 2):
            for h in range(2):
                out = grad[p * m : (p + 1) * m, h * ch : (h + 1) * ch].reshape(STEP, TILE, ch)
                for c in range(crops):
                    igrad[c, pl.ds(x0, STEP), 2 * p + h] = out[:, c * nz : (c + 1) * nz]

        lax.fori_loop(jnp.where(i == 0, 1, 3), jnp.where(i == 0, 3, na), sum_two, 0)

        return 0

    lax.fori_loop(0, nx // STEP, back, 0)

    load_m.wait()
    load_s.wait()
    moment[...] = 0.9 * moment[...]
    second[...] = 0.999 * second[...]
    result = s3[a].astype(f32)
    for d in range(1, na):
        three(d).wait_recv()
        result = result + p3[d].astype(f32)
    total[core * 2 + x] = result.astype(bf16)
    for d in range(3):
        four(d).start()
    for d in range(3):
        four(d).wait()
    grad = total[...].reshape(4 * q, TILE, ch)[:groups].astype(f32) * scale
    mom = moment[...] + 0.1 * grad
    sec = second[...] + 0.001 * grad * grad
    first_fix = 1.0 - 0.9**10
    second_fix = 1.0 - 0.999**10
    wgrad[...] = grad
    nmoment[...] = mom
    nsecond[...] = sec
    nweight[...] = w[...] - 0.001 * (mom / first_fix) / (jnp.sqrt(sec / second_fix) + 1e-08)

    field.drain()
    dfield.drain()
    y_copy(0).wait_send()
    d_copy(0).wait_send()

    def drain_gather(d, _):
        z_copy(d).wait_send()
        y_copy(d).wait_send()
        d_copy(d).wait_send()
        x_copy(d).wait_send()
        c_copy(d, column(d)).wait_send()
        three(d).wait_send()
        return 0

    lax.fori_loop(1, na, drain_gather, 0)

    def drain_plane(d, _):
        c_copy(na + d, other(d)).wait_send()
        for k in range(3):
            two(k, d).wait_send()
        return 0

    lax.fori_loop(0, na, drain_plane, 0)

    def drain_one(o, _):
        one(o).wait_send()
        return 0

    lax.fori_loop(0, n, drain_one, 0)


def put_kernel(*refs):
    k = len(refs) // 2
    copies = [pltpu.make_async_copy(refs[i], refs[k + i], refs[-1].at[i]) for i in range(k)]
    for copy in copies:
        copy.start()
    for copy in copies:
        copy.wait()


def fused(acts, weight, moment, second, cotangent, scale):
    n = lax.axis_size("space")
    na = n // 2
    bf16, f32 = jnp.bfloat16, jnp.float32
    crops, nx, ny, nz, ch = acts.shape
    groups = weight.shape[0] // TILE
    q = -(-groups // 4)
    tiles = [v.reshape(groups, TILE, ch) for v in (weight, moment, second)]
    state = jax.ShapeDtypeStruct((groups, TILE, ch), f32)
    block = pltpu.VMEM((crops, nx, ny + 2, nz, ch), bf16)
    ends = pltpu.VMEM((2, ny + 2, crops, nx, ch), bf16)
    face = pltpu.VMEM((2, ny, crops, nx, ch), bf16)
    shifts = pltpu.VMEM((nx + 2, ny + 2, crops * nz, 3 * ch), bf16)
    wide = pltpu.VMEM((3 * 4 * 3 * ch // TILE, TILE, 2 * ch), bf16)
    HBM = pl.BlockSpec(memory_space=pltpu.HBM)

    def sem(*shape):
        return pltpu.SemaphoreType.DMA(shape)

    outs = pl.pallas_call(
        functools.partial(fused_kernel, n, scale),
        name="whole_step",
        out_shape=[jax.ShapeDtypeStruct(acts.shape, bf16), jax.ShapeDtypeStruct(acts.shape, bf16)] + [state] * 4,
        in_specs=[HBM] * 5,
        out_specs=[VM] * 6,
        scratch_shapes=[
            block, ends, face, shifts, block, ends, face, shifts,
            pltpu.VMEM((crops, nx, ny, nz, ch), bf16),
            pltpu.VMEM((groups, TILE, ch), f32), pltpu.VMEM((groups, TILE, ch), f32), pltpu.VMEM((groups, TILE, ch), f32),
            pltpu.VMEM((n, 4 * q, TILE, ch), bf16),
            wide, pltpu.VMEM((36, 2 * ch // TILE, TILE, ch), bf16),
            pltpu.VMEM((2 * ch, crops * nx * ny * nz // 2), bf16),
            pltpu.VMEM((n, 4 * q, TILE, ch), bf16),
            pltpu.VMEM((n, 2 * q, TILE, ch), bf16),
            pltpu.VMEM((n, 2 * q, TILE, ch), bf16),
            pltpu.VMEM((3, na, q, TILE, ch), bf16),
            pltpu.VMEM((na, q, TILE, ch), bf16),
            pltpu.VMEM((na, q, TILE, ch), bf16),
            pltpu.VMEM((4, q, TILE, ch), bf16),
            sem(5), sem(8), sem(8), sem(8), sem(8),
            sem(na), sem(na), sem(na), sem(na), sem(na), sem(na), sem(na), sem(na), sem(n), sem(n),
            sem(n), sem(n), sem(3, na), sem(3, na), sem(na), sem(na), sem(3), sem(3),
        ],
        compiler_params=pltpu.CompilerParams(
            collective_id=2, has_side_effects=True, vmem_limit_bytes=32 * 1024 * 1024
        ),
    )(*[pltpu.with_memory_space_constraint(v, pltpu.HBM) for v in (acts, cotangent, *tiles)])
    outs = pl.pallas_call(
        put_kernel,
        name="put",
        out_shape=like(outs),
        in_specs=[VM] * 6,
        out_specs=[HBM] * 6,
        scratch_shapes=[sem(6)],
        compiler_params=pltpu.CompilerParams(vmem_limit_bytes=2 * 1024 * 1024),
    )(*outs)
    return list(outs[:2]) + [v.reshape(weight.shape) for v in outs[2:]]


def local(acts, weight, moment, second, cotangent):
    n = lax.axis_size("space")
    crops, _, nx, ny, nz, channels = acts.shape
    total = crops * lax.axis_size("sample") * n * nx * ny * nz
    alone = n == GY * GZ and lax.axis_size("sample") == 4
    fits = crops * nz == TILE and nx == TILE and ny % 2 == 0 and channels == 128 and weight.shape[0] % TILE == 0
    if not (alone and fits):
        return plain(acts, weight, moment, second, cotangent)
    value, grad, *rest = fused(
        acts[:, 0], weight, moment, second, cotangent[:, 0], float(total) ** (-0.5)
    )
    return (value[:, None], grad[:, None], *rest)


def solution(mesh):
    in_specs = (
        P("sample", "space", None, None, None, None),
        P("space", None),
        P("space", None),
        P("space", None),
        P("sample", "space", None, None, None, None),
    )
    out_specs = (
        P("sample", "space", None, None, None, None),
        P("sample", "space", None, None, None, None),
        P("space", None),
        P("space", None),
        P("space", None),
        P("space", None),
    )
    return jax.shard_map(local, mesh=mesh, in_specs=in_specs, out_specs=out_specs, check_vma=False)
```
